32 devices in a mesh: gx: 16 (over z, y, core), gy: 2 (over x).
Axes of the slice: x: 2, y: 2, z: 4, core: 2. Of those that a mesh axis runs over, the one named last changes fastest.
Arguments:
- charge: float32 [512, 2048], P('gx', 'gy'), may hold values from -8 to 8
Outputs:
- potential: float32 [512, 2048], P('gx', 'gy')
The draws below stay inside these ranges and needn't reach their ends.
All inputs are finite; a program needn't handle non-finite values.
Results may differ from the reference program's by a relative error of at most 0.0003.
Values sent between devices are 32-bit elements; how exact they have to be, the bound alone decides.
A program may use at most 128 MiB of HBM per device.

```python
import jax
import jax.numpy as jnp
from jax import lax

P_SIZE = 32
W = 16
Q = 4
NL = 16
NX = 512
NY = 64
N_GX = 16
N_GY = 2


def draw_charge(key, part):
    key_values = jax.random.fold_in(key, 0)
    extent = (NX, NY * P_SIZE)
    return jnp.clip(jax.random.normal(key_values, extent, jnp.float32), -8.0, 8.0)


def setup_inputs(seed: int = 0) -> dict:
    streams_of = jax.random.split(jax.random.key(seed), 2)
    return {
        "charge": draw_charge(jax.random.fold_in(streams_of[1], 71), 0),
    }


highest = lax.Precision.HIGHEST

def product(left, right):
    return jnp.matmul(left, right, precision=highest)

def sine_table(length):
    counter = jnp.arange(length, dtype=jnp.int32) + 1
    multiple = counter[:, None] * counter[None, :] % (2 * (length + 1))
    return jnp.sin(jnp.pi * multiple.astype(jnp.float32) / (length + 1))

def eigen_values(length):
    counter = (jnp.arange(length, dtype=jnp.int32) + 1).astype(jnp.float32)
    return 2.0 - 2.0 * jnp.cos(jnp.pi * counter / (length + 1))

def interp_table(fine_start, fine_count, coarse_start, coarse_count, ratio):
    fine_pos = jnp.arange(fine_count, dtype=jnp.int32) + fine_start
    coarse_pos = jnp.arange(coarse_count, dtype=jnp.int32) + coarse_start
    numerator = 2 * fine_pos - (ratio - 1)
    lower_index = numerator // (2 * ratio)
    weight = ((numerator - 2 * ratio * lower_index).astype(jnp.float32) / (2 * ratio))[:, None]
    below = (coarse_pos[None, :] == lower_index[:, None]).astype(jnp.float32)
    above = (coarse_pos[None, :] == lower_index[:, None] + 1).astype(jnp.float32)
    return below * (1.0 - weight) + above * weight

def legendre_basis(length, count):
    points = (2.0 * jnp.arange(length, dtype=jnp.int32).astype(jnp.float32) + 1.0) / length - 1.0
    columns = [jnp.ones_like(points), points]
    for degree in range(2, count):
        columns.append(((2 * degree - 1) * points * columns[-1] - (degree - 1) * columns[-2]) / degree)
    columns = columns[:count]
    result = []
    for column in columns:
        vector = column
        for passes in range(2):
            for earlier in result:
                vector = vector - jnp.sum(earlier * vector) * earlier
        vector = vector / jnp.sqrt(jnp.sum(vector * vector))
        result.append(vector)
    return jnp.stack(result, axis=1)

def along_three(volume, first_table, second_table, third_table):
    volume = jnp.einsum('ai,ijk->ajk', first_table, volume, precision=highest)
    volume = jnp.einsum('bj,ijk->ibk', second_table, volume, precision=highest)
    return jnp.einsum('ck,ijk->ijc', third_table, volume, precision=highest)

def box_solve(patch):
    length = patch.shape[0] + 2 * W
    padded = jnp.pad(patch, W)
    table = sine_table(length)
    values = eigen_values(length)
    spectrum = along_three(padded, table, table, table)
    spectrum = spectrum / (values[:, None, None] + values[None, :, None] + values[None, None, :])
    return along_three(spectrum, table, table, table) * (2.0 / (length + 1)) ** 3

def coarse_charge(local):
    blocks = local.shape[0] // Q
    samples = local.reshape(blocks, Q, blocks, Q, blocks, Q).mean(axis=(1, 3, 5))
    padded = jnp.pad(samples, 1)
    beside = padded[2:, 1:-1, 1:-1] + padded[:-2, 1:-1, 1:-1]
    beside = beside + padded[1:-1, 2:, 1:-1] + padded[1:-1, :-2, 1:-1]
    beside = beside + padded[1:-1, 1:-1, 2:] + padded[1:-1, 1:-1, :-2]
    return (samples, (6.0 * samples - beside) / (Q * Q))

def face_planes(local, samples):
    length = local.shape[0]
    inner = length - 2 * W
    fine_table = interp_table(0, length, 0, samples.shape[0], Q)
    middle = fine_table[W:W + inner]

    def across_x(index):
        coarse_plane = jnp.einsum('j,jkl->kl', fine_table[index], samples, precision=highest)
        return local[index, W:W + inner, W:W + inner] - product(product(middle, coarse_plane), middle.T)

    def across_y(index):
        coarse_plane = jnp.einsum('k,jkl->jl', fine_table[index], samples, precision=highest)
        return local[W:W + inner, index, W:W + inner] - product(product(middle, coarse_plane), middle.T)
    own = jnp.stack([across_x(W - 1), across_x(W + inner), across_y(W - 1), across_y(W + inner)])
    outgoing = jnp.stack([across_x(W), across_x(W + inner - 1), across_y(W), across_y(W + inner - 1)])
    return (own, outgoing)

def coefficients(planes, basis):
    return jnp.einsum('ia,nij,jb->nab', basis, planes, basis, precision=highest)

def expand(coefs, basis):
    return jnp.einsum('ia,nab,jb->nij', basis, coefs, basis, precision=highest)

def coarse_faces(block, inner):
    cells = block.shape[2]
    edge = interp_table(-1, inner + 2, -1, cells + 2, Q)
    depth = interp_table(0, inner, 0, cells, Q)
    lateral = edge[1:inner + 1]

    def spread(plane):
        return product(product(lateral, plane), depth.T)
    return jnp.stack([spread(jnp.einsum('e,efk->fk', edge[0], block, precision=highest)), spread(jnp.einsum('e,efk->fk', edge[inner + 1], block, precision=highest)), spread(jnp.einsum('f,efk->ek', edge[0], block, precision=highest)), spread(jnp.einsum('f,efk->ek', edge[inner + 1], block, precision=highest))])

def dirichlet_solve(patch, faces):
    inner = patch.shape[0]
    source = patch.at[0].add(faces[0]).at[inner - 1].add(faces[1])
    source = source.at[:, 0].add(faces[2]).at[:, inner - 1].add(faces[3])
    table = sine_table(inner)
    values = eigen_values(inner)
    spectrum = along_three(source, table, table, table)
    spectrum = spectrum / (values[:, None, None] + values[None, :, None] + values[None, None, :])
    return along_three(spectrum, table, table, table) * (2.0 / (inner + 1)) ** 3

def coarse_solve(source):
    size_x, size_y, size_z = source.shape
    table_x = sine_table(size_x)
    table_y = sine_table(size_y)
    table_z = sine_table(size_z)
    values_x = eigen_values(size_x)
    values_y = eigen_values(size_y)
    values_z = eigen_values(size_z)
    spectrum = along_three(source, table_x, table_y, table_z)
    spectrum = spectrum * (Q * Q) / (values_x[:, None, None] + values_y[None, :, None] + values_z[None, None, :])
    scale = 2.0 / (size_x + 1) * (2.0 / (size_y + 1)) * (2.0 / (size_z + 1))
    return along_three(spectrum, table_x, table_y, table_z) * scale

def reference(charge):
    inner = P_SIZE
    cells = inner // Q
    margin_coarse = W // Q
    count = N_GX * N_GY
    patches = charge.reshape(N_GX, inner, N_GY, inner, inner).transpose(0, 2, 1, 3, 4).reshape(count, inner, inner, inner)
    basis = legendre_basis(inner, NL)

    def first_pass(patch):
        local = box_solve(patch)
        samples, spill = coarse_charge(local)
        own, outgoing = face_planes(local, samples)
        return (spill[:, :, margin_coarse:margin_coarse + cells], coefficients(own, basis), coefficients(outgoing, basis))
    spills, own_coefs, sent_coefs = lax.map(first_pass, patches)
    span = spills.shape[1]
    total = jnp.zeros((N_GX * cells + 2 * margin_coarse, N_GY * cells + 2 * margin_coarse, cells), jnp.float32)

    def deposit(index, total):
        index = index.astype(jnp.int32)
        start_x = (index // N_GY * cells).astype(jnp.int32)
        start_y = (index % N_GY * cells).astype(jnp.int32)
        anchor = jnp.zeros((), jnp.int32)
        current = lax.dynamic_slice(total, (start_x, start_y, anchor), (span, span, cells))
        return lax.dynamic_update_slice(total, current + spills[index], (start_x, start_y, anchor))
    total = lax.fori_loop(0, count, deposit, total)
    source = total[margin_coarse:margin_coarse + N_GX * cells, margin_coarse:margin_coarse + N_GY * cells]
    coarse = coarse_solve(source)
    rimmed = jnp.pad(coarse, ((1, 1), (1, 1), (0, 0)))
    grid_sent = sent_coefs.reshape(N_GX, N_GY, 4, NL, NL)
    no_pad = (0, 0)
    from_left = jnp.pad(grid_sent[:, :, 1], ((1, 0), no_pad, no_pad, no_pad))[:-1]
    from_right = jnp.pad(grid_sent[:, :, 0], ((0, 1), no_pad, no_pad, no_pad))[1:]
    from_below = jnp.pad(grid_sent[:, :, 3], (no_pad, (1, 0), no_pad, no_pad))[:, :-1]
    from_above = jnp.pad(grid_sent[:, :, 2], (no_pad, (0, 1), no_pad, no_pad))[:, 1:]
    received = jnp.stack([from_left, from_right, from_below, from_above], axis=2).reshape(count, 4, NL, NL)

    def second_pass(items):
        patch, own, incoming, index = items
        start_x = (index // N_GY * cells).astype(jnp.int32)
        start_y = (index % N_GY * cells).astype(jnp.int32)
        anchor = jnp.zeros((), jnp.int32)
        block = lax.dynamic_slice(rimmed, (start_x, start_y, anchor), (cells + 2, cells + 2, cells))
        faces = coarse_faces(block, inner) + expand(own + incoming, basis)
        return dirichlet_solve(patch, faces)
    solved = lax.map(second_pass, (patches, own_coefs, received, jnp.arange(count, dtype=jnp.int32)))
    return solved.reshape(N_GX, N_GY, inner, inner, inner).transpose(0, 2, 1, 3, 4).reshape(charge.shape)
```

```python
import functools

import jax
import jax.numpy as jnp
import ml_dtypes
import numpy as np
from jax import lax
from jax.experimental import pallas as pl
from jax.experimental.pallas import tpu as pltpu
from jax.sharding import PartitionSpec as P

P_SIZE = 32
W = 16
Q = 4
NL = 16
CLASSES = [(0, 0), (0, 1), (1, 0), (1, 1)]
MESH = pl.DeviceIdType.MESH


def sine_table(length):
    counter = np.arange(length) + 1
    return np.sin(np.pi * np.outer(counter, counter) / (length + 1))


def eigen_values(length):
    return 2.0 - 2.0 * np.cos(np.pi * (np.arange(length) + 1) / (length + 1))


def interp_table(fine_start, fine_count, coarse_start, coarse_count, ratio):
    fine_pos = np.arange(fine_count) + fine_start
    coarse_pos = np.arange(coarse_count) + coarse_start
    numerator = 2 * fine_pos - (ratio - 1)
    lower = numerator // (2 * ratio)
    weight = ((numerator - 2 * ratio * lower) / (2 * ratio))[:, None]
    below = coarse_pos[None, :] == lower[:, None]
    above = coarse_pos[None, :] == lower[:, None] + 1
    return below * (1.0 - weight) + above * weight


def legendre_basis(length, count):
    points = (2.0 * np.arange(length) + 1.0) / length - 1.0
    columns = [np.ones_like(points), points]
    for degree in range(2, count):
        columns.append(
            ((2 * degree - 1) * points * columns[-1] - (degree - 1) * columns[-2]) / degree
        )
    result = []
    for vector in columns[:count]:
        for passes in range(2):
            for earlier in result:
                vector = vector - np.sum(earlier * vector) * earlier
        result.append(vector / np.sqrt(np.sum(vector * vector)))
    return np.stack(result, axis=1)


def fold(length):
    half = length // 2
    eye = np.eye(length)
    return np.concatenate([eye[:half] + eye[::-1][:half], eye[:half] - eye[::-1][:half]])


def split(table):
    high = table.astype(ml_dtypes.bfloat16)
    low = (table - high.astype(np.float64)).astype(ml_dtypes.bfloat16)
    return high, low


def pack(blocks, row_tile):
    parts, places, row = [], {}, 0
    for name, block in blocks.items():
        rows = -(-block.shape[0] // row_tile) * row_tile
        part = np.zeros((rows, 128))
        part[: block.shape[0], : block.shape[1]] = block
        parts.append(part)
        places[name] = (row, rows, block.shape[1])
        row += rows
    return np.concatenate(parts), places


@functools.lru_cache(maxsize=None)
def tables(n_gx, n_gy):
    n, length, cells = P_SIZE, P_SIZE + 2 * W, P_SIZE // Q
    blocks, margin = length // Q, W // Q
    half, hl, hb, hn = n // 2, length // 2, blocks // 2, NL // 2
    quad, wide = hb * hb, hn * hn
    nx, ny, nz = n_gx * cells, n_gy * cells, cells
    modes = ny * nz
    s_l, s_n = sine_table(length), sine_table(n)
    u_n, u_b = fold(n), fold(blocks)
    basis = legendre_basis(n, NL)
    average = np.kron(np.eye(blocks), np.full((1, Q), 1.0 / Q))
    fine = interp_table(0, length, 0, blocks, Q)
    middle = fine[W : W + n]
    picks = [W - 1, W, W + n - 1, W + n]
    a_full = average @ s_l
    b_full = basis.T @ s_l[W : W + n]
    swapped = [1, 0, 3, 2]
    big = {}

    folding = np.zeros((4, 4, n, 4, 2 * 4, half))
    for c, (p, q) in enumerate(CLASSES):
        for vi in range(4):
            for y4 in range(4):
                il = [y4, 4 + y4, 3 - y4, 7 - y4][vi]
                sign = -1.0 if vi > 1 and p == 1 else 1.0
                folding[vi, y4, :, c, il, :] = sign * u_n[q * half : (q + 1) * half].T
    folding = folding.reshape(4 * 128, 4 * 128)
    plain = {"fold": folding, "unfold": folding.T}

    inner = s_l[:, W : W + n] @ u_n.T / 2
    f1 = [inner[p::2, p * half : (p + 1) * half] for p in (0, 1)]
    a1 = [(u_b @ a_full)[p * hb : (p + 1) * hb, p::2] for p in (0, 1)]
    b1 = [b_full[p::2, p::2] for p in (0, 1)]
    for c, (p, q) in enumerate(CLASSES):
        big["fwd%d" % c] = np.kron(f1[p], f1[q]).T
        part = np.zeros((hl * hl, 256))
        sample, coef = np.kron(a1[p], a1[q]).T, np.kron(b1[p], b1[q]).T
        part[:, :128] = np.concatenate([sample, coef] if c % 2 == 0 else [coef, sample], axis=1)
        part[:, 128:192] = np.kron(s_l[picks][:, p::2], b_full[:, q::2]).T
        big["back%d" % c] = part

    unfold = u_b.T / 2
    pair = np.kron(unfold, unfold).reshape(blocks * blocks, 2, hb, 2, hb)

    def from_samples(table):
        folded = np.einsum("os,spaqb->pqabo", table, pair)
        return folded.reshape(4 * quad, table.shape[0])

    bm = basis.T @ middle
    lin_x = from_samples(np.kron(bm, bm)).reshape(4 * quad, NL, NL)
    lin = np.zeros((4 * quad, 384))
    for place, c in enumerate(swapped):
        p, q = CLASSES[c]
        lin[:, place * wide : (place + 1) * wide] = lin_x[:, p::2, q::2].reshape(4 * quad, wide)
    lin[:, 256:320] = from_samples(np.kron(fine[picks], bm))
    big["lin"] = lin
    k1 = [(s_n @ u_n.T / 2)[p::2, p * half : (p + 1) * half] for p in (0, 1)]
    big["near"] = np.concatenate([np.kron(k1[p], k1[q]).T for p, q in CLASSES])
    r1 = [(u_n @ s_n / 2)[p * half : (p + 1) * half, p::2] for p in (0, 1)]
    big["far"] = np.concatenate([np.kron(r1[p], r1[q]).T for p, q in CLASSES])

    second = 2 * np.eye(blocks) - np.eye(blocks, k=1) - np.eye(blocks, k=-1)
    s_y, s_z = sine_table(ny), sine_table(nz)
    proj_z = np.zeros((nz, blocks))
    proj_z[:, margin : margin + cells] = s_z
    edge = interp_table(-1, n + 2, -1, cells + 2, Q)
    depth = interp_table(0, n, 0, cells, Q)
    lateral = edge[1 : n + 1]
    s_ext = np.zeros((ny + 2, ny))
    s_ext[1:-1] = s_y
    sp = np.concatenate([s_n[0::2], s_n[1::2]])
    deep = sp @ depth @ s_z

    def by_class(first, second_table):
        parts = []
        for p, q in CLASSES:
            parts.append(
                np.kron(first[p * half : (p + 1) * half], second_table[q * half : (q + 1) * half])
            )
        return np.concatenate(parts).T

    factor = (2.0 / (ny + 1)) * (2.0 / (nz + 1))
    spread, drop = [], []
    for b in range(n_gy):
        proj_y = np.zeros((ny, blocks))
        for j in range(blocks):
            at = j + b * cells - margin
            if 0 <= at < ny:
                proj_y[:, j] = s_y[:, at]
        flat = np.kron(proj_y, proj_z)
        curved = np.kron(proj_y @ second, proj_z) + np.kron(proj_y, proj_z @ second)
        spread.append(
            factor * np.concatenate([from_samples(curved), from_samples(flat)], axis=1)
        )
        local_s = s_ext[b * cells : b * cells + cells + 2]
        rim = np.outer(sp[:, 0], edge[0] @ local_s) + np.outer(sp[:, n - 1], edge[n + 1] @ local_s)
        drop.append(
            np.concatenate([by_class(sp @ lateral @ local_s, deep), by_class(rim, deep)])
        )
    big["spread"] = np.stack(spread)
    big["drop"] = np.stack(drop)
    sb = s_n @ basis
    sbp = np.concatenate([sb[0::2], sb[1::2]])
    facex = np.zeros((4 * wide, n * n))
    for place, c in enumerate(swapped):
        p, q = CLASSES[c]
        facex[place * wide : (place + 1) * wide, c * 256 : c * 256 + 256] = np.kron(
            sb[p::2, p::2], sb[q::2, q::2]
        ).T
    big["facex"] = facex
    ends = np.stack([sp[:, 0], sp[:, n - 1], sp[:, 0], sp[:, n - 1]], axis=1)
    big["facey"] = by_class(ends, sbp)

    mu_y, mu_z = eigen_values(ny), eigen_values(nz)
    theta = np.arccosh(1.0 + (mu_y[:, None] + mu_z[None, :]).reshape(1, modes) / 2)
    below = 2 * np.sinh(theta) * (1.0 - np.exp(-2 * theta * (nx + 1)))
    apart = np.abs(np.arange(48) - 20)[:, None]
    toep = (np.exp(-theta * apart) + np.exp(-theta * np.maximum(2 * (nx + 1) - apart, 0))) / below
    total = (np.arange(2 * nx + 32) - 13)[:, None]
    hank = np.exp(-theta * np.maximum(total + 2, 0)) + np.exp(-theta * np.maximum(2 * nx - total, 0))
    hank = hank / below

    u12 = np.zeros((64, 16))
    u12[:32, :10] = np.outer(s_n[:, 0], edge[0]) + np.outer(s_n[:, n - 1], edge[n + 1])
    u12[32:, :10] = s_n @ lateral
    place = np.arange(n_gx)
    mine = []
    for a in range(n_gx):
        rank = np.arange(16)[:, None]
        at = cells * a - margin + rank
        inside = (at >= 0) & (at < nx)
        rightward = inside * np.exp(-theta * (15 - rank)) * (1 - np.exp(-2 * theta * (at + 1) * inside))
        leftward = inside * np.exp(-theta * rank) * (1 - np.exp(-2 * theta * (nx - at) * inside))
        row = np.arange(16)[:, None]
        x = cells * a - 1 + row
        used = row < cells + 2
        falling = used * np.exp(-theta * row) * (1 - np.exp(-2 * theta * np.maximum(nx - x, 0))) / below
        rising = (
            used
            * np.exp(-theta * np.maximum(cells + 1 - row, 0))
            * (1 - np.exp(-2 * theta * (x + 1)))
            / below
        )
        away = (a - place)[:, None]
        before = (away >= 2) * np.exp(-theta * np.maximum(cells * away - 12, 0))
        after = (away <= -2) * np.exp(-theta * np.maximum(-cells * away - 12, 0))
        mine.append(
            np.concatenate([rightward, leftward, u12 @ falling, u12 @ rising, before, after])
        )
    singles = {
        "mine": np.stack(mine).astype(np.float32),
        "toep": toep.astype(np.float32),
        "hank": hank.astype(np.float32),
    }

    mu_l, mu_n = eigen_values(length), eigen_values(n)
    sums = np.ones((8, hl * hl))
    for c, (p, q) in enumerate(CLASSES):
        sums[c] = (mu_l[p::2][:, None] + mu_l[q::2][None, :]).ravel()
    sums[4, : n * n] = np.concatenate(
        [(mu_n[p::2][:, None] + mu_n[q::2][None, :]).ravel() for p, q in CLASSES]
    )
    singles["sums"] = sums.astype(np.float32)
    columns, column_places = pack(
        {"mul": mu_l[:, None], "mun": mu_n[:, None], "ends": s_n[:, [0, n - 1]]}, 8
    )
    singles["columns"] = columns.astype(np.float32)

    scale = (2.0 / (length + 1)) ** 3
    flat = np.zeros((24, length))
    flat[:4] = fine[picks] @ a_full * scale
    flat[8:24] = bm @ a_full * scale
    lefts = {
        "sl": s_l[:, W : W + n],
        "source": np.concatenate([a_full, second @ a_full], axis=1) * scale,
        "flat": flat,
        "picks": s_l[picks] * scale,
        "coefs": b_full * scale,
        "sn": s_n,
        "u12": u12,
        "sb": sb,
    }
    left, left_places = pack(lefts, 16)
    doubled, row, spots = [], 0, {}
    for name, (start, rows, cols) in left_places.items():
        doubled += list(split(left[start : start + rows]))
        spots[name] = (row, rows, cols)
        row += 2 * rows
    singles["lefts"] = np.concatenate(doubled)
    for name, value in plain.items():
        singles[name] = value.astype(ml_dtypes.bfloat16)
    for name, value in big.items():
        singles[name] = np.stack(split(value), axis=value.ndim - 2)
    return singles, column_places, spots


def halves(value):
    high = value.astype(jnp.bfloat16)
    return high, (value - high.astype(jnp.float32)).astype(jnp.bfloat16)


def mm(left, right):
    return jnp.dot(left, right, preferred_element_type=jnp.float32)


def right_mul(value, high_table, low_table):
    rows = value.shape[0]
    high, low = halves(value)
    both = mm(jnp.concatenate([high, low], axis=0), high_table)
    return both[:rows] + both[rows:] + mm(high, low_table)


NAMES = [
    "charge", "fold", "lefts", "sums", "columns",
    "fwd0", "fwd1", "back0", "fwd2", "back1", "fwd3", "back2", "back3",
    "spread", "mine", "lin", "near", "facex", "facey", "toep", "hank", "drop", "far", "unfold",
]


def window(name, shape):
    if name in ("spread", "drop", "mine"):
        return shape[1:]
    if name == "hank":
        return (48,) + shape[1:]
    return shape


def kernel(column_places, spots, n_gx, n_gy, *refs):
    count = len(NAMES)
    hbm = dict(zip(NAMES, refs[:count]))
    out_ref = refs[count]
    vmem = dict(zip(NAMES, refs[count + 1 : 2 * count + 1]))
    (
        mom_ref, far_ref, near_ref, cx_ref, cy_ref, rx_ref, ry_ref,
        load_sem, f_send, f_recv, p_send, p_recv, c_send, c_recv,
    ) = refs[2 * count + 1 :]
    ndev = n_gx * n_gy
    a = lax.axis_index("gx")
    b = lax.axis_index("gy")
    me = a * n_gy + b
    n, cells = P_SIZE, P_SIZE // Q

    loads = {}
    for i, name in enumerate(NAMES):
        source = hbm[name]
        if name in ("spread", "drop"):
            source = source.at[b]
        if name == "mine":
            source = source.at[a]
        if name == "hank":
            source = source.at[pl.ds(pl.multiple_of(a * 16, 16), 48)]
        loads[name] = pltpu.make_async_copy(source, vmem[name], load_sem.at[i])
        loads[name].start()

    barrier = pltpu.get_barrier_semaphore()

    def greet(r, carry):
        peer = lax.rem(me + r, ndev)
        pl.semaphore_signal(
            barrier, inc=1, device_id=(peer // n_gy, lax.rem(peer, n_gy)), device_id_type=MESH
        )
        return carry

    with jax.named_scope("greet"):
        lax.fori_loop(1, ndev, greet, 0)

    def ready(*wanted):
        for name in wanted:
            loads[name].wait()

    def table(name):
        return vmem[name][0], vmem[name][1]

    def column(name):
        row, rows, cols = column_places[name]
        return vmem["columns"][row : row + rows, 0:cols]

    def left_mul(name, value):
        row, rows, cols = spots[name]
        high, low = halves(value)
        both = mm(vmem["lefts"][row : row + 2 * rows, 0:cols], high)
        rest = mm(vmem["lefts"][row : row + rows, 0:cols], low)
        return both[:rows] + both[rows:] + rest

    groups = [[0, 1, 7, 6], [2, 3, 5, 4]]
    with jax.named_scope("fold"):
        ready("charge", "fold")
        sides = [
            jnp.concatenate([vmem["charge"][:, v * 128 : (v + 1) * 128] for v in group], axis=1)
            for group in groups
        ]
        high, low = halves(jnp.concatenate(sides, axis=0))
        both = mm(jnp.concatenate([high, low], axis=0), vmem["fold"][...])
        both = both[: 2 * n] + both[2 * n :]
        folded = jnp.concatenate(
            [
                both[s * n : (s + 1) * n, c * 128 : (c + 1) * 128]
                for c in range(4)
                for s in range(2)
            ],
            axis=1,
        )
        ready("lefts")
        wide = left_mul("sl", folded)
        ready("sums", "columns")

    def forward(c):
        ready("fwd%d" % c)
        spectrum = right_mul(wide[:, c * 256 : (c + 1) * 256], *table("fwd%d" % c))
        return spectrum / (column("mul") + vmem["sums"][c : c + 1, :])

    def backward(c, spectrum):
        ready("back%d" % c)
        return right_mul(spectrum, *table("back%d" % c))

    with jax.named_scope("classes"):
        s0 = forward(0)
        s1 = forward(1)
        y0 = backward(0, s0)
        s2 = forward(2)
        y1 = backward(1, s1)
        s3 = forward(3)
        y2 = backward(2, s2)
        y3 = backward(3, s3)
    with jax.named_scope("spread"):
        first = lax.broadcasted_iota(jnp.int32, (n + 2 * W, 128), 1) < 64
        sample = jnp.concatenate(
            [jnp.where(first, u[:, :128], v[:, :128]) for u, v in ((y0, y1), (y2, y3))], axis=1
        )
        ready("spread", "mine")
        modes = near_ref.shape[-1]
        spread = right_mul(sample, *table("spread"))
        packet = left_mul("source", jnp.concatenate([spread[:, :modes], spread[:, modes:]], axis=0))
        near_ref[1, b] = packet
        mine = vmem["mine"]
        rightward = jnp.sum(packet * mine[0:16], axis=0, keepdims=True)
        leftward = jnp.sum(packet * mine[16:32], axis=0, keepdims=True)
        for g in range(modes // 128):
            mom_ref[g, 0:1] = rightward[:, g * 128 : (g + 1) * 128]
            mom_ref[g, 1:2] = leftward[:, g * 128 : (g + 1) * 128]

    with jax.named_scope("barrier"):
        pl.semaphore_wait(barrier, ndev - 1)

    def remote(source, target, send, recv, device):
        return pltpu.make_async_remote_copy(
            src_ref=source,
            dst_ref=target,
            send_sem=send,
            recv_sem=recv,
            device_id=device,
            device_id_type=MESH,
        )

    def start_far(r, carry):
        d = n_gx - r
        for j in range(n_gy):

            @pl.when(a + d < n_gx)
            def _():
                remote(
                    mom_ref.at[:, pl.ds(0, 1)],
                    far_ref.at[b, :, pl.ds(a, 1)],
                    f_send,
                    f_recv,
                    (a + d, j),
                ).start()

            @pl.when(a >= d)
            def _():
                remote(
                    mom_ref.at[:, pl.ds(1, 1)],
                    far_ref.at[b, :, pl.ds(a, 1)],
                    f_send,
                    f_recv,
                    (a - d, j),
                ).start()

        return carry

    def for_near(act):
        for step in (0, 1, 2):
            for j in range(n_gy):
                other = a + step - 1
                fine = (other >= 0) & (other < n_gx)
                if step == 1:
                    fine = b != j

                @pl.when(fine)
                def _():
                    act(step, j, (other, j))

    with jax.named_scope("send"):
        lax.fori_loop(1, n_gx - 1, start_far, 0)

        def send_near(step, j, device):
            remote(
                near_ref.at[1, b],
                near_ref.at[2 - step, b],
                p_send.at[step, j],
                p_recv.at[2 - step, b],
                device,
            ).start()

        for_near(send_near)

    with jax.named_scope("lin"):
        ready("lin")
        coef = jnp.concatenate(
            [jnp.where(first, v[:, :128], u[:, :128]) for u, v in ((y0, y1), (y2, y3))], axis=1
        )
        slab = y0[:, 128:] + y1[:, 128:] + y2[:, 128:] + y3[:, 128:]
        flat = right_mul(left_mul("flat", sample), *table("lin"))
        cx = left_mul("picks", coef)[0:8] - flat[0:8, 0:256]
        cy = left_mul("coefs", slab) - flat[8:24, 256:384]
        cx_ref[...] = cx
        cy_ref[...] = cy

    upper, lower = lax.rem(b + 1, n_gy), lax.rem(b + n_gy - 1, n_gy)
    go_right = remote(cx_ref.at[pl.ds(2, 1)], rx_ref.at[pl.ds(0, 1)], c_send.at[0], c_recv.at[0], (a + 1, b))
    go_left = remote(cx_ref.at[pl.ds(1, 1)], rx_ref.at[pl.ds(1, 1)], c_send.at[1], c_recv.at[1], (a - 1, b))
    go_up = remote(cy_ref, ry_ref.at[0], c_send.at[2], c_recv.at[2], (a, upper))
    go_down = remote(cy_ref, ry_ref.at[1], c_send.at[3], c_recv.at[3], (a, lower))

    with jax.named_scope("sendc"):

        @pl.when(a < n_gx - 1)
        def _():
            go_right.start()

        @pl.when(a > 0)
        def _():
            go_left.start()

        go_up.start()
        go_down.start()

    with jax.named_scope("near"):
        ready("near")
        narrow = left_mul("sn", folded)
        spectrum = jnp.concatenate(
            [
                right_mul(
                    narrow[:, c * 256 : (c + 1) * 256],
                    vmem["near"][0, c * 256 : (c + 1) * 256],
                    vmem["near"][1, c * 256 : (c + 1) * 256],
                )
                for c in range(4)
            ],
            axis=1,
        )
        scale = (2.0 / (n + 1)) ** 3
        inverse = scale / (column("mun") + vmem["sums"][4:5, 0 : n * n])

    with jax.named_scope("wait_c"):

        @pl.when(a < n_gx - 1)
        def _():
            go_right.wait_send()
            go_left.wait_recv()

        @pl.when(a > 0)
        def _():
            go_left.wait_send()
            go_right.wait_recv()

        go_up.wait()
        go_down.wait()

    with jax.named_scope("face"):
        ready("facex", "facey")
        from_left = jnp.where(a > 0, rx_ref[0:1], 0.0)
        from_right = jnp.where(a < n_gx - 1, rx_ref[1:2], 0.0)
        ends = jnp.concatenate(
            [cx[0:1] + from_left, cx[3:4] + from_right, jnp.zeros((6, cx.shape[1]), jnp.float32)]
        )
        ends = right_mul(ends, *table("facex"))
        spectrum = spectrum + column("ends")[:, 0:1] * ends[0:1]
        spectrum = spectrum + column("ends")[:, 1:2] * ends[1:2]
        group = lax.broadcasted_iota(jnp.int32, (16, 128), 1) // 16
        total = jnp.where((group == 0) | (group == 3), cy, 0.0)
        total = total + jnp.where((group == 2) & (b > 0), ry_ref[0], 0.0)
        total = total + jnp.where((group == 1) & (b < n_gy - 1), ry_ref[1], 0.0)
        spectrum = spectrum + right_mul(left_mul("sb", total)[:, 0:64], *table("facey"))

    with jax.named_scope("wait_p"):

        def wait_near(step, j, device):
            remote(
                near_ref.at[1, b], near_ref.at[step, j], p_send.at[step, j], p_recv.at[step, j], device
            ).wait()

        for_near(wait_near)

    with jax.named_scope("green"):
        ready("toep", "hank")
        row = lax.broadcasted_iota(jnp.int32, (8, modes), 0)

        def gathered(step):
            value = near_ref[step, 0]
            for j in range(1, n_gy):
                value = value + near_ref[step, j]
            return value

        past = jnp.where(a > 0, gathered(0), 0.0)
        here = gathered(1)
        next_ = jnp.where(a < n_gx - 1, gathered(2), 0.0)
        source = jnp.concatenate(
            [
                jnp.where((row >= 4) | (a > 1), past[0:8], 0.0),
                past[8:16] + jnp.where((row >= 4) | (a > 0), here[0:8], 0.0),
                jnp.where((row < 4) | (a < n_gx - 1), here[8:16] + next_[0:8], 0.0),
                jnp.where((row < 4) | (a < n_gx - 2), next_[8:16], 0.0),
            ]
        )
        values = []
        for i in range(cells + 2):
            influence = vmem["toep"][9 - i : 41 - i] - vmem["hank"][i : i + 32]
            values.append(jnp.sum(influence * source, axis=0, keepdims=True))
        values.append(jnp.zeros((16 - len(values), modes), jnp.float32))
        lifted = left_mul("u12", jnp.concatenate(values, axis=0))

    with jax.named_scope("wait_f"):

        def settle(each):
            block = far_ref.at[:, :, pl.ds(0, each)]
            remote(block, block, f_send, f_recv, (a, b)).wait()

        edge = (a == 0) | (a == n_gx - 1)

        @pl.when(edge)
        def _():
            settle(n_gx - 2)

        @pl.when(jnp.logical_not(edge))
        def _():
            settle(n_gx - 3)

    with jax.named_scope("final"):
        origin = lax.broadcasted_iota(jnp.int32, (n_gx, modes), 0)
        before = jnp.zeros((n_gx, modes), jnp.float32)
        after = before
        for j in range(n_gy):
            sent = jnp.concatenate([far_ref[j, g] for g in range(modes // 128)], axis=1)
            before = before + jnp.where(origin <= a - 2, sent, 0.0)
            after = after + jnp.where(origin >= a + 2, sent, 0.0)
        before = jnp.sum(before * mine[160 : 160 + n_gx], axis=0, keepdims=True)
        after = jnp.sum(after * mine[160 + n_gx : 160 + 2 * n_gx], axis=0, keepdims=True)
        lifted = lifted + mine[32:96] * before + mine[96:160] * after
        ready("drop", "far", "unfold")
        spectrum = spectrum + right_mul(
            jnp.concatenate([lifted[:n], lifted[n:]], axis=1), *table("drop")
        )
        spectrum = left_mul("sn", spectrum * inverse)
        parts = [
            right_mul(
                spectrum[:, c * 256 : (c + 1) * 256],
                vmem["far"][0, c * 256 : (c + 1) * 256],
                vmem["far"][1, c * 256 : (c + 1) * 256],
            )
            for c in range(4)
        ]
    with jax.named_scope("unfold"):
        sides = [
            jnp.concatenate([part[:, s * 128 : (s + 1) * 128] for part in parts], axis=1)
            for s in range(2)
        ]
        high, low = halves(jnp.concatenate(sides, axis=0))
        both = mm(jnp.concatenate([high, low], axis=0), vmem["unfold"][...])
        both = both[: 2 * n] + both[2 * n :]
        for s, group in enumerate(groups):
            for i, v in enumerate(group):
                out_ref[:, v * 128 : (v + 1) * 128] = both[
                    s * n : (s + 1) * n, i * 128 : (i + 1) * 128
                ]


def emit(in_ref, out_ref, sem):
    copy = pltpu.make_async_copy(in_ref, out_ref, sem)
    copy.start()
    copy.wait()


def body(n_gx, n_gy, charge):
    singles, column_places, spots = tables(n_gx, n_gy)
    arrays = [charge] + [jnp.asarray(singles[name]) for name in NAMES[1:]]
    scratch = [
        pltpu.VMEM(window(name, array.shape), array.dtype) for name, array in zip(NAMES, arrays)
    ]
    modes = n_gy * (P_SIZE // Q) ** 2
    scratch += [
        pltpu.VMEM((modes // 128, 8, 128), jnp.float32),
        pltpu.VMEM((n_gy, modes // 128, n_gx, 128), jnp.float32),
        pltpu.VMEM((3, n_gy, 16, modes), jnp.float32),
        pltpu.VMEM((8, 256), jnp.float32),
        pltpu.VMEM((16, 128), jnp.float32),
        pltpu.VMEM((8, 256), jnp.float32),
        pltpu.VMEM((2, 16, 128), jnp.float32),
        pltpu.SemaphoreType.DMA((len(NAMES),)),
        pltpu.SemaphoreType.DMA,
        pltpu.SemaphoreType.DMA,
        pltpu.SemaphoreType.DMA((3, n_gy)),
        pltpu.SemaphoreType.DMA((3, n_gy)),
        pltpu.SemaphoreType.DMA((4,)),
        pltpu.SemaphoreType.DMA((4,)),
    ]
    hbm = pl.BlockSpec(memory_space=pl.ANY)
    vm = pl.BlockSpec(memory_space=pltpu.VMEM)
    solved = pl.pallas_call(
        functools.partial(kernel, column_places, spots, n_gx, n_gy),
        out_shape=pltpu.VMEM(charge.shape, charge.dtype),
        in_specs=[hbm] * len(NAMES),
        out_specs=vm,
        scratch_shapes=scratch,
        name="mlc",
        compiler_params=pltpu.CompilerParams(
            collective_id=0, has_side_effects=True, vmem_limit_bytes=60 * 1024 * 1024
        ),
    )(*arrays)
    return pl.pallas_call(
        emit,
        out_shape=jax.ShapeDtypeStruct(charge.shape, charge.dtype),
        in_specs=[vm],
        out_specs=hbm,
        scratch_shapes=[pltpu.SemaphoreType.DMA],
        name="emit",
        compiler_params=pltpu.CompilerParams(vmem_limit_bytes=1024 * 1024),
    )(solved)


def solution(mesh):
    run = functools.partial(body, mesh.shape["gx"], mesh.shape["gy"])
    spec = P("gx", "gy")
    return jax.shard_map(run, mesh=mesh, in_specs=(spec,), out_specs=spec, check_vma=False)
```

```python
import functools

import jax
import jax.numpy as jnp
import ml_dtypes
import numpy as np
from jax import lax
from jax.experimental import pallas as pl
from jax.experimental.pallas import tpu as pltpu
from jax.sharding import PartitionSpec as P

P_SIZE = 32
W = 16
Q = 4
NL = 16
CLASSES = [(0, 0), (0, 1), (1, 0), (1, 1)]
MESH = pl.DeviceIdType.MESH


def sine_table(length):
    counter = np.arange(length) + 1
    return np.sin(np.pi * np.outer(counter, counter) / (length + 1))


def eigen_values(length):
    return 2.0 - 2.0 * np.cos(np.pi * (np.arange(length) + 1) / (length + 1))


def interp_table(fine_start, fine_count, coarse_start, coarse_count, ratio):
    fine_pos = np.arange(fine_count) + fine_start
    coarse_pos = np.arange(coarse_count) + coarse_start
    numerator = 2 * fine_pos - (ratio - 1)
    lower = numerator // (2 * ratio)
    weight = ((numerator - 2 * ratio * lower) / (2 * ratio))[:, None]
    below = coarse_pos[None, :] == lower[:, None]
    above = coarse_pos[None, :] == lower[:, None] + 1
    return below * (1.0 - weight) + above * weight


def legendre_basis(length, count):
    points = (2.0 * np.arange(length) + 1.0) / length - 1.0
    columns = [np.ones_like(points), points]
    for degree in range(2, count):
        columns.append(
            ((2 * degree - 1) * points * columns[-1] - (degree - 1) * columns[-2]) / degree
        )
    result = []
    for vector in columns[:count]:
        for passes in range(2):
            for earlier in result:
                vector = vector - np.sum(earlier * vector) * earlier
        result.append(vector / np.sqrt(np.sum(vector * vector)))
    return np.stack(result, axis=1)


def fold(length):
    half = length // 2
    eye = np.eye(length)
    return np.concatenate([eye[:half] + eye[::-1][:half], eye[:half] - eye[::-1][:half]])


def split(table):
    high = table.astype(ml_dtypes.bfloat16)
    low = (table - high.astype(np.float64)).astype(ml_dtypes.bfloat16)
    return high, low


def pack(blocks, row_tile):
    parts, places, row = [], {}, 0
    for name, block in blocks.items():
        rows = -(-block.shape[0] // row_tile) * row_tile
        part = np.zeros((rows, 128))
        part[: block.shape[0], : block.shape[1]] = block
        parts.append(part)
        places[name] = (row, rows, block.shape[1])
        row += rows
    return np.concatenate(parts), places


@functools.lru_cache(maxsize=None)
def tables(n_gx, n_gy):
    n, length, cells = P_SIZE, P_SIZE + 2 * W, P_SIZE // Q
    blocks, margin = length // Q, W // Q
    half, hl, hb, hn = n // 2, length // 2, blocks // 2, NL // 2
    quad, wide = hb * hb, hn * hn
    nx, ny, nz = n_gx * cells, n_gy * cells, cells
    modes = ny * nz
    s_l, s_n = sine_table(length), sine_table(n)
    u_n, u_b = fold(n), fold(blocks)
    basis = legendre_basis(n, NL)
    average = np.kron(np.eye(blocks), np.full((1, Q), 1.0 / Q))
    fine = interp_table(0, length, 0, blocks, Q)
    middle = fine[W : W + n]
    picks = [W - 1, W, W + n - 1, W + n]
    a_full = average @ s_l
    b_full = basis.T @ s_l[W : W + n]
    order = np.arange(4 * NL).reshape(4, hn, 2).transpose(2, 0, 1).ravel()
    big = {}

    folding = np.zeros((4, 4, n, 4, 2 * 4, half))
    for c, (p, q) in enumerate(CLASSES):
        for vi in range(4):
            for y4 in range(4):
                il = [y4, 4 + y4, 3 - y4, 7 - y4][vi]
                sign = -1.0 if vi > 1 and p == 1 else 1.0
                folding[vi, y4, :, c, il, :] = sign * u_n[q * half : (q + 1) * half].T
    folding = folding.reshape(4 * 128, 4 * 128)
    plain = {"fold": folding, "unfold": folding.T}

    inner = s_l[:, W : W + n] @ u_n.T / 2
    f1 = [inner[p::2, p * half : (p + 1) * half] for p in (0, 1)]
    a1 = [(u_b @ a_full)[p * hb : (p + 1) * hb, p::2] for p in (0, 1)]
    b1 = [b_full[p::2, p::2] for p in (0, 1)]
    keep, pick = np.eye(hb), np.concatenate([np.zeros((hn, hb)), np.eye(hn)], axis=1)
    keep = np.concatenate([keep, np.zeros((hb, hn))], axis=1)
    for p in (0, 1):
        big["fy%d" % p] = np.kron(f1[p].T, np.eye(half))
        high, low = split(np.kron(np.eye(8), f1[p].T))
        plain["fz%d" % p] = np.concatenate([high, high, low])
        plain["bz%d" % p] = np.concatenate(
            split(np.kron(np.eye(8), np.concatenate([a1[p], b1[p]]).T)), axis=1
        )
        sample = np.kron(a1[p], keep).T
        slab = np.kron(s_l[picks][:, p::2], pick).T
        big["by%d" % p] = np.concatenate(
            [sample, sample, slab, slab, np.kron(b1[p], pick).T], axis=1
        )

    unfold = u_b.T / 2
    pair = np.kron(unfold, unfold).reshape(blocks * blocks, 2, hb, 2, hb)

    def from_samples(table):
        folded = np.einsum("os,spaqb->pqabo", table, pair)
        return folded.reshape(4 * quad, table.shape[0])

    bm = basis.T @ middle
    lin_x = from_samples(np.kron(bm, bm)).reshape(4 * quad, NL, NL)
    lin = np.zeros((4 * quad, 384))
    for c, (p, q) in enumerate(CLASSES):
        lin[:, c * wide : (c + 1) * wide] = lin_x[:, p::2, q::2].reshape(4 * quad, wide)
    lin[:, 256:320] = from_samples(np.kron(fine[picks], bm))[:, order]
    big["lin"] = lin
    k1 = [(s_n @ u_n.T / 2)[p::2, p * half : (p + 1) * half] for p in (0, 1)]
    big["near"] = np.concatenate([np.kron(k1[p], k1[q]).T for p, q in CLASSES])
    r1 = [(u_n @ s_n / 2)[p * half : (p + 1) * half, p::2] for p in (0, 1)]
    big["far"] = np.concatenate([np.kron(r1[p], r1[q]).T for p, q in CLASSES])

    second = 2 * np.eye(blocks) - np.eye(blocks, k=1) - np.eye(blocks, k=-1)
    s_y, s_z = sine_table(ny), sine_table(nz)
    proj_z = np.zeros((nz, blocks))
    proj_z[:, margin : margin + cells] = s_z
    edge = interp_table(-1, n + 2, -1, cells + 2, Q)
    depth = interp_table(0, n, 0, cells, Q)
    lateral = edge[1 : n + 1]
    s_ext = np.zeros((ny + 2, ny))
    s_ext[1:-1] = s_y
    sp = np.concatenate([s_n[0::2], s_n[1::2]])
    deep = sp @ depth @ s_z

    def by_class(first, second_table):
        parts = []
        for p, q in CLASSES:
            parts.append(
                np.kron(first[p * half : (p + 1) * half], second_table[q * half : (q + 1) * half])
            )
        return np.concatenate(parts).T

    factor = (2.0 / (ny + 1)) * (2.0 / (nz + 1))
    spread, drop = [], []
    for b in range(n_gy):
        proj_y = np.zeros((ny, blocks))
        for j in range(blocks):
            at = j + b * cells - margin
            if 0 <= at < ny:
                proj_y[:, j] = s_y[:, at]
        flat = np.kron(proj_y, proj_z)
        curved = np.kron(proj_y @ second, proj_z) + np.kron(proj_y, proj_z @ second)
        spread.append(
            factor * np.concatenate([from_samples(curved), from_samples(flat)], axis=1)
        )
        local_s = s_ext[b * cells : b * cells + cells + 2]
        rim = np.outer(sp[:, 0], edge[0] @ local_s) + np.outer(sp[:, n - 1], edge[n + 1] @ local_s)
        drop.append(
            np.concatenate([by_class(sp @ lateral @ local_s, deep), by_class(rim, deep)])
        )
    big["spread"] = np.stack(spread)
    big["drop"] = np.stack(drop)
    sb = s_n @ basis
    sbp = np.concatenate([sb[0::2], sb[1::2]])
    facex = np.zeros((4 * wide, n * n))
    for c, (p, q) in enumerate(CLASSES):
        facex[c * wide : (c + 1) * wide, c * 256 : c * 256 + 256] = np.kron(
            sb[p::2, p::2], sb[q::2, q::2]
        ).T
    big["facex"] = facex
    ends = np.stack([sp[:, 0], sp[:, n - 1], sp[:, 0], sp[:, n - 1]], axis=1)
    big["facey"] = by_class(ends, sbp)[order]

    mu_y, mu_z = eigen_values(ny), eigen_values(nz)
    theta = np.arccosh(1.0 + (mu_y[:, None] + mu_z[None, :]).reshape(1, modes) / 2)
    below = 2 * np.sinh(theta) * (1.0 - np.exp(-2 * theta * (nx + 1)))
    apart = np.abs(np.arange(48) - 20)[:, None]
    toep = (np.exp(-theta * apart) + np.exp(-theta * np.maximum(2 * (nx + 1) - apart, 0))) / below
    total = (np.arange(2 * nx + 32) - 13)[:, None]
    hank = np.exp(-theta * np.maximum(total + 2, 0)) + np.exp(-theta * np.maximum(2 * nx - total, 0))
    hank = hank / below

    u12 = np.zeros((64, 16))
    u12[:32, :10] = np.outer(s_n[:, 0], edge[0]) + np.outer(s_n[:, n - 1], edge[n + 1])
    u12[32:, :10] = s_n @ lateral
    place = np.arange(n_gx)
    mine = []
    for a in range(n_gx):
        rank = np.arange(16)[:, None]
        at = cells * a - margin + rank
        inside = (at >= 0) & (at < nx)
        rightward = inside * np.exp(-theta * (15 - rank)) * (1 - np.exp(-2 * theta * (at + 1) * inside))
        leftward = inside * np.exp(-theta * rank) * (1 - np.exp(-2 * theta * (nx - at) * inside))
        row = np.arange(16)[:, None]
        x = cells * a - 1 + row
        used = row < cells + 2
        falling = used * np.exp(-theta * row) * (1 - np.exp(-2 * theta * np.maximum(nx - x, 0))) / below
        rising = (
            used
            * np.exp(-theta * np.maximum(cells + 1 - row, 0))
            * (1 - np.exp(-2 * theta * (x + 1)))
            / below
        )
        away = (a - place)[:, None]
        before = (away >= 2) * np.exp(-theta * np.maximum(cells * away - 12, 0))
        after = (away <= -2) * np.exp(-theta * np.maximum(-cells * away - 12, 0))
        mine.append(
            np.concatenate([rightward, leftward, u12 @ falling, u12 @ rising, before, after])
        )
    singles = {
        "mine": np.stack(mine).astype(np.float32),
        "toep": toep.astype(np.float32),
        "hank": hank.astype(np.float32),
    }

    mu_l, mu_n = eigen_values(length), eigen_values(n)
    sums = np.ones((8, hl * hl))
    for c, (p, q) in enumerate(CLASSES):
        sums[c] = (mu_l[p::2][:, None] + mu_l[q::2][None, :]).ravel()
    sums[4, : n * n] = np.concatenate(
        [(mu_n[p::2][:, None] + mu_n[q::2][None, :]).ravel() for p, q in CLASSES]
    )
    singles["sums"] = sums.astype(np.float32)
    columns, column_places = pack(
        {"mul": mu_l[:, None], "mun": mu_n[:, None], "ends": s_n[:, [0, n - 1]]}, 8
    )
    singles["columns"] = columns.astype(np.float32)

    scale = (2.0 / (length + 1)) ** 3
    flat = np.zeros((24, length))
    flat[:4] = fine[picks] @ a_full * scale
    flat[8:24] = bm @ a_full * scale
    lefts = {
        "sl": s_l[:, W : W + n],
        "source": np.concatenate([a_full, second @ a_full], axis=1) * scale,
        "flat": flat,
        "picks": s_l[picks] * scale,
        "coefs": b_full * scale,
        "sn": s_n,
        "u12": u12,
        "sb": sb,
    }
    left, left_places = pack(lefts, 16)
    doubled, row, spots = [], 0, {}
    for name, (start, rows, cols) in left_places.items():
        doubled += list(split(left[start : start + rows]))
        spots[name] = (row, rows, cols)
        row += 2 * rows
    singles["lefts"] = np.concatenate(doubled)
    for name, value in plain.items():
        singles[name] = value.astype(ml_dtypes.bfloat16)
    for name, value in big.items():
        singles[name] = np.stack(split(value), axis=value.ndim - 2)
    return singles, column_places, spots


def halves(value):
    high = value.astype(jnp.bfloat16)
    return high, (value - high.astype(jnp.float32)).astype(jnp.bfloat16)


def mm(left, right):
    return jnp.dot(left, right, preferred_element_type=jnp.float32)


def right_mul(value, high_table, low_table):
    rows = value.shape[0]
    high, low = halves(value)
    both = mm(jnp.concatenate([high, low], axis=0), high_table)
    return both[:rows] + both[rows:] + mm(high, low_table)


NAMES = [
    "charge", "fold", "lefts", "fy0", "fy1", "fz0", "sums", "columns", "bz0", "fz1", "bz1", "by0", "by1",
    "spread", "mine", "lin", "near", "facex", "facey", "toep", "hank", "drop", "far", "unfold",
]


def window(name, shape):
    if name in ("spread", "drop", "mine"):
        return shape[1:]
    if name == "hank":
        return (48,) + shape[1:]
    return shape


def kernel(column_places, spots, n_gx, n_gy, *refs):
    count = len(NAMES)
    hbm = dict(zip(NAMES, refs[:count]))
    out_ref = refs[count]
    vmem = dict(zip(NAMES, refs[count + 1 : 2 * count + 1]))
    (
        mom_ref, far_ref, near_ref, cx_ref, cy_ref, rx_ref, ry_ref,
        load_sem, f_send, f_recv, p_send, p_recv, c_send, c_recv,
    ) = refs[2 * count + 1 :]
    ndev = n_gx * n_gy
    a = lax.axis_index("gx")
    b = lax.axis_index("gy")
    me = a * n_gy + b
    n, cells = P_SIZE, P_SIZE // Q

    loads = {}
    for i, name in enumerate(NAMES):
        source = hbm[name]
        if name in ("spread", "drop"):
            source = source.at[b]
        if name == "mine":
            source = source.at[a]
        if name == "hank":
            source = source.at[pl.ds(pl.multiple_of(a * 16, 16), 48)]
        loads[name] = pltpu.make_async_copy(source, vmem[name], load_sem.at[i])
        loads[name].start()

    barrier = pltpu.get_barrier_semaphore()

    def greet(r, carry):
        peer = lax.rem(me + r, ndev)
        pl.semaphore_signal(
            barrier, inc=1, device_id=(peer // n_gy, lax.rem(peer, n_gy)), device_id_type=MESH
        )
        return carry

    with jax.named_scope("greet"):
        lax.fori_loop(1, ndev, greet, 0)

    def ready(*wanted):
        for name in wanted:
            loads[name].wait()

    def table(name):
        return vmem[name][0], vmem[name][1]

    def column(name):
        row, rows, cols = column_places[name]
        return vmem["columns"][row : row + rows, 0:cols]

    def left_mul(name, value):
        row, rows, cols = spots[name]
        high, low = halves(value)
        both = mm(vmem["lefts"][row : row + 2 * rows, 0:cols], high)
        rest = mm(vmem["lefts"][row : row + rows, 0:cols], low)
        return both[:rows] + both[rows:] + rest

    groups = [[0, 1, 7, 6], [2, 3, 5, 4]]
    with jax.named_scope("fold"):
        with jax.named_scope("f_w"):
            ready("charge", "fold", "lefts")
        sides = [
            jnp.concatenate([vmem["charge"][:, v * 128 : (v + 1) * 128] for v in group], axis=1)
            for group in groups
        ]
        high, low = halves(jnp.concatenate(sides, axis=0))
        both = mm(jnp.concatenate([high, low], axis=0), vmem["fold"][...])
        both = both[: 2 * n] + both[2 * n :]
        folded = jnp.concatenate(
            [
                both[s * n : (s + 1) * n, c * 128 : (c + 1) * 128]
                for c in range(4)
                for s in range(2)
            ],
            axis=1,
        )
        wide = left_mul("sl", folded)

    half = n + 2 * W

    def along_y(p):
        pair = [wide[:, c * 256 : (c + 1) * 256] for c in (2 * p, 2 * p + 1)]
        return right_mul(jnp.concatenate(pair, axis=0), *table("fy%d" % p))

    def along_z(q, lifts):
        rows = [
            lift[q * half : (q + 1) * half, k * 128 : (k + 1) * 128]
            for lift in lifts
            for k in range(4)
        ]
        high, low = halves(jnp.concatenate(rows, axis=0))
        weights = vmem["fz%d" % q]
        return mm(jnp.concatenate([high, low], axis=1), weights[0:256]) + mm(high, weights[256:384])

    def divided(q, spectrum):
        parts = []
        for p in range(2):
            for k in range(4):
                at = (4 * p + k) * half
                divisor = column("mul") + vmem["sums"][2 * p + q : 2 * p + q + 1, k * 256 : (k + 1) * 256]
                parts.append(spectrum[at : at + half] / divisor)
        return jnp.concatenate(parts, axis=0)

    def back_z(q, spectrum):
        high, low = halves(spectrum)
        both = mm(jnp.concatenate([high, low], axis=0), vmem["bz%d" % q][...])
        rows = spectrum.shape[0]
        return both[:rows, :128] + both[rows:, :128] + both[:rows, 128:]

    def back_y(p, drops):
        rows = []
        for drop in drops:
            parts = [drop[(4 * p + k) * half : (4 * p + k + 1) * half] for k in range(4)]
            rows.append(jnp.concatenate(parts, axis=1))
        both = right_mul(jnp.concatenate(rows, axis=0), *table("by%d" % p))
        return both[:half], both[half:]

    with jax.named_scope("k_wy"):
        ready("fy0", "fy1")
    with jax.named_scope("k_y"):
        lifts = [along_y(0), along_y(1)]
    with jax.named_scope("k_wz"):
        ready("fz0", "fz1", "sums", "columns")
    with jax.named_scope("k_z"):
        up0 = along_z(0, lifts)
        up1 = along_z(1, lifts)
    with jax.named_scope("k_d"):
        up0 = divided(0, up0)
        up1 = divided(1, up1)
    with jax.named_scope("k_wb"):
        ready("bz0", "bz1", "by0", "by1")
    with jax.named_scope("k_bz"):
        drops = [back_z(0, up0), back_z(1, up1)]
    with jax.named_scope("k_by"):
        y0, y1 = back_y(0, drops)
        y2, y3 = back_y(1, drops)
    with jax.named_scope("spread"):
        lane = lax.broadcasted_iota(jnp.int32, (half, 128), 1)
        sample = jnp.concatenate(
            [jnp.where(lane < 64, u[:, :128], v[:, :128]) for u, v in ((y0, y1), (y2, y3))], axis=1
        )
        ready("spread", "mine")
        modes = near_ref.shape[-1]
        spread = right_mul(sample, *table("spread"))
        packet = left_mul("source", jnp.concatenate([spread[:, :modes], spread[:, modes:]], axis=0))
        near_ref[1, b] = packet
        mine = vmem["mine"]
        rightward = jnp.sum(packet * mine[0:16], axis=0, keepdims=True)
        leftward = jnp.sum(packet * mine[16:32], axis=0, keepdims=True)
        for g in range(modes // 128):
            mom_ref[g, 0:1] = rightward[:, g * 128 : (g + 1) * 128]
            mom_ref[g, 1:2] = leftward[:, g * 128 : (g + 1) * 128]

    with jax.named_scope("barrier"):
        pl.semaphore_wait(barrier, ndev - 1)

    def remote(source, target, send, recv, device):
        return pltpu.make_async_remote_copy(
            src_ref=source,
            dst_ref=target,
            send_sem=send,
            recv_sem=recv,
            device_id=device,
            device_id_type=MESH,
        )

    def start_far(r, carry):
        d = n_gx - r
        for j in range(n_gy):

            @pl.when(a + d < n_gx)
            def _():
                remote(
                    mom_ref.at[:, pl.ds(0, 1)],
                    far_ref.at[b, :, pl.ds(a, 1)],
                    f_send,
                    f_recv,
                    (a + d, j),
                ).start()

            @pl.when(a >= d)
            def _():
                remote(
                    mom_ref.at[:, pl.ds(1, 1)],
                    far_ref.at[b, :, pl.ds(a, 1)],
                    f_send,
                    f_recv,
                    (a - d, j),
                ).start()

        return carry

    def for_near(act):
        for step in (0, 1, 2):
            for j in range(n_gy):
                other = a + step - 1
                fine = (other >= 0) & (other < n_gx)
                if step == 1:
                    fine = b != j

                @pl.when(fine)
                def _():
                    act(step, j, (other, j))

    with jax.named_scope("send"):
        lax.fori_loop(1, n_gx - 1, start_far, 0)

        def send_near(step, j, device):
            remote(
                near_ref.at[1, b],
                near_ref.at[2 - step, b],
                p_send.at[step, j],
                p_recv.at[2 - step, b],
                device,
            ).start()

        for_near(send_near)

    with jax.named_scope("lin"):
        ready("lin")
        coef = jnp.concatenate([u[:, 128:] for u in (y0, y1, y2, y3)], axis=1)
        slab = jnp.where(lane < 32, y0[:, 128:] + y2[:, 128:], y1[:, 128:] + y3[:, 128:])
        flat = right_mul(left_mul("flat", sample), *table("lin"))
        coef = left_mul("picks", coef)[0:8]
        cx = jnp.concatenate(
            [
                jnp.where(
                    lane[0:8] < 64,
                    pltpu.roll(coef[:, c * 128 : (c + 1) * 128], 64, 1),
                    coef[:, (c + 1) * 128 : (c + 2) * 128],
                )
                for c in (0, 2)
            ],
            axis=1,
        )
        cx = cx - flat[0:8, 0:256]
        cy = left_mul("coefs", slab) - flat[8:24, 256:384]
        cx_ref[...] = cx
        cy_ref[...] = cy

    upper, lower = lax.rem(b + 1, n_gy), lax.rem(b + n_gy - 1, n_gy)
    go_right = remote(cx_ref.at[pl.ds(2, 1)], rx_ref.at[pl.ds(0, 1)], c_send.at[0], c_recv.at[0], (a + 1, b))
    go_left = remote(cx_ref.at[pl.ds(1, 1)], rx_ref.at[pl.ds(1, 1)], c_send.at[1], c_recv.at[1], (a - 1, b))
    go_up = remote(cy_ref, ry_ref.at[0], c_send.at[2], c_recv.at[2], (a, upper))
    go_down = remote(cy_ref, ry_ref.at[1], c_send.at[3], c_recv.at[3], (a, lower))

    with jax.named_scope("sendc"):

        @pl.when(a < n_gx - 1)
        def _():
            go_right.start()

        @pl.when(a > 0)
        def _():
            go_left.start()

        go_up.start()
        go_down.start()

    with jax.named_scope("near"):
        ready("near")
        narrow = left_mul("sn", folded)
        spectrum = jnp.concatenate(
            [
                right_mul(
                    narrow[:, c * 256 : (c + 1) * 256],
                    vmem["near"][0, c * 256 : (c + 1) * 256],
                    vmem["near"][1, c * 256 : (c + 1) * 256],
                )
                for c in range(4)
            ],
            axis=1,
        )
        scale = (2.0 / (n + 1)) ** 3
        inverse = scale / (column("mun") + vmem["sums"][4:5, 0 : n * n])

    with jax.named_scope("wait_c"):

        @pl.when(a < n_gx - 1)
        def _():
            go_right.wait_send()
            go_left.wait_recv()

        @pl.when(a > 0)
        def _():
            go_left.wait_send()
            go_right.wait_recv()

        go_up.wait()
        go_down.wait()

    with jax.named_scope("face"):
        ready("facex", "facey")
        from_left = jnp.where(a > 0, rx_ref[0:1], 0.0)
        from_right = jnp.where(a < n_gx - 1, rx_ref[1:2], 0.0)
        ends = jnp.concatenate(
            [cx[0:1] + from_left, cx[3:4] + from_right, jnp.zeros((6, cx.shape[1]), jnp.float32)]
        )
        ends = right_mul(ends, *table("facex"))
        spectrum = spectrum + column("ends")[:, 0:1] * ends[0:1]
        spectrum = spectrum + column("ends")[:, 1:2] * ends[1:2]
        group = jnp.where(lane[0:16] < 64, lax.rem(lane[0:16], 32) // 8, 4)
        total = jnp.where((group == 0) | (group == 3), cy, 0.0)
        total = total + jnp.where((group == 2) & (b > 0), ry_ref[0], 0.0)
        total = total + jnp.where((group == 1) & (b < n_gy - 1), ry_ref[1], 0.0)
        spectrum = spectrum + right_mul(left_mul("sb", total)[:, 0:64], *table("facey"))

    with jax.named_scope("wait_p"):

        def wait_near(step, j, device):
            remote(
                near_ref.at[1, b], near_ref.at[step, j], p_send.at[step, j], p_recv.at[step, j], device
            ).wait()

        for_near(wait_near)

    with jax.named_scope("green"):
        ready("toep", "hank")
        row = lax.broadcasted_iota(jnp.int32, (8, modes), 0)

        def gathered(step):
            value = near_ref[step, 0]
            for j in range(1, n_gy):
                value = value + near_ref[step, j]
            return value

        past = jnp.where(a > 0, gathered(0), 0.0)
        here = gathered(1)
        next_ = jnp.where(a < n_gx - 1, gathered(2), 0.0)
        source = jnp.concatenate(
            [
                jnp.where((row >= 4) | (a > 1), past[0:8], 0.0),
                past[8:16] + jnp.where((row >= 4) | (a > 0), here[0:8], 0.0),
                jnp.where((row < 4) | (a < n_gx - 1), here[8:16] + next_[0:8], 0.0),
                jnp.where((row < 4) | (a < n_gx - 2), next_[8:16], 0.0),
            ]
        )
        values = []
        for i in range(cells + 2):
            influence = vmem["toep"][9 - i : 41 - i] - vmem["hank"][i : i + 32]
            values.append(jnp.sum(influence * source, axis=0, keepdims=True))
        values.append(jnp.zeros((16 - len(values), modes), jnp.float32))
        lifted = left_mul("u12", jnp.concatenate(values, axis=0))

    with jax.named_scope("wait_f"):

        def settle(each):
            block = far_ref.at[:, :, pl.ds(0, each)]
            remote(block, block, f_send, f_recv, (a, b)).wait()

        edge = (a == 0) | (a == n_gx - 1)

        @pl.when(edge)
        def _():
            settle(n_gx - 2)

        @pl.when(jnp.logical_not(edge))
        def _():
            settle(n_gx - 3)

    with jax.named_scope("final"):
        origin = lax.broadcasted_iota(jnp.int32, (n_gx, modes), 0)
        before = jnp.zeros((n_gx, modes), jnp.float32)
        after = before
        for j in range(n_gy):
            sent = jnp.concatenate([far_ref[j, g] for g in range(modes // 128)], axis=1)
            before = before + jnp.where(origin <= a - 2, sent, 0.0)
            after = after + jnp.where(origin >= a + 2, sent, 0.0)
        before = jnp.sum(before * mine[160 : 160 + n_gx], axis=0, keepdims=True)
        after = jnp.sum(after * mine[160 + n_gx : 160 + 2 * n_gx], axis=0, keepdims=True)
        lifted = lifted + mine[32:96] * before + mine[96:160] * after
        ready("drop", "far", "unfold")
        spectrum = spectrum + right_mul(
            jnp.concatenate([lifted[:n], lifted[n:]], axis=1), *table("drop")
        )
        spectrum = left_mul("sn", spectrum * inverse)
        parts = [
            right_mul(
                spectrum[:, c * 256 : (c + 1) * 256],
                vmem["far"][0, c * 256 : (c + 1) * 256],
                vmem["far"][1, c * 256 : (c + 1) * 256],
            )
            for c in range(4)
        ]
    with jax.named_scope("unfold"):
        sides = [
            jnp.concatenate([part[:, s * 128 : (s + 1) * 128] for part in parts], axis=1)
            for s in range(2)
        ]
        high, low = halves(jnp.concatenate(sides, axis=0))
        both = mm(jnp.concatenate([high, low], axis=0), vmem["unfold"][...])
        both = both[: 2 * n] + both[2 * n :]
        for s, group in enumerate(groups):
            for i, v in enumerate(group):
                out_ref[:, v * 128 : (v + 1) * 128] = both[
                    s * n : (s + 1) * n, i * 128 : (i + 1) * 128
                ]


def emit(in_ref, out_ref, sem):
    copy = pltpu.make_async_copy(in_ref, out_ref, sem)
    copy.start()
    copy.wait()


def body(n_gx, n_gy, charge):
    singles, column_places, spots = tables(n_gx, n_gy)
    arrays = [charge] + [jnp.asarray(singles[name]) for name in NAMES[1:]]
    scratch = [
        pltpu.VMEM(window(name, array.shape), array.dtype) for name, array in zip(NAMES, arrays)
    ]
    modes = n_gy * (P_SIZE // Q) ** 2
    scratch += [
        pltpu.VMEM((modes // 128, 8, 128), jnp.float32),
        pltpu.VMEM((n_gy, modes // 128, n_gx, 128), jnp.float32),
        pltpu.VMEM((3, n_gy, 16, modes), jnp.float32),
        pltpu.VMEM((8, 256), jnp.float32),
        pltpu.VMEM((16, 128), jnp.float32),
        pltpu.VMEM((8, 256), jnp.float32),
        pltpu.VMEM((2, 16, 128), jnp.float32),
        pltpu.SemaphoreType.DMA((len(NAMES),)),
        pltpu.SemaphoreType.DMA,
        pltpu.SemaphoreType.DMA,
        pltpu.SemaphoreType.DMA((3, n_gy)),
        pltpu.SemaphoreType.DMA((3, n_gy)),
        pltpu.SemaphoreType.DMA((4,)),
        pltpu.SemaphoreType.DMA((4,)),
    ]
    hbm = pl.BlockSpec(memory_space=pl.ANY)
    vm = pl.BlockSpec(memory_space=pltpu.VMEM)
    solved = pl.pallas_call(
        functools.partial(kernel, column_places, spots, n_gx, n_gy),
        out_shape=pltpu.VMEM(charge.shape, charge.dtype),
        in_specs=[hbm] * len(NAMES),
        out_specs=vm,
        scratch_shapes=scratch,
        name="mlc",
        compiler_params=pltpu.CompilerParams(
            collective_id=0, has_side_effects=True, vmem_limit_bytes=60 * 1024 * 1024
        ),
    )(*arrays)
    return pl.pallas_call(
        emit,
        out_shape=jax.ShapeDtypeStruct(charge.shape, charge.dtype),
        in_specs=[vm],
        out_specs=hbm,
        scratch_shapes=[pltpu.SemaphoreType.DMA],
        name="emit",
        compiler_params=pltpu.CompilerParams(vmem_limit_bytes=1024 * 1024),
    )(solved)


def solution(mesh):
    run = functools.partial(body, mesh.shape["gx"], mesh.shape["gy"])
    spec = P("gx", "gy")
    return jax.shard_map(run, mesh=mesh, in_specs=(spec,), out_specs=spec, check_vma=False)
```

```python
import functools

import jax
import jax.numpy as jnp
import ml_dtypes
import numpy as np
from jax import lax
from jax.experimental import pallas as pl
from jax.experimental.pallas import tpu as pltpu
from jax.sharding import PartitionSpec as P

P_SIZE = 32
W = 16
Q = 4
NL = 16
CLASSES = [(0, 0), (0, 1), (1, 0), (1, 1)]
MESH = pl.DeviceIdType.MESH


def sine_table(length):
    counter = np.arange(length) + 1
    return np.sin(np.pi * np.outer(counter, counter) / (length + 1))


def eigen_values(length):
    return 2.0 - 2.0 * np.cos(np.pi * (np.arange(length) + 1) / (length + 1))


def interp_table(fine_start, fine_count, coarse_start, coarse_count, ratio):
    fine_pos = np.arange(fine_count) + fine_start
    coarse_pos = np.arange(coarse_count) + coarse_start
    numerator = 2 * fine_pos - (ratio - 1)
    lower = numerator // (2 * ratio)
    weight = ((numerator - 2 * ratio * lower) / (2 * ratio))[:, None]
    below = coarse_pos[None, :] == lower[:, None]
    above = coarse_pos[None, :] == lower[:, None] + 1
    return below * (1.0 - weight) + above * weight


def legendre_basis(length, count):
    points = (2.0 * np.arange(length) + 1.0) / length - 1.0
    columns = [np.ones_like(points), points]
    for degree in range(2, count):
        columns.append(
            ((2 * degree - 1) * points * columns[-1] - (degree - 1) * columns[-2]) / degree
        )
    result = []
    for vector in columns[:count]:
        for passes in range(2):
            for earlier in result:
                vector = vector - np.sum(earlier * vector) * earlier
        result.append(vector / np.sqrt(np.sum(vector * vector)))
    return np.stack(result, axis=1)


def fold(length):
    half = length // 2
    eye = np.eye(length)
    return np.concatenate([eye[:half] + eye[::-1][:half], eye[:half] - eye[::-1][:half]])


def split(table):
    high = table.astype(ml_dtypes.bfloat16)
    low = (table - high.astype(np.float64)).astype(ml_dtypes.bfloat16)
    return high, low


@functools.lru_cache(maxsize=None)
def tables(n_gx, n_gy):
    n, length, cells = P_SIZE, P_SIZE + 2 * W, P_SIZE // Q
    blocks, margin = length // Q, W // Q
    half, hl, hb, hn = n // 2, length // 2, blocks // 2, NL // 2
    quad, wide = hb * hb, hn * hn
    nx, ny, nz = n_gx * cells, n_gy * cells, cells
    modes = ny * nz
    s_l, s_n = sine_table(length), sine_table(n)
    u_n, u_b = fold(n), fold(blocks)
    basis = legendre_basis(n, NL)
    average = np.kron(np.eye(blocks), np.full((1, Q), 1.0 / Q))
    fine = interp_table(0, length, 0, blocks, Q)
    middle = fine[W : W + n]
    picks = [W - 1, W, W + n - 1, W + n]
    a_full = average @ s_l
    b_full = basis.T @ s_l[W : W + n]
    order = np.arange(4 * NL).reshape(4, hn, 2).transpose(2, 0, 1).ravel()
    big = {}

    folding = np.zeros((2, 4, n, 2, 2, 4, half))
    for p, q in CLASSES:
        for y4 in range(4):
            piece = u_n[q * half : (q + 1) * half].T
            folding[0, y4, :, p, q, y4, :] = piece
            folding[1, y4, :, p, q, 3 - y4, :] = piece if p == 0 else -piece
    plain = {"fold": folding.reshape(256, 256)}
    folding = np.zeros((4, 4, n, 4, 2 * 4, half))
    for c, (p, q) in enumerate(CLASSES):
        for vi in range(4):
            for y4 in range(4):
                il = [y4, 4 + y4, 3 - y4, 7 - y4][vi]
                sign = -1.0 if vi > 1 and p == 1 else 1.0
                folding[vi, y4, :, c, il, :] = sign * u_n[q * half : (q + 1) * half].T
    folding = folding.reshape(4 * 128, 4 * 128)
    plain["unfold"] = folding.T

    inner = s_l[:, W : W + n] @ u_n.T / 2
    f1 = [inner[p::2, p * half : (p + 1) * half] for p in (0, 1)]
    a1 = [(u_b @ a_full)[p * hb : (p + 1) * hb, p::2] for p in (0, 1)]
    b1 = [b_full[p::2, p::2] for p in (0, 1)]
    keep, pick = np.eye(hb), np.concatenate([np.zeros((hn, hb)), np.eye(hn)], axis=1)
    keep = np.concatenate([keep, np.zeros((hb, hn))], axis=1)
    for p in (0, 1):
        big["fy%d" % p] = np.kron(f1[p].T, np.eye(half))
        high, low = split(np.kron(np.eye(8), f1[p].T))
        plain["fz%d" % p] = np.concatenate([high, high])
        plain["gz%d" % p] = low
        plain["bz%d" % p] = np.concatenate(
            split(np.kron(np.eye(8), np.concatenate([a1[p], b1[p]]).T)), axis=1
        )
        sample = np.kron(a1[p], keep).T
        slab = np.kron(s_l[picks][:, p::2], pick).T
        big["by%d" % p] = np.concatenate(
            [sample, sample, slab, slab, np.kron(b1[p], pick).T], axis=1
        )

    unfold = u_b.T / 2
    pair = np.kron(unfold, unfold).reshape(blocks * blocks, 2, hb, 2, hb)

    def from_samples(table):
        folded = np.einsum("os,spaqb->pqabo", table, pair)
        return folded.reshape(4 * quad, table.shape[0])

    bm = basis.T @ middle
    lin_x = from_samples(np.kron(bm, bm)).reshape(4 * quad, NL, NL)
    lin = np.zeros((4 * quad, 384))
    for c, (p, q) in enumerate(CLASSES):
        lin[:, c * wide : (c + 1) * wide] = lin_x[:, p::2, q::2].reshape(4 * quad, wide)
    lin[:, 256:320] = from_samples(np.kron(fine[picks], bm))[:, order]
    big["lin"] = lin
    k1 = [(s_n @ u_n.T / 2)[p::2, p * half : (p + 1) * half] for p in (0, 1)]
    for c, (p, q) in enumerate(CLASSES):
        big["near%d" % c] = np.kron(k1[p], k1[q]).T
    r1 = [(u_n @ s_n / 2)[p * half : (p + 1) * half, p::2] for p in (0, 1)]
    for c, (p, q) in enumerate(CLASSES):
        big["far%d" % c] = np.kron(r1[p], r1[q]).T

    second = 2 * np.eye(blocks) - np.eye(blocks, k=1) - np.eye(blocks, k=-1)
    s_y, s_z = sine_table(ny), sine_table(nz)
    proj_z = np.zeros((nz, blocks))
    proj_z[:, margin : margin + cells] = s_z
    edge = interp_table(-1, n + 2, -1, cells + 2, Q)
    depth = interp_table(0, n, 0, cells, Q)
    lateral = edge[1 : n + 1]
    s_ext = np.zeros((ny + 2, ny))
    s_ext[1:-1] = s_y
    sp = np.concatenate([s_n[0::2], s_n[1::2]])
    deep = sp @ depth @ s_z

    def by_class(first, second_table):
        parts = []
        for p, q in CLASSES:
            parts.append(
                np.kron(first[p * half : (p + 1) * half], second_table[q * half : (q + 1) * half])
            )
        return np.concatenate(parts).T

    factor = (2.0 / (ny + 1)) * (2.0 / (nz + 1))
    spread, drop = [], []
    for b in range(n_gy):
        proj_y = np.zeros((ny, blocks))
        for j in range(blocks):
            at = j + b * cells - margin
            if 0 <= at < ny:
                proj_y[:, j] = s_y[:, at]
        flat = np.kron(proj_y, proj_z)
        curved = np.kron(proj_y @ second, proj_z) + np.kron(proj_y, proj_z @ second)
        spread.append(
            factor * np.concatenate([from_samples(curved), from_samples(flat)], axis=1)
        )
        local_s = s_ext[b * cells : b * cells + cells + 2]
        rim = np.outer(sp[:, 0], edge[0] @ local_s) + np.outer(sp[:, n - 1], edge[n + 1] @ local_s)
        drop.append(
            np.concatenate([by_class(sp @ lateral @ local_s, deep), by_class(rim, deep)])
        )
    big["spread"] = np.stack(spread)
    big["drop"] = np.stack(drop)
    sb = s_n @ basis
    sbp = np.concatenate([sb[0::2], sb[1::2]])
    facex = np.zeros((4 * wide, n * n))
    for c, (p, q) in enumerate(CLASSES):
        facex[c * wide : (c + 1) * wide, c * 256 : c * 256 + 256] = np.kron(
            sb[p::2, p::2], sb[q::2, q::2]
        ).T
    big["facex"] = facex
    ends = np.stack([sp[:, 0], sp[:, n - 1], sp[:, 0], sp[:, n - 1]], axis=1)
    big["facey"] = by_class(ends, sbp)[order]

    mu_y, mu_z = eigen_values(ny), eigen_values(nz)
    theta = np.arccosh(1.0 + (mu_y[:, None] + mu_z[None, :]).reshape(1, modes) / 2)
    below = 2 * np.sinh(theta) * (1.0 - np.exp(-2 * theta * (nx + 1)))
    apart = np.abs(np.arange(48) - 20)[:, None]
    toep = (np.exp(-theta * apart) + np.exp(-theta * np.maximum(2 * (nx + 1) - apart, 0))) / below
    total = (np.arange(2 * nx + 32) - 13)[:, None]
    hank = np.exp(-theta * np.maximum(total + 2, 0)) + np.exp(-theta * np.maximum(2 * nx - total, 0))
    hank = hank / below

    u12 = np.zeros((64, 16))
    u12[:32, :10] = np.outer(s_n[:, 0], edge[0]) + np.outer(s_n[:, n - 1], edge[n + 1])
    u12[32:, :10] = s_n @ lateral
    place = np.arange(n_gx)
    mine = []
    for a in range(n_gx):
        rank = np.arange(16)[:, None]
        at = cells * a - margin + rank
        inside = (at >= 0) & (at < nx)
        rightward = inside * np.exp(-theta * (15 - rank)) * (1 - np.exp(-2 * theta * (at + 1) * inside))
        leftward = inside * np.exp(-theta * rank) * (1 - np.exp(-2 * theta * (nx - at) * inside))
        row = np.arange(16)[:, None]
        x = cells * a - 1 + row
        used = row < cells + 2
        falling = used * np.exp(-theta * row) * (1 - np.exp(-2 * theta * np.maximum(nx - x, 0))) / below
        rising = (
            used
            * np.exp(-theta * np.maximum(cells + 1 - row, 0))
            * (1 - np.exp(-2 * theta * (x + 1)))
            / below
        )
        away = (a - place)[:, None]
        before = (away >= 2) * np.exp(-theta * np.maximum(cells * away - 12, 0))
        after = (away <= -2) * np.exp(-theta * np.maximum(-cells * away - 12, 0))
        mine.append(
            np.concatenate(
                [
                    rightward,
                    leftward,
                    u12 @ falling,
                    u12 @ rising,
                    toep,
                    hank[2 * cells * a : 2 * cells * a + 48],
                    before,
                    after,
                ]
            )
        )
    mu_l, mu_n = eigen_values(length), eigen_values(n)
    reciprocal = []
    for q in (0, 1):
        for p in (0, 1):
            pair_sum = (mu_l[p::2][:, None] + mu_l[q::2][None, :]).reshape(4, 1, 256)
            reciprocal.append((1.0 / (mu_l[None, :, None] + pair_sum)).reshape(4 * length, 256))
    for p, q in CLASSES:
        pair_sum = (mu_n[p::2][:, None] + mu_n[q::2][None, :]).reshape(1, 256)
        reciprocal.append((2.0 / (n + 1)) ** 3 / (mu_n[:, None] + pair_sum))
    ends = np.zeros((n, 256))
    ends[:, :2] = s_n[:, [0, n - 1]]
    reciprocal.append(ends)

    scale = (2.0 / (length + 1)) ** 3
    flat = np.zeros((32, length))
    flat[:4] = fine[picks] @ a_full * scale
    flat[16:] = bm @ a_full * scale
    lefts = {
        "sl": s_l[:, W : W + n],
        "source": np.concatenate([a_full, second @ a_full], axis=1) * scale,
        "flat": flat,
        "picks": np.concatenate([s_l[picks] * scale, np.zeros((12, length))]),
        "coefs": b_full * scale,
        "sn": s_n,
        "u12": u12,
        "sb": sb,
    }
    big.update(lefts)
    singles = {
        "mine": np.stack(mine).astype(np.float32),
        "recip": np.concatenate(reciprocal).astype(np.float32),
    }
    places = {}
    for group, names in GROUPS.items():
        packs, row = [], 0
        for name in names:
            if name in plain:
                parts = [plain[name].astype(ml_dtypes.bfloat16)]
            else:
                parts = split(big[name])
            depth, width = parts[0].shape[-2:]
            place = {"left": (row, depth, width)}
            lefty = name in lefts
            step = 256 if not lefty else width
            tiles = []
            for part in parts:
                start = row
                for at in range(0, width, step):
                    tile = np.zeros(part.shape[:-1] + (256,), ml_dtypes.bfloat16)
                    piece = part[..., at : at + step]
                    tile[..., : piece.shape[-1]] = piece
                    packs.append(tile)
                    tiles.append((row, depth))
                    row += depth
            count = len(tiles) // len(parts)
            place["tiles"] = [tiles[k * count : (k + 1) * count] for k in range(len(parts))]
            places[name] = (group, place)
        most = max(tile.ndim for tile in packs)
        if most == 3:
            packs = [np.broadcast_to(tile, (n_gy,) + tile.shape[-2:]) for tile in packs]
        singles[group] = np.concatenate(packs, axis=-2)
    return singles, places


GROUPS = {
    "first": ["fold", "sl"],
    "upy": ["fy0", "fy1"],
    "upz": ["fz0", "gz0", "fz1", "gz1", "bz0", "bz1"],
    "downy": ["by0", "by1", "source"],
    "spread": ["spread"],
    "side": ["flat", "picks", "coefs", "sn", "sb", "u12", "lin"]
    + ["near%d" % c for c in range(4)]
    + ["facex", "facey"],
    "drop": ["drop"],
    "last": ["far%d" % c for c in range(4)] + ["unfold"],
}
NAMES = ["charge", "first", "upy", "upz", "recip", "downy", "spread", "mine", "side", "drop", "last"]


def halves(value):
    high = value.astype(jnp.bfloat16)
    return high, (value - high.astype(jnp.float32)).astype(jnp.bfloat16)


def mm(left, right):
    return jnp.dot(left, right, preferred_element_type=jnp.float32)


def window(name, shape):
    return shape[1:] if name in ("spread", "drop", "mine") else shape


def kernel(places, n_gx, n_gy, *refs):
    count = len(NAMES)
    hbm = dict(zip(NAMES, refs[:count]))
    out_ref = refs[count]
    vmem = dict(zip(NAMES, refs[count + 1 : 2 * count + 1]))
    (
        fold_ref, w_ref, z_ref, b_ref, y_ref,
        mom_ref, far_ref, near_ref, cx_ref, cy_ref, rx_ref, ry_ref, tally_ref,
        load_sem, f_send, f_recv, p_send, p_recv,
    ) = refs[2 * count + 1 :]
    ndev = n_gx * n_gy
    a = lax.axis_index("gx")
    b = lax.axis_index("gy")
    me = a * n_gy + b
    n, cells = P_SIZE, P_SIZE // Q
    half = n + 2 * W
    modes = near_ref.shape[-1]

    loads = {}
    for i, name in enumerate(NAMES):
        source = hbm[name]
        if name in ("spread", "drop"):
            source = source.at[b]
        if name == "mine":
            source = source.at[a]
        loads[name] = pltpu.make_async_copy(source, vmem[name], load_sem.at[i])
        loads[name].start()

    barrier = pltpu.get_barrier_semaphore()

    def greet(r, carry):
        peer = lax.rem(me + r, ndev)
        pl.semaphore_signal(
            barrier, inc=1, device_id=(peer // n_gy, lax.rem(peer, n_gy)), device_id_type=MESH
        )
        return carry

    with jax.named_scope("greet"):
        lax.fori_loop(1, ndev, greet, 0)

    def tile(name, part, i):
        group, place = places[name]
        row, depth = place["tiles"][part][i]
        return vmem[group][row : row + depth, :]

    def table(name, part):
        count = len(places[name][1]["tiles"][part])
        return jnp.concatenate([tile(name, part, i) for i in range(count)], axis=1)

    def right_mul(high, low, name):
        rows = high.shape[0]
        both = mm(jnp.concatenate([high, low], axis=0), table(name, 0))
        return both[:rows] + both[rows:] + mm(high, table(name, 1))

    def left_mul(name, high, low):
        group, place = places[name]
        row, rows, cols = place["left"]
        both = mm(vmem[group][row : row + 2 * rows, 0:cols], high)
        return both[:rows] + both[rows:] + mm(vmem[group][row : row + rows, 0:cols], low)

    groups = [[0, 1, 7, 6], [2, 3, 5, 4]]
    with jax.named_scope("w_charge"):
        loads["charge"].wait()
    with jax.named_scope("w_first"):
        loads["first"].wait()
    with jax.named_scope("fold"):
        charge = vmem["charge"]
        pairs = [
            jnp.concatenate([charge[:, v * 128 : (v + 1) * 128] for v in (u, 7 - u)], axis=1)
            for u in range(4)
        ]
        high, low = halves(jnp.concatenate(pairs, axis=0))
        both = mm(jnp.concatenate([high, low], axis=0), tile("fold", 0, 0))
        both = both[: 4 * n] + both[4 * n :]
        lane = lax.broadcasted_iota(jnp.int32, (half, 128), 1)
        folded = []
        for p in range(2):
            rows = [both[v * n : (v + 1) * n, p * 128 : (p + 1) * 128] for v in range(4)]
            turn = [pltpu.roll(row, 64, 1) for row in rows]
            left = lane[:n] < 64
            folded += [jnp.where(left, rows[v], turn[v + 1]) for v in (0, 2)]
            folded += [jnp.where(left, turn[v], rows[v + 1]) for v in (0, 2)]
        folded = halves(jnp.concatenate(folded, axis=1))
        fold_ref[0] = folded[0]
        fold_ref[1] = folded[1]
        wide = halves(left_mul("sl", *folded))
        for c in range(4):
            at = slice(c * 256, (c + 1) * 256)
            q = c % 2
            w_ref[c // 2, q * half : (q + 1) * half] = wide[0][:, at]
            w_ref[c // 2, (2 + q) * half : (3 + q) * half] = wide[1][:, at]
    with jax.named_scope("w_upy"):
        loads["upy"].wait()
    with jax.named_scope("upy"):
        for p in range(2):
            name = "fy%d" % p
            both = mm(w_ref[p], table(name, 0))
            lift = both[: 2 * half] + both[2 * half :] + mm(w_ref[p, 0 : 2 * half], table(name, 1))
            high, low = halves(lift)
            for q in range(2):
                for k in range(4):
                    at = (4 * p + k) * half
                    rows, lanes = slice(q * half, (q + 1) * half), slice(k * 128, (k + 1) * 128)
                    z_ref[q, at : at + half, 0:128] = high[rows, lanes]
                    z_ref[q, at : at + half, 128:256] = low[rows, lanes]
    with jax.named_scope("w_upz"):
        loads["upz"].wait()
        loads["recip"].wait()
    with jax.named_scope("upz"):
        rows = 8 * half
        for q in range(2):
            up = mm(z_ref[q], tile("fz%d" % q, 0, 0)) + mm(z_ref[q, :, 0:128], tile("gz%d" % q, 0, 0))
            high, low = halves(up * vmem["recip"][q * rows : (q + 1) * rows])
            b_ref[q, 0:rows] = high
            b_ref[q, rows : 2 * rows] = low
    with jax.named_scope("downz"):
        for q in range(2):
            both = mm(b_ref[q], tile("bz%d" % q, 0, 0))
            high, low = halves(both[:rows, :128] + both[rows:, :128] + both[:rows, 128:])
            for p in range(2):
                for k in range(4):
                    at, lanes = (4 * p + k) * half, slice(k * 128, (k + 1) * 128)
                    y_ref[p, q * half : (q + 1) * half, lanes] = high[at : at + half]
                    y_ref[p, (2 + q) * half : (3 + q) * half, lanes] = low[at : at + half]
    with jax.named_scope("w_downy"):
        loads["downy"].wait()
    with jax.named_scope("downy"):
        ys = []
        for p in range(2):
            name = "by%d" % p
            both = mm(y_ref[p], tile(name, 0, 0))
            both = both[: 2 * half] + both[2 * half :] + mm(y_ref[p, 0 : 2 * half], tile(name, 1, 0))
            ys += [both[:half], both[half:]]
        y0, y1, y2, y3 = ys
    with jax.named_scope("w_spread"):
        loads["spread"].wait()
        loads["mine"].wait()
    with jax.named_scope("spread"):
        sample = halves(
            jnp.concatenate(
                [jnp.where(lane < 64, u[:, :128], v[:, :128]) for u, v in ((y0, y1), (y2, y3))],
                axis=1,
            )
        )
        high, low = halves(right_mul(*sample, "spread"))
        packet = left_mul(
            "source",
            jnp.concatenate([high[:, :modes], high[:, modes:]], axis=0),
            jnp.concatenate([low[:, :modes], low[:, modes:]], axis=0),
        )
        near_ref[n_gy + b] = packet
        mine = vmem["mine"]
        rightward = jnp.sum(packet * mine[0:16], axis=0, keepdims=True)
        leftward = jnp.sum(packet * mine[16:32], axis=0, keepdims=True)
        for g in range(modes // 128):
            mom_ref[g, 0:1] = rightward[:, g * 128 : (g + 1) * 128]
            mom_ref[g, 1:2] = leftward[:, g * 128 : (g + 1) * 128]

    with jax.named_scope("barrier"):
        pl.semaphore_wait(barrier, ndev - 1)

    def remote(source, target, send, recv, device):
        return pltpu.make_async_remote_copy(
            src_ref=source,
            dst_ref=target,
            send_sem=send,
            recv_sem=recv,
            device_id=device,
            device_id_type=MESH,
        )

    def start_far(r, carry):
        d = n_gx - r
        for j in range(n_gy):
            for row, other, fine in ((0, a + d, a + d < n_gx), (1, a - d, a >= d)):

                @pl.when(fine)
                def _():
                    remote(
                        mom_ref.at[:, pl.ds(row, 1)],
                        far_ref.at[b, :, pl.ds(a, 1)],
                        f_send,
                        f_recv,
                        (other, j),
                    ).start()

        return carry

    with jax.named_scope("send"):
        lax.fori_loop(1, n_gx - 1, start_far, 0)
        for step in (0, 1, 2):
            for j in range(n_gy):
                other = a + step - 1
                fine = (other >= 0) & (other < n_gx)
                if step == 1:
                    fine = b != j

                @pl.when(fine)
                def _():
                    remote(
                        near_ref.at[n_gy + b],
                        near_ref.at[(2 - step) * n_gy + b],
                        p_send,
                        p_recv,
                        (other, j),
                    ).start()

    with jax.named_scope("w_side"):
        loads["side"].wait()
    with jax.named_scope("lin"):
        coef = halves(jnp.concatenate([u[:, 128:] for u in (y0, y1, y2, y3)], axis=1))
        slab = halves(jnp.where(lane < 32, y0[:, 128:] + y2[:, 128:], y1[:, 128:] + y3[:, 128:]))
        flat = right_mul(*halves(left_mul("flat", *sample)), "lin")
        coef = left_mul("picks", *coef)[0:8]
        cx = jnp.concatenate(
            [
                jnp.where(
                    lane[0:8] < 64,
                    pltpu.roll(coef[:, c * 128 : (c + 1) * 128], 64, 1),
                    coef[:, (c + 1) * 128 : (c + 2) * 128],
                )
                for c in (0, 2)
            ],
            axis=1,
        )
        cx = cx - flat[0:8, 0:256]
        cy = left_mul("coefs", *slab) - flat[16:32, 256:384]
        cx_ref[...] = cx
        cy_ref[...] = cy

    upper, lower = lax.rem(b + 1, n_gy), lax.rem(b + n_gy - 1, n_gy)
    with jax.named_scope("sendc"):

        @pl.when(a < n_gx - 1)
        def _():
            remote(
                cx_ref.at[pl.ds(2, 1)], rx_ref.at[pl.ds(0, 1)], p_send, p_recv, (a + 1, b)
            ).start()

        @pl.when(a > 0)
        def _():
            remote(
                cx_ref.at[pl.ds(1, 1)], rx_ref.at[pl.ds(1, 1)], p_send, p_recv, (a - 1, b)
            ).start()

        remote(cy_ref, ry_ref.at[0], p_send, p_recv, (a, upper)).start()
        remote(cy_ref, ry_ref.at[1], p_send, p_recv, (a, lower)).start()

    with jax.named_scope("near"):
        narrow = halves(left_mul("sn", fold_ref[0], fold_ref[1]))
        spectrum = []
        for c in range(4):
            at = slice(c * 256, (c + 1) * 256)
            spectrum.append(right_mul(narrow[0][:, at], narrow[1][:, at], "near%d" % c))
        spectrum = jnp.concatenate(spectrum, axis=1)

    edge = (a == 0) | (a == n_gx - 1)
    inner = jnp.logical_not(edge)

    def settle_near(sides):
        lines = 16 * (modes // 128) * ((1 + sides) * n_gy - 1) + 2 * sides + 32
        block = tally_ref.at[pl.ds(0, lines)]
        remote(block, block, p_send, p_recv, (a, b)).wait()

    with jax.named_scope("wait_p"):

        @pl.when(edge)
        def _():
            settle_near(1)

        @pl.when(inner)
        def _():
            settle_near(2)

    with jax.named_scope("face"):
        from_left = jnp.where(a > 0, rx_ref[0:1], 0.0)
        from_right = jnp.where(a < n_gx - 1, rx_ref[1:2], 0.0)
        ends = jnp.concatenate(
            [cx[0:1] + from_left, cx[3:4] + from_right, jnp.zeros((14, cx.shape[1]), jnp.float32)]
        )
        ends = right_mul(*halves(ends), "facex")
        fine = 16 * half
        column = vmem["recip"][fine + 4 * n : fine + 5 * n, 0:2]
        spectrum = spectrum + column[:, 0:1] * ends[0:1] + column[:, 1:2] * ends[1:2]
        group = jnp.where(lane[0:16] < 64, lax.rem(lane[0:16], 32) // 8, 4)
        total = jnp.where((group == 0) | (group == 3), cy, 0.0)
        total = total + jnp.where((group == 2) & (b > 0), ry_ref[0], 0.0)
        total = total + jnp.where((group == 1) & (b < n_gy - 1), ry_ref[1], 0.0)
        total = left_mul("sb", *halves(total))[:, 0:64]
        spectrum = spectrum + right_mul(*halves(total), "facey")
    with jax.named_scope("green"):
        row = lax.broadcasted_iota(jnp.int32, (8, modes), 0)

        def gathered(step):
            value = near_ref[step * n_gy]
            for j in range(1, n_gy):
                value = value + near_ref[step * n_gy + j]
            return value

        past = jnp.where(a > 0, gathered(0), 0.0)
        here = gathered(1)
        next_ = jnp.where(a < n_gx - 1, gathered(2), 0.0)
        source = jnp.concatenate(
            [
                jnp.where((row >= 4) | (a > 1), past[0:8], 0.0),
                past[8:16] + jnp.where((row >= 4) | (a > 0), here[0:8], 0.0),
                jnp.where((row < 4) | (a < n_gx - 1), here[8:16] + next_[0:8], 0.0),
                jnp.where((row < 4) | (a < n_gx - 2), next_[8:16], 0.0),
            ]
        )
        values = []
        for i in range(cells + 2):
            influence = mine[169 - i : 201 - i] - mine[208 + i : 240 + i]
            values.append(jnp.sum(influence * source, axis=0, keepdims=True))
        values.append(jnp.zeros((16 - len(values), modes), jnp.float32))
        lifted = left_mul("u12", *halves(jnp.concatenate(values, axis=0)))

    with jax.named_scope("w_last"):
        loads["drop"].wait()
        loads["last"].wait()

    def settle_far(each):
        block = far_ref.at[:, :, pl.ds(0, each)]
        remote(block, block, f_send, f_recv, (a, b)).wait()

    with jax.named_scope("wait_f"):

        @pl.when(edge)
        def _():
            settle_far(n_gx - 2)

        @pl.when(inner)
        def _():
            settle_far(n_gx - 3)

    with jax.named_scope("final"):
        origin = lax.broadcasted_iota(jnp.int32, (n_gx, modes), 0)
        before = jnp.zeros((n_gx, modes), jnp.float32)
        after = before
        for j in range(n_gy):
            sent = jnp.concatenate([far_ref[j, g] for g in range(modes // 128)], axis=1)
            before = before + jnp.where(origin <= a - 2, sent, 0.0)
            after = after + jnp.where(origin >= a + 2, sent, 0.0)
        before = jnp.sum(before * mine[256 : 256 + n_gx], axis=0, keepdims=True)
        after = jnp.sum(after * mine[256 + n_gx : 256 + 2 * n_gx], axis=0, keepdims=True)
        lifted = lifted + mine[32:96] * before + mine[96:160] * after
        lifted = halves(jnp.concatenate([lifted[:n], lifted[n:]], axis=1))
        inverse = jnp.concatenate(
            [vmem["recip"][fine + c * n : fine + (c + 1) * n] for c in range(4)], axis=1
        )
        spectrum = (spectrum + right_mul(*lifted, "drop")) * inverse
        high, low = halves(left_mul("sn", *halves(spectrum)))
        parts = []
        for c in range(4):
            at = slice(c * 256, (c + 1) * 256)
            parts.append(right_mul(high[:, at], low[:, at], "far%d" % c))
    with jax.named_scope("unfold"):
        sides = [
            jnp.concatenate([part[:, s * 128 : (s + 1) * 128] for part in parts], axis=1)
            for s in range(2)
        ]
        high, low = halves(jnp.concatenate(sides, axis=0))
        stacked = jnp.concatenate([high, low], axis=0)
        both = mm(stacked, table("unfold", 0))
        both = both[: 2 * n] + both[2 * n :]
        for s, group in enumerate(groups):
            for i, v in enumerate(group):
                out_ref[:, v * 128 : (v + 1) * 128] = both[
                    s * n : (s + 1) * n, i * 128 : (i + 1) * 128
                ]


def emit(in_ref, out_ref, sem):
    copy = pltpu.make_async_copy(in_ref, out_ref, sem)
    copy.start()
    copy.wait()


def body(n_gx, n_gy, charge):
    singles, places = tables(n_gx, n_gy)
    arrays = [charge] + [jnp.asarray(singles[name]) for name in NAMES[1:]]
    scratch = [
        pltpu.VMEM(window(name, array.shape), array.dtype) for name, array in zip(NAMES, arrays)
    ]
    modes = n_gy * (P_SIZE // Q) ** 2
    half = P_SIZE + 2 * W
    scratch += [
        pltpu.VMEM((2, P_SIZE, 1024), jnp.bfloat16),
        pltpu.VMEM((2, 4 * half, 256), jnp.bfloat16),
        pltpu.VMEM((2, 8 * half, 256), jnp.bfloat16),
        pltpu.VMEM((2, 16 * half, 256), jnp.bfloat16),
        pltpu.VMEM((2, 4 * half, 512), jnp.bfloat16),
        pltpu.VMEM((modes // 128, 8, 128), jnp.float32),
        pltpu.VMEM((n_gy, modes // 128, n_gx, 128), jnp.float32),
        pltpu.VMEM((3 * n_gy, 16, modes), jnp.float32),
        pltpu.VMEM((8, 256), jnp.float32),
        pltpu.VMEM((16, 128), jnp.float32),
        pltpu.VMEM((8, 256), jnp.float32),
        pltpu.VMEM((2, 16, 128), jnp.float32),
        pltpu.VMEM((16 * (modes // 128) * (3 * n_gy - 1) + 40, 128), jnp.float32),
        pltpu.SemaphoreType.DMA((len(NAMES),)),
        pltpu.SemaphoreType.DMA,
        pltpu.SemaphoreType.DMA,
        pltpu.SemaphoreType.DMA,
        pltpu.SemaphoreType.DMA,
    ]
    hbm = pl.BlockSpec(memory_space=pl.ANY)
    vm = pl.BlockSpec(memory_space=pltpu.VMEM)
    solved = pl.pallas_call(
        functools.partial(kernel, places, n_gx, n_gy),
        out_shape=pltpu.VMEM(charge.shape, charge.dtype),
        in_specs=[hbm] * len(NAMES),
        out_specs=vm,
        scratch_shapes=scratch,
        name="mlc",
        compiler_params=pltpu.CompilerParams(
            collective_id=0, has_side_effects=True, vmem_limit_bytes=60 * 1024 * 1024
        ),
    )(*arrays)
    return pl.pallas_call(
        emit,
        out_shape=jax.ShapeDtypeStruct(charge.shape, charge.dtype),
        in_specs=[vm],
        out_specs=hbm,
        scratch_shapes=[pltpu.SemaphoreType.DMA],
        name="emit",
        compiler_params=pltpu.CompilerParams(vmem_limit_bytes=1024 * 1024),
    )(solved)


def solution(mesh):
    run = functools.partial(body, mesh.shape["gx"], mesh.shape["gy"])
    spec = P("gx", "gy")
    return jax.shard_map(run, mesh=mesh, in_specs=(spec,), out_specs=spec, check_vma=False)
```

```python
import functools

import jax
import jax.numpy as jnp
import ml_dtypes
import numpy as np
from jax import lax
from jax.experimental import pallas as pl
from jax.experimental.pallas import tpu as pltpu
from jax.sharding import PartitionSpec as P

P_SIZE = 32
W = 16
Q = 4
NL = 16
CLASSES = [(0, 0), (0, 1), (1, 0), (1, 1)]
MESH = pl.DeviceIdType.MESH


def sine_table(length):
    counter = np.arange(length) + 1
    return np.sin(np.pi * np.outer(counter, counter) / (length + 1))


def eigen_values(length):
    return 2.0 - 2.0 * np.cos(np.pi * (np.arange(length) + 1) / (length + 1))


def interp_table(fine_start, fine_count, coarse_start, coarse_count, ratio):
    fine_pos = np.arange(fine_count) + fine_start
    coarse_pos = np.arange(coarse_count) + coarse_start
    numerator = 2 * fine_pos - (ratio - 1)
    lower = numerator // (2 * ratio)
    weight = ((numerator - 2 * ratio * lower) / (2 * ratio))[:, None]
    below = coarse_pos[None, :] == lower[:, None]
    above = coarse_pos[None, :] == lower[:, None] + 1
    return below * (1.0 - weight) + above * weight


def legendre_basis(length, count):
    points = (2.0 * np.arange(length) + 1.0) / length - 1.0
    columns = [np.ones_like(points), points]
    for degree in range(2, count):
        columns.append(
            ((2 * degree - 1) * points * columns[-1] - (degree - 1) * columns[-2]) / degree
        )
    result = []
    for vector in columns[:count]:
        for passes in range(2):
            for earlier in result:
                vector = vector - np.sum(earlier * vector) * earlier
        result.append(vector / np.sqrt(np.sum(vector * vector)))
    return np.stack(result, axis=1)


def fold(length):
    half = length // 2
    eye = np.eye(length)
    return np.concatenate([eye[:half] + eye[::-1][:half], eye[:half] - eye[::-1][:half]])


def split(table):
    high = table.astype(ml_dtypes.bfloat16)
    low = (table - high.astype(np.float64)).astype(ml_dtypes.bfloat16)
    return high, low


@functools.lru_cache(maxsize=None)
def tables(n_gx, n_gy):
    n, length, cells = P_SIZE, P_SIZE + 2 * W, P_SIZE // Q
    blocks, margin = length // Q, W // Q
    half, hl, hb, hn = n // 2, length // 2, blocks // 2, NL // 2
    quad, wide = hb * hb, hn * hn
    nx, ny, nz = n_gx * cells, n_gy * cells, cells
    modes = ny * nz
    s_l, s_n = sine_table(length), sine_table(n)
    u_n, u_b = fold(n), fold(blocks)
    basis = legendre_basis(n, NL)
    average = np.kron(np.eye(blocks), np.full((1, Q), 1.0 / Q))
    fine = interp_table(0, length, 0, blocks, Q)
    middle = fine[W : W + n]
    picks = [W - 1, W, W + n - 1, W + n]
    a_full = average @ s_l
    b_full = basis.T @ s_l[W : W + n]
    order = np.arange(4 * NL).reshape(4, hn, 2).transpose(2, 0, 1).ravel()
    big = {}

    folding = np.zeros((2, 4, n, 2, 2, 4, half))
    for p, q in CLASSES:
        for y4 in range(4):
            piece = u_n[q * half : (q + 1) * half].T
            folding[0, y4, :, p, q, y4, :] = piece
            folding[1, y4, :, p, q, 3 - y4, :] = piece if p == 0 else -piece
    plain = {"fold": folding.reshape(256, 256)}
    folding = np.zeros((4, 4, n, 4, 2 * 4, half))
    for c, (p, q) in enumerate(CLASSES):
        for vi in range(4):
            for y4 in range(4):
                il = [y4, 4 + y4, 3 - y4, 7 - y4][vi]
                sign = -1.0 if vi > 1 and p == 1 else 1.0
                folding[vi, y4, :, c, il, :] = sign * u_n[q * half : (q + 1) * half].T
    folding = folding.reshape(4 * 128, 4 * 128)
    plain["unfold"] = folding.T

    inner = s_l[:, W : W + n] @ u_n.T / 2
    f1 = [inner[p::2, p * half : (p + 1) * half] for p in (0, 1)]
    a1 = [(u_b @ a_full)[p * hb : (p + 1) * hb, p::2] for p in (0, 1)]
    b1 = [b_full[p::2, p::2] for p in (0, 1)]
    keep, pick = np.eye(hb), np.concatenate([np.zeros((hn, hb)), np.eye(hn)], axis=1)
    keep = np.concatenate([keep, np.zeros((hb, hn))], axis=1)
    for p in (0, 1):
        big["fy%d" % p] = np.kron(f1[p].T, np.eye(half))
        high, low = split(np.kron(np.eye(8), f1[p].T))
        plain["fz%d" % p] = np.concatenate([high, high])
        plain["gz%d" % p] = low
        plain["bz%d" % p] = np.concatenate(
            split(np.kron(np.eye(8), np.concatenate([a1[p], b1[p]]).T)), axis=1
        )
        sample = np.kron(a1[p], keep).T
        slab = np.kron(s_l[picks][:, p::2], pick).T
        plain["by%d" % p] = np.concatenate(split(np.concatenate([sample, sample], axis=1)), axis=1)
        plain["cy%d" % p] = np.concatenate(
            split(np.concatenate([slab, slab, np.kron(b1[p], pick).T], axis=1)), axis=1
        )

    unfold = u_b.T / 2
    pair = np.kron(unfold, unfold).reshape(blocks * blocks, 2, hb, 2, hb)

    def from_samples(table):
        folded = np.einsum("os,spaqb->pqabo", table, pair)
        return folded.reshape(4 * quad, table.shape[0])

    bm = basis.T @ middle
    lin_x = from_samples(np.kron(bm, bm)).reshape(4 * quad, NL, NL)
    lin = np.zeros((4 * quad, 384))
    for c, (p, q) in enumerate(CLASSES):
        lin[:, c * wide : (c + 1) * wide] = lin_x[:, p::2, q::2].reshape(4 * quad, wide)
    lin[:, 256:320] = from_samples(np.kron(fine[picks], bm))[:, order]
    big["lin"] = lin
    k1 = [(s_n @ u_n.T / 2)[p::2, p * half : (p + 1) * half] for p in (0, 1)]
    for c, (p, q) in enumerate(CLASSES):
        big["near%d" % c] = np.kron(k1[p], k1[q]).T
    r1 = [(u_n @ s_n / 2)[p * half : (p + 1) * half, p::2] for p in (0, 1)]
    for c, (p, q) in enumerate(CLASSES):
        big["far%d" % c] = np.kron(r1[p], r1[q]).T

    second = 2 * np.eye(blocks) - np.eye(blocks, k=1) - np.eye(blocks, k=-1)
    s_y, s_z = sine_table(ny), sine_table(nz)
    proj_z = np.zeros((nz, blocks))
    proj_z[:, margin : margin + cells] = s_z
    edge = interp_table(-1, n + 2, -1, cells + 2, Q)
    depth = interp_table(0, n, 0, cells, Q)
    lateral = edge[1 : n + 1]
    s_ext = np.zeros((ny + 2, ny))
    s_ext[1:-1] = s_y
    sp = np.concatenate([s_n[0::2], s_n[1::2]])
    deep = sp @ depth @ s_z

    def by_class(first, second_table):
        parts = []
        for p, q in CLASSES:
            parts.append(
                np.kron(first[p * half : (p + 1) * half], second_table[q * half : (q + 1) * half])
            )
        return np.concatenate(parts).T

    factor = (2.0 / (ny + 1)) * (2.0 / (nz + 1))
    spread, drop = [], []
    for b in range(n_gy):
        proj_y = np.zeros((ny, blocks))
        for j in range(blocks):
            at = j + b * cells - margin
            if 0 <= at < ny:
                proj_y[:, j] = s_y[:, at]
        flat = np.kron(proj_y, proj_z)
        curved = np.kron(proj_y @ second, proj_z) + np.kron(proj_y, proj_z @ second)
        spread.append(
            factor * np.concatenate([from_samples(curved), from_samples(flat)], axis=1)
        )
        local_s = s_ext[b * cells : b * cells + cells + 2]
        rim = np.outer(sp[:, 0], edge[0] @ local_s) + np.outer(sp[:, n - 1], edge[n + 1] @ local_s)
        drop.append(
            np.concatenate([by_class(sp @ lateral @ local_s, deep), by_class(rim, deep)])
        )
    big["spread"] = np.stack(spread)
    big["drop"] = np.stack(drop)
    sb = s_n @ basis
    sbp = np.concatenate([sb[0::2], sb[1::2]])
    facex = np.zeros((4 * wide, n * n))
    for c, (p, q) in enumerate(CLASSES):
        facex[c * wide : (c + 1) * wide, c * 256 : c * 256 + 256] = np.kron(
            sb[p::2, p::2], sb[q::2, q::2]
        ).T
    big["facex"] = facex
    ends = np.stack([sp[:, 0], sp[:, n - 1], sp[:, 0], sp[:, n - 1]], axis=1)
    big["facey"] = by_class(ends, sbp)[order]

    mu_y, mu_z = eigen_values(ny), eigen_values(nz)
    theta = np.arccosh(1.0 + (mu_y[:, None] + mu_z[None, :]).reshape(1, modes) / 2)
    below = 2 * np.sinh(theta) * (1.0 - np.exp(-2 * theta * (nx + 1)))
    apart = np.abs(np.arange(48) - 20)[:, None]
    toep = (np.exp(-theta * apart) + np.exp(-theta * np.maximum(2 * (nx + 1) - apart, 0))) / below
    total = (np.arange(2 * nx + 32) - 13)[:, None]
    hank = np.exp(-theta * np.maximum(total + 2, 0)) + np.exp(-theta * np.maximum(2 * nx - total, 0))
    hank = hank / below

    u12 = np.zeros((64, 16))
    u12[:32, :10] = np.outer(s_n[:, 0], edge[0]) + np.outer(s_n[:, n - 1], edge[n + 1])
    u12[32:, :10] = s_n @ lateral
    place = np.arange(n_gx)
    mine = []
    for a in range(n_gx):
        rank = np.arange(16)[:, None]
        at = cells * a - margin + rank
        inside = (at >= 0) & (at < nx)
        rightward = inside * np.exp(-theta * (15 - rank)) * (1 - np.exp(-2 * theta * (at + 1) * inside))
        leftward = inside * np.exp(-theta * rank) * (1 - np.exp(-2 * theta * (nx - at) * inside))
        row = np.arange(16)[:, None]
        x = cells * a - 1 + row
        used = row < cells + 2
        falling = used * np.exp(-theta * row) * (1 - np.exp(-2 * theta * np.maximum(nx - x, 0))) / below
        rising = (
            used
            * np.exp(-theta * np.maximum(cells + 1 - row, 0))
            * (1 - np.exp(-2 * theta * (x + 1)))
            / below
        )
        away = (a - place)[:, None]
        before = (away >= 2) * np.exp(-theta * np.maximum(cells * away - 12, 0))
        after = (away <= -2) * np.exp(-theta * np.maximum(-cells * away - 12, 0))
        mine.append(
            np.concatenate(
                [
                    rightward,
                    leftward,
                    u12 @ falling,
                    u12 @ rising,
                    toep,
                    hank[2 * cells * a : 2 * cells * a + 48],
                    before,
                    after,
                ]
            )
        )
    mu_l, mu_n = eigen_values(length), eigen_values(n)
    reciprocal = []
    for q in (0, 1):
        for p in (0, 1):
            pair_sum = (mu_l[p::2][:, None] + mu_l[q::2][None, :]).reshape(1, hl * hl)
            table = 1.0 / (mu_l[:, None] + pair_sum)
            reciprocal.append(table.reshape(length, 4, 256).transpose(1, 0, 2).reshape(-1, 256))
    for p, q in CLASSES:
        pair_sum = (mu_n[p::2][:, None] + mu_n[q::2][None, :]).reshape(1, 256)
        reciprocal.append((2.0 / (n + 1)) ** 3 / (mu_n[:, None] + pair_sum))
    ends = np.zeros((n, 256))
    ends[:, :2] = s_n[:, [0, n - 1]]
    reciprocal.append(ends)

    scale = (2.0 / (length + 1)) ** 3
    blank = np.zeros((12, length))
    lefts = {
        "sl": s_l[:, W : W + n],
        "means": a_full * scale,
        "flat": np.concatenate([fine[picks], blank[:, :blocks], bm]),
        "picks": np.concatenate([s_l[picks], blank, b_full]) * scale,
        "sn": s_n,
        "u12": u12,
        "sb": sb,
    }
    for name, value in lefts.items():
        high, low = split(value)
        plain[name] = np.concatenate([high, high, low], axis=1)
    singles = {
        "mine": np.stack(mine).astype(np.float32),
        "recip": np.concatenate(reciprocal).astype(np.float32),
    }
    places = {}
    for group, names in GROUPS.items():
        packs, row = [], 0
        for name in names:
            if name in plain:
                parts = [plain[name].astype(ml_dtypes.bfloat16)]
            else:
                parts = split(big[name])
            depth, width = parts[0].shape[-2:]
            place = {"left": (row, depth, width)}
            step = 256
            tiles = []
            for part in parts:
                for at in range(0, width, step):
                    tile = np.zeros(part.shape[:-1] + (256,), ml_dtypes.bfloat16)
                    piece = part[..., at : at + step]
                    tile[..., : piece.shape[-1]] = piece
                    packs.append(tile)
                    tiles.append((row, depth))
                    row += depth
            count = len(tiles) // len(parts)
            place["tiles"] = [tiles[k * count : (k + 1) * count] for k in range(len(parts))]
            places[name] = (group, place)
        most = max(tile.ndim for tile in packs)
        if most == 3:
            packs = [np.broadcast_to(tile, (n_gy,) + tile.shape[-2:]) for tile in packs]
        singles[group] = np.concatenate(packs, axis=-2)
    return singles, places


GROUPS = {
    "first": ["fold", "sl"],
    "upy": ["fy0", "fy1"],
    "upz": ["fz0", "gz0", "fz1", "gz1", "means", "bz0", "bz1"],
    "downy": ["by0", "by1"],
    "spread": ["spread"],
    "side": ["picks", "flat", "sn", "sb", "u12", "lin", "cy0", "cy1"]
    + ["near%d" % c for c in range(4)]
    + ["facex", "facey"],
    "drop": ["drop"],
    "last": ["far%d" % c for c in range(4)] + ["unfold"],
}
NAMES = ["charge", "first", "upy", "upz", "recip", "downy", "spread", "mine", "side", "drop", "last"]


def halves(value):
    high = value.astype(jnp.bfloat16)
    return high, (value - high.astype(jnp.float32)).astype(jnp.bfloat16)


def mm(left, right):
    return jnp.dot(left, right, preferred_element_type=jnp.float32)


def window(name, shape):
    return shape[1:] if name in ("spread", "drop", "mine") else shape


def kernel(places, n_gx, n_gy, *refs):
    count = len(NAMES)
    hbm = dict(zip(NAMES, refs[:count]))
    out_ref = refs[count]
    vmem = dict(zip(NAMES, refs[count + 1 : 2 * count + 1]))
    (
        fold_ref, w_ref, z_ref, x_ref, s_ref, b_ref, y_ref, c_ref, d_ref,
        mom_ref, far_ref, near_ref, cx_ref, cy_ref, rx_ref, ry_ref, tally_ref,
        load_sem, f_send, f_recv, p_send, p_recv,
    ) = refs[2 * count + 1 :]
    ndev = n_gx * n_gy
    a = lax.axis_index("gx")
    b = lax.axis_index("gy")
    me = a * n_gy + b
    n, cells = P_SIZE, P_SIZE // Q
    half = n + 2 * W
    modes = near_ref.shape[-1]

    loads = {}
    slabs = []
    for i in range(4):
        rows = pl.ds(i * (n // 4), n // 4)
        slabs.append(
            pltpu.make_async_copy(
                hbm["charge"].at[rows], vmem["charge"].at[rows], load_sem.at[len(NAMES) + i - 1]
            )
        )
        slabs[-1].start()
    for i, name in enumerate(NAMES[1:]):
        source = hbm[name]
        if name in ("spread", "drop"):
            source = source.at[b]
        if name == "mine":
            source = source.at[a]
        loads[name] = pltpu.make_async_copy(source, vmem[name], load_sem.at[i])
        loads[name].start()

    barrier = pltpu.get_barrier_semaphore()

    def greet(r, carry):
        peer = lax.rem(me + r, ndev)
        pl.semaphore_signal(
            barrier, inc=1, device_id=(peer // n_gy, lax.rem(peer, n_gy)), device_id_type=MESH
        )
        return carry

    with jax.named_scope("greet"):
        lax.fori_loop(1, ndev, greet, 0)

    def tile(name, part, i):
        group, place = places[name]
        row, depth = place["tiles"][part][i]
        return vmem[group][row : row + depth, :]

    def table(name, part):
        count = len(places[name][1]["tiles"][part])
        return jnp.concatenate([tile(name, part, i) for i in range(count)], axis=1)

    def right_mul(high, low, name):
        rows = high.shape[0]
        both = mm(jnp.concatenate([high, low], axis=0), table(name, 0))
        return both[:rows] + both[rows:] + mm(high, table(name, 1))

    def left_mul(name, high, low):
        group, place = places[name]
        row, rows, cols = place["left"]
        return mm(vmem[group][row : row + rows, 0:cols], jnp.concatenate([high, low, high], axis=0))

    groups = [[0, 1, 7, 6], [2, 3, 5, 4]]
    with jax.named_scope("w_charge"):
        for slab in slabs:
            slab.wait()
    with jax.named_scope("w_first"):
        loads["first"].wait()
    with jax.named_scope("fold"):
        charge = vmem["charge"]
        pairs = [
            jnp.concatenate([charge[:, v * 128 : (v + 1) * 128] for v in (u, 7 - u)], axis=1)
            for u in range(4)
        ]
        high, low = halves(jnp.concatenate(pairs, axis=0))
        both = mm(jnp.concatenate([high, low], axis=0), tile("fold", 0, 0))
        both = both[: 4 * n] + both[4 * n :]
        lane = lax.broadcasted_iota(jnp.int32, (half, 128), 1)
        folded = []
        for p in range(2):
            rows = [both[v * n : (v + 1) * n, p * 128 : (p + 1) * 128] for v in range(4)]
            turn = [pltpu.roll(row, 64, 1) for row in rows]
            left = lane[:n] < 64
            folded += [jnp.where(left, rows[v], turn[v + 1]) for v in (0, 2)]
            folded += [jnp.where(left, turn[v], rows[v + 1]) for v in (0, 2)]
        folded = halves(jnp.concatenate(folded, axis=1))
        fold_ref[0] = folded[0]
        fold_ref[1] = folded[1]
        for c in range(4):
            at = slice(c * 256, (c + 1) * 256)
            q = c % 2
            w_ref[c // 2, q * n : (q + 1) * n] = folded[0][:, at]
            w_ref[c // 2, (2 + q) * n : (3 + q) * n] = folded[1][:, at]
    with jax.named_scope("w_upy"):
        loads["upy"].wait()
    with jax.named_scope("upy"):
        for p in range(2):
            name = "fy%d" % p
            both = mm(w_ref[p], table(name, 0))
            lift = both[: 2 * n] + both[2 * n :] + mm(w_ref[p, 0 : 2 * n], table(name, 1))
            high, low = halves(lift)
            for q in range(2):
                for k in range(4):
                    at = (4 * p + k) * n
                    rows, lanes = slice(q * n, (q + 1) * n), slice(k * 128, (k + 1) * 128)
                    z_ref[q, at : at + n, 0:128] = high[rows, lanes]
                    z_ref[q, at : at + n, 128:256] = low[rows, lanes]
    with jax.named_scope("w_upz"):
        loads["upz"].wait()
    with jax.named_scope("upz"):
        for q in range(2):
            up = mm(z_ref[q], tile("fz%d" % q, 0, 0)) + mm(z_ref[q, :, 0:128], tile("gz%d" % q, 0, 0))
            high, low = halves(up)
            for k in range(8):
                rows, lanes = slice(k * n, (k + 1) * n), slice((8 * q + k) * 256, (8 * q + k + 1) * 256)
                x_ref[0:n, lanes] = high[rows]
                x_ref[n : 2 * n, lanes] = low[rows]
    with jax.named_scope("w_recip"):
        loads["recip"].wait()
    with jax.named_scope("upx"):
        group, place = places["sl"]
        row, rows, cols = place["left"]
        weights = vmem[group][row : row + rows, 0:cols]
        for q in range(2):
            lanes = slice(q * 2048, (q + 1) * 2048)
            spectrum = mm(
                weights, jnp.concatenate([x_ref[:, lanes], x_ref[0:n, lanes]], axis=0)
            )
            divisor = [
                vmem["recip"][(8 * q + k) * half : (8 * q + k + 1) * half] for k in range(8)
            ]
            high, low = halves(spectrum * jnp.concatenate(divisor, axis=1))
            s_ref[0:half, lanes] = high
            s_ref[half : 2 * half, lanes] = low

    def down(name, rows, b_ref, y_ref, finish):
        group, place = places[name]
        row, _, cols = place["left"]
        weights = vmem[group][row : row + rows, 0:cols]
        for q in range(2):
            lanes = slice(q * 2048, (q + 1) * 2048)
            short = mm(weights, jnp.concatenate([s_ref[:, lanes], s_ref[0:half, lanes]], axis=0))
            high, low = halves(short)
            for k in range(8):
                lanes = slice(k * 256, (k + 1) * 256)
                b_ref[q, k * rows : (k + 1) * rows] = high[:, lanes]
                b_ref[q, (8 + k) * rows : (9 + k) * rows] = low[:, lanes]
        for q in range(2):
            both = mm(b_ref[q], tile("bz%d" % q, 0, 0))
            block = 8 * rows
            high, low = halves(both[:block, :128] + both[block:, :128] + both[:block, 128:])
            for p in range(2):
                for k in range(4):
                    at, lanes = (4 * p + k) * rows, slice(k * 128, (k + 1) * 128)
                    y_ref[p, q * rows : (q + 1) * rows, lanes] = high[at : at + rows]
                    y_ref[p, (2 + q) * rows : (3 + q) * rows, lanes] = low[at : at + rows]
        ys = []
        finish()
        for p in range(2):
            both = mm(y_ref[p], tile("%sy%d" % ("b" if name == "means" else "c", p), 0, 0))
            both = both[: 2 * rows, :128] + both[2 * rows :, :128] + both[: 2 * rows, 128:]
            ys += [both[:rows], both[rows:]]
        return ys

    def arrive():
        loads["downy"].wait()
        loads["spread"].wait()
        loads["mine"].wait()

    with jax.named_scope("down"):
        y0, y1, y2, y3 = down("means", 16, b_ref, y_ref, arrive)
    with jax.named_scope("spread"):
        sample = jnp.concatenate(
            [jnp.where(lane[0:16] < 64, u, v) for u, v in ((y0, y1), (y2, y3))], axis=1
        )
        sample = halves(sample)
        spread = right_mul(*sample, "spread")
        bend = spread[:, modes:]
        gap = jnp.zeros((1, modes), jnp.float32)
        packet = spread[:, :modes] + 2.0 * bend
        packet = packet - jnp.concatenate([gap, bend[:-1]]) - jnp.concatenate([bend[1:], gap])
        mine = vmem["mine"]
        near_ref[n_gy + b] = packet
        rightward = jnp.sum(packet * mine[0:16], axis=0, keepdims=True)
        leftward = jnp.sum(packet * mine[16:32], axis=0, keepdims=True)
        for g in range(modes // 128):
            mom_ref[g, 0:1] = rightward[:, g * 128 : (g + 1) * 128]
            mom_ref[g, 1:2] = leftward[:, g * 128 : (g + 1) * 128]

    with jax.named_scope("barrier"):
        pl.semaphore_wait(barrier, ndev - 1)

    def remote(source, target, send, recv, device):
        return pltpu.make_async_remote_copy(
            src_ref=source,
            dst_ref=target,
            send_sem=send,
            recv_sem=recv,
            device_id=device,
            device_id_type=MESH,
        )

    def start_far(r, carry):
        d = n_gx - r
        for j in range(n_gy):
            for row, other, fine in ((0, a + d, a + d < n_gx), (1, a - d, a >= d)):

                @pl.when(fine)
                def _():
                    remote(
                        mom_ref.at[:, pl.ds(row, 1)],
                        far_ref.at[b, :, pl.ds(a, 1)],
                        f_send,
                        f_recv,
                        (other, j),
                    ).start()

        return carry

    with jax.named_scope("send"):
        lax.fori_loop(1, n_gx - 1, start_far, 0)
        for step in (0, 1, 2):
            for j in range(n_gy):
                other = a + step - 1
                fine = (other >= 0) & (other < n_gx)
                if step == 1:
                    fine = b != j

                @pl.when(fine)
                def _():
                    remote(
                        near_ref.at[n_gy + b],
                        near_ref.at[(2 - step) * n_gy + b],
                        p_send,
                        p_recv,
                        (other, j),
                    ).start()

    with jax.named_scope("w_side"):
        loads["side"].wait()
    with jax.named_scope("lin"):
        y0, y1, y2, y3 = down("picks", 32, c_ref, d_ref, lambda: None)
        flat = right_mul(*halves(left_mul("flat", *sample)), "lin")
        cx = jnp.concatenate(
            [
                jnp.where(lane[0:8] < 64, pltpu.roll(u[0:8], 64, 1), v[0:8])
                for u, v in ((y0, y1), (y2, y3))
            ],
            axis=1,
        )
        cx = cx - flat[0:8, 0:256]
        cy = jnp.where(lane[0:16] < 32, y0[16:] + y2[16:], y1[16:] + y3[16:])
        cy = cy - flat[16:32, 256:384]
        cx_ref[...] = cx
        cy_ref[...] = cy

    upper, lower = lax.rem(b + 1, n_gy), lax.rem(b + n_gy - 1, n_gy)
    with jax.named_scope("sendc"):

        @pl.when(a < n_gx - 1)
        def _():
            remote(
                cx_ref.at[pl.ds(2, 1)], rx_ref.at[pl.ds(0, 1)], p_send, p_recv, (a + 1, b)
            ).start()

        @pl.when(a > 0)
        def _():
            remote(
                cx_ref.at[pl.ds(1, 1)], rx_ref.at[pl.ds(1, 1)], p_send, p_recv, (a - 1, b)
            ).start()

        remote(cy_ref, ry_ref.at[0], p_send, p_recv, (a, upper)).start()
        remote(cy_ref, ry_ref.at[1], p_send, p_recv, (a, lower)).start()

    with jax.named_scope("near"):
        narrow = halves(left_mul("sn", fold_ref[0], fold_ref[1]))
        spectrum = []
        for c in range(4):
            at = slice(c * 256, (c + 1) * 256)
            spectrum.append(right_mul(narrow[0][:, at], narrow[1][:, at], "near%d" % c))
        spectrum = jnp.concatenate(spectrum, axis=1)

    edge = (a == 0) | (a == n_gx - 1)
    inner = jnp.logical_not(edge)

    def settle_near(sides):
        lines = 16 * (modes // 128) * ((1 + sides) * n_gy - 1) + 2 * sides + 32
        block = tally_ref.at[pl.ds(0, lines)]
        remote(block, block, p_send, p_recv, (a, b)).wait()

    with jax.named_scope("wait_p"):

        @pl.when(edge)
        def _():
            settle_near(1)

        @pl.when(inner)
        def _():
            settle_near(2)

    with jax.named_scope("face"):
        from_left = jnp.where(a > 0, rx_ref[0:1], 0.0)
        from_right = jnp.where(a < n_gx - 1, rx_ref[1:2], 0.0)
        ends = jnp.concatenate(
            [cx[0:1] + from_left, cx[3:4] + from_right, jnp.zeros((14, cx.shape[1]), jnp.float32)]
        )
        ends = right_mul(*halves(ends), "facex")
        fine = 16 * half
        column = vmem["recip"][fine + 4 * n : fine + 5 * n, 0:2]
        spectrum = spectrum + column[:, 0:1] * ends[0:1] + column[:, 1:2] * ends[1:2]
        group = jnp.where(lane[0:16] < 64, lax.rem(lane[0:16], 32) // 8, 4)
        total = jnp.where((group == 0) | (group == 3), cy, 0.0)
        total = total + jnp.where((group == 2) & (b > 0), ry_ref[0], 0.0)
        total = total + jnp.where((group == 1) & (b < n_gy - 1), ry_ref[1], 0.0)
        total = left_mul("sb", *halves(total))[:, 0:64]
        spectrum = spectrum + right_mul(*halves(total), "facey")
    with jax.named_scope("green"):
        row = lax.broadcasted_iota(jnp.int32, (8, modes), 0)

        def gathered(step):
            value = near_ref[step * n_gy]
            for j in range(1, n_gy):
                value = value + near_ref[step * n_gy + j]
            return value

        past = jnp.where(a > 0, gathered(0), 0.0)
        here = gathered(1)
        next_ = jnp.where(a < n_gx - 1, gathered(2), 0.0)
        source = jnp.concatenate(
            [
                jnp.where((row >= 4) | (a > 1), past[0:8], 0.0),
                past[8:16] + jnp.where((row >= 4) | (a > 0), here[0:8], 0.0),
                jnp.where((row < 4) | (a < n_gx - 1), here[8:16] + next_[0:8], 0.0),
                jnp.where((row < 4) | (a < n_gx - 2), next_[8:16], 0.0),
            ]
        )
        values = []
        for i in range(cells + 2):
            influence = mine[169 - i : 201 - i] - mine[208 + i : 240 + i]
            values.append(jnp.sum(influence * source, axis=0, keepdims=True))
        values.append(jnp.zeros((16 - len(values), modes), jnp.float32))
        lifted = left_mul("u12", *halves(jnp.concatenate(values, axis=0)))

    with jax.named_scope("w_last"):
        loads["drop"].wait()
        loads["last"].wait()

    def settle_far(each):
        block = far_ref.at[:, :, pl.ds(0, each)]
        remote(block, block, f_send, f_recv, (a, b)).wait()

    with jax.named_scope("wait_f"):

        @pl.when(edge)
        def _():
            settle_far(n_gx - 2)

        @pl.when(inner)
        def _():
            settle_far(n_gx - 3)

    with jax.named_scope("final"):
        origin = lax.broadcasted_iota(jnp.int32, (n_gx, modes), 0)
        before = jnp.zeros((n_gx, modes), jnp.float32)
        after = before
        for j in range(n_gy):
            sent = jnp.concatenate([far_ref[j, g] for g in range(modes // 128)], axis=1)
            before = before + jnp.where(origin <= a - 2, sent, 0.0)
            after = after + jnp.where(origin >= a + 2, sent, 0.0)
        before = jnp.sum(before * mine[256 : 256 + n_gx], axis=0, keepdims=True)
        after = jnp.sum(after * mine[256 + n_gx : 256 + 2 * n_gx], axis=0, keepdims=True)
        lifted = lifted + mine[32:96] * before + mine[96:160] * after
        lifted = halves(jnp.concatenate([lifted[:n], lifted[n:]], axis=1))
        inverse = jnp.concatenate(
            [vmem["recip"][fine + c * n : fine + (c + 1) * n] for c in range(4)], axis=1
        )
        spectrum = (spectrum + right_mul(*lifted, "drop")) * inverse
        high, low = halves(left_mul("sn", *halves(spectrum)))
        parts = []
        for c in range(4):
            at = slice(c * 256, (c + 1) * 256)
            parts.append(right_mul(high[:, at], low[:, at], "far%d" % c))
    with jax.named_scope("unfold"):
        sides = [
            jnp.concatenate([part[:, s * 128 : (s + 1) * 128] for part in parts], axis=1)
            for s in range(2)
        ]
        high, low = halves(jnp.concatenate(sides, axis=0))
        stacked = jnp.concatenate([high, low], axis=0)
        both = mm(stacked, table("unfold", 0))
        both = both[: 2 * n] + both[2 * n :]
        for s, group in enumerate(groups):
            for i, v in enumerate(group):
                out_ref[:, v * 128 : (v + 1) * 128] = both[
                    s * n : (s + 1) * n, i * 128 : (i + 1) * 128
                ]


def emit(in_ref, out_ref, sem):
    copy = pltpu.make_async_copy(in_ref, out_ref, sem)
    copy.start()
    copy.wait()


def body(n_gx, n_gy, charge):
    singles, places = tables(n_gx, n_gy)
    arrays = [charge] + [jnp.asarray(singles[name]) for name in NAMES[1:]]
    scratch = [
        pltpu.VMEM(window(name, array.shape), array.dtype) for name, array in zip(NAMES, arrays)
    ]
    modes = n_gy * (P_SIZE // Q) ** 2
    half = P_SIZE + 2 * W
    scratch += [
        pltpu.VMEM((2, P_SIZE, 1024), jnp.bfloat16),
        pltpu.VMEM((2, 4 * P_SIZE, 256), jnp.bfloat16),
        pltpu.VMEM((2, 8 * P_SIZE, 256), jnp.bfloat16),
        pltpu.VMEM((2 * P_SIZE, 4096), jnp.bfloat16),
        pltpu.VMEM((2 * half, 4096), jnp.bfloat16),
        pltpu.VMEM((2, 256, 256), jnp.bfloat16),
        pltpu.VMEM((2, 64, 512), jnp.bfloat16),
        pltpu.VMEM((2, 512, 256), jnp.bfloat16),
        pltpu.VMEM((2, 128, 512), jnp.bfloat16),
        pltpu.VMEM((modes // 128, 8, 128), jnp.float32),
        pltpu.VMEM((n_gy, modes // 128, n_gx, 128), jnp.float32),
        pltpu.VMEM((3 * n_gy, 16, modes), jnp.float32),
        pltpu.VMEM((8, 256), jnp.float32),
        pltpu.VMEM((16, 128), jnp.float32),
        pltpu.VMEM((8, 256), jnp.float32),
        pltpu.VMEM((2, 16, 128), jnp.float32),
        pltpu.VMEM((16 * (modes // 128) * (3 * n_gy - 1) + 40, 128), jnp.float32),
        pltpu.SemaphoreType.DMA((len(NAMES) + 3,)),
        pltpu.SemaphoreType.DMA,
        pltpu.SemaphoreType.DMA,
        pltpu.SemaphoreType.DMA,
        pltpu.SemaphoreType.DMA,
    ]
    hbm = pl.BlockSpec(memory_space=pl.ANY)
    vm = pl.BlockSpec(memory_space=pltpu.VMEM)
    solved = pl.pallas_call(
        functools.partial(kernel, places, n_gx, n_gy),
        out_shape=pltpu.VMEM(charge.shape, charge.dtype),
        in_specs=[hbm] * len(NAMES),
        out_specs=vm,
        scratch_shapes=scratch,
        name="mlc",
        compiler_params=pltpu.CompilerParams(
            collective_id=0, has_side_effects=True, vmem_limit_bytes=60 * 1024 * 1024
        ),
    )(*arrays)
    return pl.pallas_call(
        emit,
        out_shape=jax.ShapeDtypeStruct(charge.shape, charge.dtype),
        in_specs=[vm],
        out_specs=hbm,
        scratch_shapes=[pltpu.SemaphoreType.DMA],
        name="emit",
        compiler_params=pltpu.CompilerParams(vmem_limit_bytes=1024 * 1024),
    )(solved)


def solution(mesh):
    run = functools.partial(body, mesh.shape["gx"], mesh.shape["gy"])
    spec = P("gx", "gy")
    return jax.shard_map(run, mesh=mesh, in_specs=(spec,), out_specs=spec, check_vma=False)
```

```python
import functools

import jax
import jax.numpy as jnp
import ml_dtypes
import numpy as np
from jax import lax
from jax.experimental import pallas as pl
from jax.experimental.pallas import tpu as pltpu
from jax.sharding import PartitionSpec as P

P_SIZE = 32
W = 16
Q = 4
NL = 16
CLASSES = [(0, 0), (0, 1), (1, 0), (1, 1)]
MESH = pl.DeviceIdType.MESH


def sine_table(length):
    counter = np.arange(length) + 1
    return np.sin(np.pi * np.outer(counter, counter) / (length + 1))


def eigen_values(length):
    return 2.0 - 2.0 * np.cos(np.pi * (np.arange(length) + 1) / (length + 1))


def interp_table(fine_start, fine_count, coarse_start, coarse_count, ratio):
    fine_pos = np.arange(fine_count) + fine_start
    coarse_pos = np.arange(coarse_count) + coarse_start
    numerator = 2 * fine_pos - (ratio - 1)
    lower = numerator // (2 * ratio)
    weight = ((numerator - 2 * ratio * lower) / (2 * ratio))[:, None]
    below = coarse_pos[None, :] == lower[:, None]
    above = coarse_pos[None, :] == lower[:, None] + 1
    return below * (1.0 - weight) + above * weight


def legendre_basis(length, count):
    points = (2.0 * np.arange(length) + 1.0) / length - 1.0
    columns = [np.ones_like(points), points]
    for degree in range(2, count):
        columns.append(
            ((2 * degree - 1) * points * columns[-1] - (degree - 1) * columns[-2]) / degree
        )
    result = []
    for vector in columns[:count]:
        for passes in range(2):
            for earlier in result:
                vector = vector - np.sum(earlier * vector) * earlier
        result.append(vector / np.sqrt(np.sum(vector * vector)))
    return np.stack(result, axis=1)


def fold(length):
    half = length // 2
    eye = np.eye(length)
    return np.concatenate([eye[:half] + eye[::-1][:half], eye[:half] - eye[::-1][:half]])


def split(table):
    high = table.astype(ml_dtypes.bfloat16)
    low = (table - high.astype(np.float64)).astype(ml_dtypes.bfloat16)
    return high, low


@functools.lru_cache(maxsize=None)
def tables(n_gx, n_gy):
    n, length, cells = P_SIZE, P_SIZE + 2 * W, P_SIZE // Q
    blocks, margin = length // Q, W // Q
    half, hl, hb, hn = n // 2, length // 2, blocks // 2, NL // 2
    quad, wide = hb * hb, hn * hn
    nx, ny, nz = n_gx * cells, n_gy * cells, cells
    modes = ny * nz
    s_l, s_n = sine_table(length), sine_table(n)
    u_n, u_b = fold(n), fold(blocks)
    basis = legendre_basis(n, NL)
    average = np.kron(np.eye(blocks), np.full((1, Q), 1.0 / Q))
    fine = interp_table(0, length, 0, blocks, Q)
    middle = fine[W : W + n]
    picks = [W - 1, W, W + n - 1, W + n]
    a_full = average @ s_l
    b_full = basis.T @ s_l[W : W + n]
    order = np.arange(4 * NL).reshape(4, hn, 2).transpose(2, 0, 1).ravel()
    big = {}

    folding = np.zeros((4, 4, n, 4, 2 * 4, half))
    for c, (p, q) in enumerate(CLASSES):
        for vi in range(4):
            for y4 in range(4):
                il = [y4, 4 + y4, 3 - y4, 7 - y4][vi]
                sign = -1.0 if vi > 1 and p == 1 else 1.0
                folding[vi, y4, :, c, il, :] = sign * u_n[q * half : (q + 1) * half].T
    folding = folding.reshape(4 * 128, 4 * 128)
    plain = {"unfold": folding.T}

    inner = s_l[:, W : W + n] @ u_n.T / 2
    f1 = [inner[p::2, p * half : (p + 1) * half] for p in (0, 1)]
    a1 = [(u_b @ a_full)[p * hb : (p + 1) * hb, p::2] for p in (0, 1)]
    b1 = [b_full[p::2, p::2] for p in (0, 1)]
    keep, pick = np.eye(hb), np.concatenate([np.zeros((hn, hb)), np.eye(hn)], axis=1)
    keep = np.concatenate([keep, np.zeros((hb, hn))], axis=1)
    compact = []
    for p in (0, 1):
        for part in split(np.repeat(f1[p].T, half, axis=1)):
            compact.append(part.astype(np.float32))
        high, low = split(np.kron(np.eye(8), f1[p].T))
        plain["fz%d" % p] = np.concatenate([high, high])
        plain["gz%d" % p] = low
        plain["bz%d" % p] = np.concatenate(
            split(np.kron(np.eye(8), np.concatenate([a1[p], b1[p]]).T)), axis=1
        )
        sample = np.kron(a1[p], keep).T
        slab = np.kron(s_l[picks][:, p::2], pick).T
        plain["by%d" % p] = np.concatenate(split(np.concatenate([sample, sample], axis=1)), axis=1)
        plain["cy%d" % p] = np.concatenate(
            split(np.concatenate([slab, slab, np.kron(b1[p], pick).T], axis=1)), axis=1
        )

    unfold = u_b.T / 2
    pair = np.kron(unfold, unfold).reshape(blocks * blocks, 2, hb, 2, hb)

    def from_samples(table):
        folded = np.einsum("os,spaqb->pqabo", table, pair)
        return folded.reshape(4 * quad, table.shape[0])

    bm = basis.T @ middle
    lin_x = from_samples(np.kron(bm, bm)).reshape(4 * quad, NL, NL)
    lin = np.zeros((4 * quad, 384))
    for c, (p, q) in enumerate(CLASSES):
        lin[:, c * wide : (c + 1) * wide] = lin_x[:, p::2, q::2].reshape(4 * quad, wide)
    lin[:, 256:320] = from_samples(np.kron(fine[picks], bm))[:, order]
    big["lin"] = lin
    k1 = [(s_n @ u_n.T / 2)[p::2, p * half : (p + 1) * half] for p in (0, 1)]
    for c, (p, q) in enumerate(CLASSES):
        big["near%d" % c] = np.kron(k1[p], k1[q]).T
    r1 = [(u_n @ s_n / 2)[p * half : (p + 1) * half, p::2] for p in (0, 1)]
    for c, (p, q) in enumerate(CLASSES):
        big["far%d" % c] = np.kron(r1[p], r1[q]).T

    second = 2 * np.eye(blocks) - np.eye(blocks, k=1) - np.eye(blocks, k=-1)
    s_y, s_z = sine_table(ny), sine_table(nz)
    proj_z = np.zeros((nz, blocks))
    proj_z[:, margin : margin + cells] = s_z
    edge = interp_table(-1, n + 2, -1, cells + 2, Q)
    depth = interp_table(0, n, 0, cells, Q)
    lateral = edge[1 : n + 1]
    s_ext = np.zeros((ny + 2, ny))
    s_ext[1:-1] = s_y
    sp = np.concatenate([s_n[0::2], s_n[1::2]])
    deep = sp @ depth @ s_z

    def by_class(first, second_table):
        parts = []
        for p, q in CLASSES:
            parts.append(
                np.kron(first[p * half : (p + 1) * half], second_table[q * half : (q + 1) * half])
            )
        return np.concatenate(parts).T

    factor = (2.0 / (ny + 1)) * (2.0 / (nz + 1))
    spread, drop = [], []
    for b in range(n_gy):
        proj_y = np.zeros((ny, blocks))
        for j in range(blocks):
            at = j + b * cells - margin
            if 0 <= at < ny:
                proj_y[:, j] = s_y[:, at]
        flat = np.kron(proj_y, proj_z)
        curved = np.kron(proj_y @ second, proj_z) + np.kron(proj_y, proj_z @ second)
        spread.append(
            factor * np.concatenate([from_samples(curved), from_samples(flat)], axis=1)
        )
        local_s = s_ext[b * cells : b * cells + cells + 2]
        rim = np.outer(sp[:, 0], edge[0] @ local_s) + np.outer(sp[:, n - 1], edge[n + 1] @ local_s)
        drop.append(
            np.concatenate([by_class(sp @ lateral @ local_s, deep), by_class(rim, deep)])
        )
    big["spread"] = np.stack(spread)
    big["drop"] = np.stack(drop)
    sb = s_n @ basis
    sbp = np.concatenate([sb[0::2], sb[1::2]])
    facex = np.zeros((4 * wide, n * n))
    for c, (p, q) in enumerate(CLASSES):
        facex[c * wide : (c + 1) * wide, c * 256 : c * 256 + 256] = np.kron(
            sb[p::2, p::2], sb[q::2, q::2]
        ).T
    big["facex"] = facex
    ends = np.stack([sp[:, 0], sp[:, n - 1], sp[:, 0], sp[:, n - 1]], axis=1)
    big["facey"] = by_class(ends, sbp)[order]

    mu_y, mu_z = eigen_values(ny), eigen_values(nz)
    theta = np.arccosh(1.0 + (mu_y[:, None] + mu_z[None, :]).reshape(1, modes) / 2)
    below = 2 * np.sinh(theta) * (1.0 - np.exp(-2 * theta * (nx + 1)))
    apart = np.abs(np.arange(48) - 20)[:, None]
    toep = (np.exp(-theta * apart) + np.exp(-theta * np.maximum(2 * (nx + 1) - apart, 0))) / below
    total = (np.arange(2 * nx + 32) - 13)[:, None]
    hank = np.exp(-theta * np.maximum(total + 2, 0)) + np.exp(-theta * np.maximum(2 * nx - total, 0))
    hank = hank / below

    u12 = np.zeros((64, 16))
    u12[:32, :10] = np.outer(s_n[:, 0], edge[0]) + np.outer(s_n[:, n - 1], edge[n + 1])
    u12[32:, :10] = s_n @ lateral
    place = np.arange(n_gx)
    mine = []
    for a in range(n_gx):
        rank = np.arange(16)[:, None]
        at = cells * a - margin + rank
        inside = (at >= 0) & (at < nx)
        rightward = inside * np.exp(-theta * (15 - rank)) * (1 - np.exp(-2 * theta * (at + 1) * inside))
        leftward = inside * np.exp(-theta * rank) * (1 - np.exp(-2 * theta * (nx - at) * inside))
        row = np.arange(16)[:, None]
        x = cells * a - 1 + row
        used = row < cells + 2
        falling = used * np.exp(-theta * row) * (1 - np.exp(-2 * theta * np.maximum(nx - x, 0))) / below
        rising = (
            used
            * np.exp(-theta * np.maximum(cells + 1 - row, 0))
            * (1 - np.exp(-2 * theta * (x + 1)))
            / below
        )
        away = (a - place)[:, None]
        before = (away >= 2) * np.exp(-theta * np.maximum(cells * away - 12, 0))
        after = (away <= -2) * np.exp(-theta * np.maximum(-cells * away - 12, 0))
        mine.append(
            np.concatenate(
                [
                    rightward,
                    leftward,
                    u12 @ falling,
                    u12 @ rising,
                    toep,
                    hank[2 * cells * a : 2 * cells * a + 48],
                    before,
                    after,
                ]
            )
        )
    mu_l, mu_n = eigen_values(length), eigen_values(n)
    reciprocal = []
    for q in (0, 1):
        for p in (0, 1):
            pair_sum = (mu_l[p::2][:, None] + mu_l[q::2][None, :]).reshape(1, hl * hl)
            table = 1.0 / (mu_l[:, None] + pair_sum)
            reciprocal.append(table.reshape(length, 4, 256).transpose(1, 0, 2).reshape(-1, 256))
    for p, q in CLASSES:
        pair_sum = (mu_n[p::2][:, None] + mu_n[q::2][None, :]).reshape(1, 256)
        reciprocal.append((2.0 / (n + 1)) ** 3 / (mu_n[:, None] + pair_sum))
    ends = np.zeros((n, 256))
    ends[:, :2] = s_n[:, [0, n - 1]]
    reciprocal.append(ends)

    scale = (2.0 / (length + 1)) ** 3
    blank = np.zeros((12, length))
    lefts = {
        "sl": s_l[:, W : W + n],
        "means": a_full * scale,
        "flat": np.concatenate([fine[picks], blank[:, :blocks], bm]),
        "picks": np.concatenate([s_l[picks], blank, b_full]) * scale,
        "sn": s_n,
        "u12": u12,
        "sb": sb,
    }
    for name, value in lefts.items():
        high, low = split(value)
        plain[name] = np.concatenate([high, high, low], axis=1)
    singles = {
        "mine": np.stack(mine).astype(np.float32),
        "recip": np.concatenate(reciprocal).astype(np.float32),
        "compact": np.concatenate(compact),
    }
    places = {}
    for group, names in GROUPS.items():
        packs, row = [], 0
        for name in names:
            if name in plain:
                parts = [plain[name].astype(ml_dtypes.bfloat16)]
            else:
                parts = split(big[name])
            depth, width = parts[0].shape[-2:]
            place = {"left": (row, depth, width)}
            step = 256
            tiles = []
            for part in parts:
                for at in range(0, width, step):
                    tile = np.zeros(part.shape[:-1] + (256,), ml_dtypes.bfloat16)
                    piece = part[..., at : at + step]
                    tile[..., : piece.shape[-1]] = piece
                    packs.append(tile)
                    tiles.append((row, depth))
                    row += depth
            count = len(tiles) // len(parts)
            place["tiles"] = [tiles[k * count : (k + 1) * count] for k in range(len(parts))]
            places[name] = (group, place)
        most = max(tile.ndim for tile in packs)
        if most == 3:
            packs = [np.broadcast_to(tile, (n_gy,) + tile.shape[-2:]) for tile in packs]
        singles[group] = np.concatenate(packs, axis=-2)
    return singles, places


GROUPS = {
    "upz": ["fz0", "gz0", "fz1", "gz1", "sl", "means", "bz0", "bz1"],
    "downy": ["by0", "by1"],
    "spread": ["spread"],
    "side": ["picks", "flat", "sn", "sb", "u12", "lin", "cy0", "cy1"]
    + ["near%d" % c for c in range(4)]
    + ["facex", "facey"],
    "drop": ["drop"],
    "last": ["far%d" % c for c in range(4)] + ["unfold"],
}
NAMES = [
    "charge", "compact", "upz", "recip", "downy", "spread", "mine", "side", "drop", "last",
]
WAITS = [
    ["charge"], ["compact"], ["upz"], ["recip"], ["downy", "spread"], ["mine"],
    ["side", "drop", "last"],
]
CUTS = {"charge": 4, "compact": 4}


def halves(value):
    high = value.astype(jnp.bfloat16)
    return high, (value - high.astype(jnp.float32)).astype(jnp.bfloat16)


def mm(left, right):
    return jnp.dot(left, right, preferred_element_type=jnp.float32)


def window(name, shape):
    return shape[1:] if name in ("spread", "drop", "mine") else shape


def kernel(places, n_gx, n_gy, *refs):
    count = len(NAMES)
    hbm = dict(zip(NAMES, refs[:count]))
    out_ref = refs[count]
    charge_ref, compact_ref, recip_ref, mine_ref, tables_ref = refs[count + 1 : count + 6]
    vmem = {"charge": charge_ref, "compact": compact_ref, "recip": recip_ref, "mine": mine_ref}
    (
        sign_ref, grow_ref, fold_ref, w_ref, z_ref, x_ref, s_ref, b_ref, y_ref, c_ref, d_ref,
        mom_ref, far_ref, near_ref, cx_ref, cy_ref, rx_ref, ry_ref, tally_ref,
        load_sem, f_send, f_recv, p_send, p_recv,
    ) = refs[count + 6 :]
    ndev = n_gx * n_gy
    a = lax.axis_index("gx")
    b = lax.axis_index("gy")
    me = a * n_gy + b
    n, cells = P_SIZE, P_SIZE // Q
    half = n + 2 * W
    modes = near_ref.shape[-1]

    loads, base = {}, 0
    for i, names in enumerate(WAITS):
        start = base
        for name in names:
            source = hbm[name]
            if name in ("spread", "drop"):
                source = source.at[b]
            if name == "mine":
                source = source.at[a]
            if name in GROUPS:
                rows = source.shape[0]
                vmem[name] = tables_ref.at[pl.ds(base, rows)]
                base += rows
            cuts = CUTS.get(name, 1)
            each = source.shape[0] // cuts
            for k in range(cuts):
                part = pl.ds(k * each, each)
                pltpu.make_async_copy(
                    source.at[part], vmem[name].at[part], load_sem.at[i]
                ).start()
        target = tables_ref.at[pl.ds(start, base - start)] if base > start else vmem[names[0]]
        loads[names[0]] = pltpu.make_async_copy(target, target, load_sem.at[i])

    barrier = pltpu.get_barrier_semaphore()

    def greet(r, carry):
        peer = lax.rem(me + r, ndev)
        pl.semaphore_signal(
            barrier, inc=1, device_id=(peer // n_gy, lax.rem(peer, n_gy)), device_id_type=MESH
        )
        return carry

    with jax.named_scope("greet"):
        lax.fori_loop(1, ndev, greet, 0)

    def tile(name, part, i):
        group, place = places[name]
        row, depth = place["tiles"][part][i]
        return vmem[group][row : row + depth, :]

    def table(name, part):
        count = len(places[name][1]["tiles"][part])
        return jnp.concatenate([tile(name, part, i) for i in range(count)], axis=1)

    def right_mul(high, low, name):
        rows = high.shape[0]
        both = mm(jnp.concatenate([high, low], axis=0), table(name, 0))
        return both[:rows] + both[rows:] + mm(high, table(name, 1))

    def left_mul(name, high, low):
        group, place = places[name]
        row, rows, cols = place["left"]
        return mm(vmem[group][row : row + rows, 0:cols], jnp.concatenate([high, low, high], axis=0))

    groups = [[0, 1, 7, 6], [2, 3, 5, 4]]
    with jax.named_scope("signs"):
        z = lax.broadcasted_iota(jnp.int32, (n, 256), 0)
        at = lax.broadcasted_iota(jnp.int32, (n, 256), 1)
        odd = jnp.where((at // 64) % 2 == 1, -1.0, 1.0)
        base = jnp.where(z == at % 16, 1.0, 0.0) + jnp.where(z == 31 - at % 16, odd, 0.0)
        for side in range(2):
            for y in range(4):
                spot = (at // 16) % 4 == (3 - y if side else y)
                flip = jnp.where(at >= 128, -1.0, 1.0) if side else 1.0
                rows = (side * 4 + y) * n
                sign_ref[rows : rows + n] = jnp.where(spot, base * flip, 0.0).astype(jnp.bfloat16)

    with jax.named_scope("w_charge"):
        loads["charge"].wait()
    with jax.named_scope("fold"):
        charge = vmem["charge"]
        pairs = [
            jnp.concatenate([charge[:, v * 128 : (v + 1) * 128] for v in (u, 7 - u)], axis=1)
            for u in range(4)
        ]
        high, low = halves(jnp.concatenate(pairs, axis=0))
        both = mm(jnp.concatenate([high, low], axis=0), sign_ref[...])
        both = both[: 4 * n] + both[4 * n :]
        lane = lax.broadcasted_iota(jnp.int32, (half, 128), 1)
        folded = []
        for p in range(2):
            rows = [both[v * n : (v + 1) * n, p * 128 : (p + 1) * 128] for v in range(4)]
            turn = [pltpu.roll(row, 64, 1) for row in rows]
            left = lane[:n] < 64
            folded += [jnp.where(left, rows[v], turn[v + 1]) for v in (0, 2)]
            folded += [jnp.where(left, turn[v], rows[v + 1]) for v in (0, 2)]
        folded = halves(jnp.concatenate(folded, axis=1))
        fold_ref[0] = folded[0]
        fold_ref[1] = folded[1]
        for c in range(4):
            at = slice(c * 256, (c + 1) * 256)
            q = c % 2
            w_ref[c // 2, q * n : (q + 1) * n] = folded[0][:, at]
            w_ref[c // 2, (2 + q) * n : (3 + q) * n] = folded[1][:, at]
    with jax.named_scope("grow"):
        loads["compact"].wait()
        same = lax.broadcasted_iota(jnp.int32, (16, 512), 0)
        same = jnp.where(lax.broadcasted_iota(jnp.int32, (16, 512), 1) % 16 == same, 1.0, 0.0)
        same = same.astype(jnp.bfloat16)
        for t in range(4):
            for i in range(16):
                line = jnp.broadcast_to(compact_ref[t * 16 + i : t * 16 + i + 1], (16, 512))
                grow_ref[t, i * 16 : (i + 1) * 16] = line.astype(jnp.bfloat16) * same
    with jax.named_scope("upy"):
        for p in range(2):
            both = mm(w_ref[p], grow_ref[2 * p])
            lift = both[: 2 * n] + both[2 * n :] + mm(w_ref[p, 0 : 2 * n], grow_ref[2 * p + 1])
            high, low = halves(lift)
            for q in range(2):
                for k in range(4):
                    at = (4 * p + k) * n
                    rows, lanes = slice(q * n, (q + 1) * n), slice(k * 128, (k + 1) * 128)
                    z_ref[q, at : at + n, 0:128] = high[rows, lanes]
                    z_ref[q, at : at + n, 128:256] = low[rows, lanes]
    with jax.named_scope("w_upz"):
        loads["upz"].wait()
    with jax.named_scope("upz"):
        for q in range(2):
            up = mm(z_ref[q], tile("fz%d" % q, 0, 0)) + mm(z_ref[q, :, 0:128], tile("gz%d" % q, 0, 0))
            high, low = halves(up)
            for k in range(8):
                rows, lanes = slice(k * n, (k + 1) * n), slice((8 * q + k) * 256, (8 * q + k + 1) * 256)
                x_ref[0:n, lanes] = high[rows]
                x_ref[n : 2 * n, lanes] = low[rows]
    with jax.named_scope("w_recip"):
        loads["recip"].wait()
    with jax.named_scope("upx"):
        group, place = places["sl"]
        row, rows, cols = place["left"]
        weights = vmem[group][row : row + rows, 0:cols]
        for q in range(2):
            lanes = slice(q * 2048, (q + 1) * 2048)
            spectrum = mm(
                weights, jnp.concatenate([x_ref[:, lanes], x_ref[0:n, lanes]], axis=0)
            )
            divisor = [
                vmem["recip"][(8 * q + k) * half : (8 * q + k + 1) * half] for k in range(8)
            ]
            high, low = halves(spectrum * jnp.concatenate(divisor, axis=1))
            s_ref[0:half, lanes] = high
            s_ref[half : 2 * half, lanes] = low

    def down(name, rows, b_ref, y_ref, finish):
        group, place = places[name]
        row, _, cols = place["left"]
        weights = vmem[group][row : row + rows, 0:cols]
        for q in range(2):
            lanes = slice(q * 2048, (q + 1) * 2048)
            short = mm(weights, jnp.concatenate([s_ref[:, lanes], s_ref[0:half, lanes]], axis=0))
            high, low = halves(short)
            for k in range(8):
                lanes = slice(k * 256, (k + 1) * 256)
                b_ref[q, k * rows : (k + 1) * rows] = high[:, lanes]
                b_ref[q, (8 + k) * rows : (9 + k) * rows] = low[:, lanes]
        for q in range(2):
            both = mm(b_ref[q], tile("bz%d" % q, 0, 0))
            block = 8 * rows
            high, low = halves(both[:block, :128] + both[block:, :128] + both[:block, 128:])
            for p in range(2):
                for k in range(4):
                    at, lanes = (4 * p + k) * rows, slice(k * 128, (k + 1) * 128)
                    y_ref[p, q * rows : (q + 1) * rows, lanes] = high[at : at + rows]
                    y_ref[p, (2 + q) * rows : (3 + q) * rows, lanes] = low[at : at + rows]
        ys = []
        finish()
        for p in range(2):
            both = mm(y_ref[p], tile("%sy%d" % ("b" if name == "means" else "c", p), 0, 0))
            both = both[: 2 * rows, :128] + both[2 * rows :, :128] + both[: 2 * rows, 128:]
            ys += [both[:rows], both[rows:]]
        return ys

    def arrive():
        loads["downy"].wait()
        loads["mine"].wait()

    with jax.named_scope("down"):
        y0, y1, y2, y3 = down("means", 16, b_ref, y_ref, arrive)
    with jax.named_scope("spread"):
        sample = jnp.concatenate(
            [jnp.where(lane[0:16] < 64, u, v) for u, v in ((y0, y1), (y2, y3))], axis=1
        )
        sample = halves(sample)
        spread = right_mul(*sample, "spread")
        bend = spread[:, modes:]
        gap = jnp.zeros((1, modes), jnp.float32)
        packet = spread[:, :modes] + 2.0 * bend
        packet = packet - jnp.concatenate([gap, bend[:-1]]) - jnp.concatenate([bend[1:], gap])
        mine = vmem["mine"]
        near_ref[n_gy + b] = packet
        rightward = jnp.sum(packet * mine[0:16], axis=0, keepdims=True)
        leftward = jnp.sum(packet * mine[16:32], axis=0, keepdims=True)
        for g in range(modes // 128):
            mom_ref[g, 0:1] = rightward[:, g * 128 : (g + 1) * 128]
            mom_ref[g, 1:2] = leftward[:, g * 128 : (g + 1) * 128]

    with jax.named_scope("barrier"):
        pl.semaphore_wait(barrier, ndev - 1)

    def remote(source, target, send, recv, device):
        return pltpu.make_async_remote_copy(
            src_ref=source,
            dst_ref=target,
            send_sem=send,
            recv_sem=recv,
            device_id=device,
            device_id_type=MESH,
        )

    def start_far(r, carry):
        d = n_gx - r
        for j in range(n_gy):
            for row, other, fine in ((0, a + d, a + d < n_gx), (1, a - d, a >= d)):

                @pl.when(fine)
                def _():
                    remote(
                        mom_ref.at[:, pl.ds(row, 1)],
                        far_ref.at[b, :, pl.ds(a, 1)],
                        f_send,
                        f_recv,
                        (other, j),
                    ).start()

        return carry

    with jax.named_scope("send"):
        lax.fori_loop(1, n_gx - 1, start_far, 0)
        for step in (0, 1, 2):
            for j in range(n_gy):
                other = a + step - 1
                fine = (other >= 0) & (other < n_gx)
                if step == 1:
                    fine = b != j

                @pl.when(fine)
                def _():
                    remote(
                        near_ref.at[n_gy + b],
                        near_ref.at[(2 - step) * n_gy + b],
                        p_send,
                        p_recv,
                        (other, j),
                    ).start()

    with jax.named_scope("w_side"):
        loads["side"].wait()
    with jax.named_scope("lin"):
        y0, y1, y2, y3 = down("picks", 32, c_ref, d_ref, lambda: None)
        flat = right_mul(*halves(left_mul("flat", *sample)), "lin")
        cx = jnp.concatenate(
            [
                jnp.where(lane[0:8] < 64, pltpu.roll(u[0:8], 64, 1), v[0:8])
                for u, v in ((y0, y1), (y2, y3))
            ],
            axis=1,
        )
        cx = cx - flat[0:8, 0:256]
        cy = jnp.where(lane[0:16] < 32, y0[16:] + y2[16:], y1[16:] + y3[16:])
        cy = cy - flat[16:32, 256:384]
        cx_ref[...] = cx
        cy_ref[...] = cy

    upper, lower = lax.rem(b + 1, n_gy), lax.rem(b + n_gy - 1, n_gy)
    with jax.named_scope("sendc"):

        @pl.when(a < n_gx - 1)
        def _():
            remote(
                cx_ref.at[pl.ds(2, 1)], rx_ref.at[pl.ds(0, 1)], p_send, p_recv, (a + 1, b)
            ).start()

        @pl.when(a > 0)
        def _():
            remote(
                cx_ref.at[pl.ds(1, 1)], rx_ref.at[pl.ds(1, 1)], p_send, p_recv, (a - 1, b)
            ).start()

        remote(cy_ref, ry_ref.at[0], p_send, p_recv, (a, upper)).start()
        remote(cy_ref, ry_ref.at[1], p_send, p_recv, (a, lower)).start()

    with jax.named_scope("near"):
        narrow = halves(left_mul("sn", fold_ref[0], fold_ref[1]))
        spectrum = []
        for c in range(4):
            at = slice(c * 256, (c + 1) * 256)
            spectrum.append(right_mul(narrow[0][:, at], narrow[1][:, at], "near%d" % c))
        spectrum = jnp.concatenate(spectrum, axis=1)

    edge = (a == 0) | (a == n_gx - 1)
    inner = jnp.logical_not(edge)

    def settle_near(sides):
        lines = 16 * (modes // 128) * ((1 + sides) * n_gy - 1) + 2 * sides + 32
        block = tally_ref.at[pl.ds(0, lines)]
        remote(block, block, p_send, p_recv, (a, b)).wait()

    with jax.named_scope("wait_p"):

        @pl.when(edge)
        def _():
            settle_near(1)

        @pl.when(inner)
        def _():
            settle_near(2)

    with jax.named_scope("face"):
        from_left = jnp.where(a > 0, rx_ref[0:1], 0.0)
        from_right = jnp.where(a < n_gx - 1, rx_ref[1:2], 0.0)
        ends = jnp.concatenate(
            [cx[0:1] + from_left, cx[3:4] + from_right, jnp.zeros((14, cx.shape[1]), jnp.float32)]
        )
        ends = right_mul(*halves(ends), "facex")
        fine = 16 * half
        column = vmem["recip"][fine + 4 * n : fine + 5 * n, 0:2]
        spectrum = spectrum + column[:, 0:1] * ends[0:1] + column[:, 1:2] * ends[1:2]
        group = jnp.where(lane[0:16] < 64, lax.rem(lane[0:16], 32) // 8, 4)
        total = jnp.where((group == 0) | (group == 3), cy, 0.0)
        total = total + jnp.where((group == 2) & (b > 0), ry_ref[0], 0.0)
        total = total + jnp.where((group == 1) & (b < n_gy - 1), ry_ref[1], 0.0)
        total = left_mul("sb", *halves(total))[:, 0:64]
        spectrum = spectrum + right_mul(*halves(total), "facey")
    with jax.named_scope("green"):
        row = lax.broadcasted_iota(jnp.int32, (8, modes), 0)

        def gathered(step):
            value = near_ref[step * n_gy]
            for j in range(1, n_gy):
                value = value + near_ref[step * n_gy + j]
            return value

        past = jnp.where(a > 0, gathered(0), 0.0)
        here = gathered(1)
        next_ = jnp.where(a < n_gx - 1, gathered(2), 0.0)
        source = jnp.concatenate(
            [
                jnp.where((row >= 4) | (a > 1), past[0:8], 0.0),
                past[8:16] + jnp.where((row >= 4) | (a > 0), here[0:8], 0.0),
                jnp.where((row < 4) | (a < n_gx - 1), here[8:16] + next_[0:8], 0.0),
                jnp.where((row < 4) | (a < n_gx - 2), next_[8:16], 0.0),
            ]
        )
        values = []
        for i in range(cells + 2):
            influence = mine[169 - i : 201 - i] - mine[208 + i : 240 + i]
            values.append(jnp.sum(influence * source, axis=0, keepdims=True))
        values.append(jnp.zeros((16 - len(values), modes), jnp.float32))
        lifted = left_mul("u12", *halves(jnp.concatenate(values, axis=0)))

    def settle_far(each):
        block = far_ref.at[:, :, pl.ds(0, each)]
        remote(block, block, f_send, f_recv, (a, b)).wait()

    with jax.named_scope("wait_f"):

        @pl.when(edge)
        def _():
            settle_far(n_gx - 2)

        @pl.when(inner)
        def _():
            settle_far(n_gx - 3)

    with jax.named_scope("final"):
        origin = lax.broadcasted_iota(jnp.int32, (n_gx, modes), 0)
        before = jnp.zeros((n_gx, modes), jnp.float32)
        after = before
        for j in range(n_gy):
            sent = jnp.concatenate([far_ref[j, g] for g in range(modes // 128)], axis=1)
            before = before + jnp.where(origin <= a - 2, sent, 0.0)
            after = after + jnp.where(origin >= a + 2, sent, 0.0)
        before = jnp.sum(before * mine[256 : 256 + n_gx], axis=0, keepdims=True)
        after = jnp.sum(after * mine[256 + n_gx : 256 + 2 * n_gx], axis=0, keepdims=True)
        lifted = lifted + mine[32:96] * before + mine[96:160] * after
        lifted = halves(jnp.concatenate([lifted[:n], lifted[n:]], axis=1))
        inverse = jnp.concatenate(
            [vmem["recip"][fine + c * n : fine + (c + 1) * n] for c in range(4)], axis=1
        )
        spectrum = (spectrum + right_mul(*lifted, "drop")) * inverse
        high, low = halves(left_mul("sn", *halves(spectrum)))
        parts = []
        for c in range(4):
            at = slice(c * 256, (c + 1) * 256)
            parts.append(right_mul(high[:, at], low[:, at], "far%d" % c))
    with jax.named_scope("unfold"):
        sides = [
            jnp.concatenate([part[:, s * 128 : (s + 1) * 128] for part in parts], axis=1)
            for s in range(2)
        ]
        high, low = halves(jnp.concatenate(sides, axis=0))
        stacked = jnp.concatenate([high, low], axis=0)
        both = mm(stacked, table("unfold", 0))
        both = both[: 2 * n] + both[2 * n :]
        for s, group in enumerate(groups):
            for i, v in enumerate(group):
                out_ref[:, v * 128 : (v + 1) * 128] = both[
                    s * n : (s + 1) * n, i * 128 : (i + 1) * 128
                ]


def emit(in_ref, out_ref, sem):
    copy = pltpu.make_async_copy(in_ref, out_ref, sem)
    copy.start()
    copy.wait()


def body(n_gx, n_gy, charge):
    singles, places = tables(n_gx, n_gy)
    arrays = [charge] + [jnp.asarray(singles[name]) for name in NAMES[1:]]
    shapes = {name: window(name, array.shape) for name, array in zip(NAMES, arrays)}
    total = sum(shapes[name][0] for name in GROUPS)
    scratch = [pltpu.VMEM(shapes[name], jnp.float32) for name in ("charge", "compact", "recip", "mine")]
    scratch.append(pltpu.VMEM((total, 256), jnp.bfloat16))
    modes = n_gy * (P_SIZE // Q) ** 2
    half = P_SIZE + 2 * W
    scratch += [
        pltpu.VMEM((256, 256), jnp.bfloat16),
        pltpu.VMEM((4, 256, 512), jnp.bfloat16),
        pltpu.VMEM((2, P_SIZE, 1024), jnp.bfloat16),
        pltpu.VMEM((2, 4 * P_SIZE, 256), jnp.bfloat16),
        pltpu.VMEM((2, 8 * P_SIZE, 256), jnp.bfloat16),
        pltpu.VMEM((2 * P_SIZE, 4096), jnp.bfloat16),
        pltpu.VMEM((2 * half, 4096), jnp.bfloat16),
        pltpu.VMEM((2, 256, 256), jnp.bfloat16),
        pltpu.VMEM((2, 64, 512), jnp.bfloat16),
        pltpu.VMEM((2, 512, 256), jnp.bfloat16),
        pltpu.VMEM((2, 128, 512), jnp.bfloat16),
        pltpu.VMEM((modes // 128, 8, 128), jnp.float32),
        pltpu.VMEM((n_gy, modes // 128, n_gx, 128), jnp.float32),
        pltpu.VMEM((3 * n_gy, 16, modes), jnp.float32),
        pltpu.VMEM((8, 256), jnp.float32),
        pltpu.VMEM((16, 128), jnp.float32),
        pltpu.VMEM((8, 256), jnp.float32),
        pltpu.VMEM((2, 16, 128), jnp.float32),
        pltpu.VMEM((16 * (modes // 128) * (3 * n_gy - 1) + 40, 128), jnp.float32),
        pltpu.SemaphoreType.DMA((len(WAITS),)),
        pltpu.SemaphoreType.DMA,
        pltpu.SemaphoreType.DMA,
        pltpu.SemaphoreType.DMA,
        pltpu.SemaphoreType.DMA,
    ]
    hbm = pl.BlockSpec(memory_space=pl.ANY)
    vm = pl.BlockSpec(memory_space=pltpu.VMEM)
    solved = pl.pallas_call(
        functools.partial(kernel, places, n_gx, n_gy),
        out_shape=pltpu.VMEM(charge.shape, charge.dtype),
        in_specs=[hbm] * len(NAMES),
        out_specs=vm,
        scratch_shapes=scratch,
        name="mlc",
        compiler_params=pltpu.CompilerParams(
            collective_id=0, has_side_effects=True, vmem_limit_bytes=60 * 1024 * 1024
        ),
    )(*arrays)
    return pl.pallas_call(
        emit,
        out_shape=jax.ShapeDtypeStruct(charge.shape, charge.dtype),
        in_specs=[vm],
        out_specs=hbm,
        scratch_shapes=[pltpu.SemaphoreType.DMA],
        name="emit",
        compiler_params=pltpu.CompilerParams(vmem_limit_bytes=1024 * 1024),
    )(solved)


def solution(mesh):
    run = functools.partial(body, mesh.shape["gx"], mesh.shape["gy"])
    spec = P("gx", "gy")
    return jax.shard_map(run, mesh=mesh, in_specs=(spec,), out_specs=spec, check_vma=False)
```

```python
import functools

import jax
import jax.numpy as jnp
import ml_dtypes
import numpy as np
from jax import lax
from jax.experimental import pallas as pl
from jax.experimental.pallas import tpu as pltpu
from jax.sharding import PartitionSpec as P

P_SIZE = 32
W = 16
Q = 4
NL = 16
CLASSES = [(0, 0), (0, 1), (1, 0), (1, 1)]
MESH = pl.DeviceIdType.MESH


def sine_table(length):
    counter = np.arange(length) + 1
    return np.sin(np.pi * np.outer(counter, counter) / (length + 1))


def eigen_values(length):
    return 2.0 - 2.0 * np.cos(np.pi * (np.arange(length) + 1) / (length + 1))


def interp_table(fine_start, fine_count, coarse_start, coarse_count, ratio):
    fine_pos = np.arange(fine_count) + fine_start
    coarse_pos = np.arange(coarse_count) + coarse_start
    numerator = 2 * fine_pos - (ratio - 1)
    lower = numerator // (2 * ratio)
    weight = ((numerator - 2 * ratio * lower) / (2 * ratio))[:, None]
    below = coarse_pos[None, :] == lower[:, None]
    above = coarse_pos[None, :] == lower[:, None] + 1
    return below * (1.0 - weight) + above * weight


def legendre_basis(length, count):
    points = (2.0 * np.arange(length) + 1.0) / length - 1.0
    columns = [np.ones_like(points), points]
    for degree in range(2, count):
        columns.append(
            ((2 * degree - 1) * points * columns[-1] - (degree - 1) * columns[-2]) / degree
        )
    result = []
    for vector in columns[:count]:
        for passes in range(2):
            for earlier in result:
                vector = vector - np.sum(earlier * vector) * earlier
        result.append(vector / np.sqrt(np.sum(vector * vector)))
    return np.stack(result, axis=1)


def fold(length):
    half = length // 2
    eye = np.eye(length)
    return np.concatenate([eye[:half] + eye[::-1][:half], eye[:half] - eye[::-1][:half]])


def split(table):
    high = table.astype(ml_dtypes.bfloat16)
    low = (table - high.astype(np.float64)).astype(ml_dtypes.bfloat16)
    return high, low


@functools.lru_cache(maxsize=None)
def tables(n_gx, n_gy):
    n, length, cells = P_SIZE, P_SIZE + 2 * W, P_SIZE // Q
    blocks, margin = length // Q, W // Q
    half, hl, hb, hn = n // 2, length // 2, blocks // 2, NL // 2
    quad, wide = hb * hb, hn * hn
    nx, ny, nz = n_gx * cells, n_gy * cells, cells
    modes = ny * nz
    s_l, s_n = sine_table(length), sine_table(n)
    u_n, u_b = fold(n), fold(blocks)
    basis = legendre_basis(n, NL)
    average = np.kron(np.eye(blocks), np.full((1, Q), 1.0 / Q))
    fine = interp_table(0, length, 0, blocks, Q)
    middle = fine[W : W + n]
    picks = [W - 1, W, W + n - 1, W + n]
    a_full = average @ s_l
    b_full = basis.T @ s_l[W : W + n]
    order = np.arange(4 * NL).reshape(4, hn, 2).transpose(2, 0, 1).ravel()
    big = {}

    folding = np.zeros((4, 4, n, 4, 2 * 4, half))
    for c, (p, q) in enumerate(CLASSES):
        for vi in range(4):
            for y4 in range(4):
                il = [y4, 4 + y4, 3 - y4, 7 - y4][vi]
                sign = -1.0 if vi > 1 and p == 1 else 1.0
                folding[vi, y4, :, c, il, :] = sign * u_n[q * half : (q + 1) * half].T
    folding = folding.reshape(4 * 128, 4 * 128)
    plain = {"unfold": folding.T}

    inner = s_l[:, W : W + n] @ u_n.T / 2
    f1 = [inner[p::2, p * half : (p + 1) * half] for p in (0, 1)]
    a1 = [(u_b @ a_full)[p * hb : (p + 1) * hb, p::2] for p in (0, 1)]
    b1 = [b_full[p::2, p::2] for p in (0, 1)]
    keep, pick = np.eye(hb), np.concatenate([np.zeros((hn, hb)), np.eye(hn)], axis=1)
    keep = np.concatenate([keep, np.zeros((hb, hn))], axis=1)
    compact = []
    for p in (0, 1):
        for part in split(np.repeat(f1[p].T, half, axis=1)):
            compact.append(part.astype(np.float32))
        high, low = split(np.kron(np.eye(8), f1[p].T))
        plain["fz%d" % p] = np.concatenate([high, high])
        plain["gz%d" % p] = low
        plain["bz%d" % p] = np.concatenate(
            split(np.kron(np.eye(8), np.concatenate([a1[p], b1[p]]).T)), axis=1
        )
        sample = np.kron(a1[p], keep).T
        slab = np.kron(s_l[picks][:, p::2], pick).T
        plain["by%d" % p] = np.concatenate(split(np.concatenate([sample, sample], axis=1)), axis=1)
        plain["cy%d" % p] = np.concatenate(
            split(np.concatenate([slab, slab, np.kron(b1[p], pick).T], axis=1)), axis=1
        )

    unfold = u_b.T / 2
    pair = np.kron(unfold, unfold).reshape(blocks * blocks, 2, hb, 2, hb)

    def from_samples(table):
        folded = np.einsum("os,spaqb->pqabo", table, pair)
        return folded.reshape(4 * quad, table.shape[0])

    bm = basis.T @ middle
    lin_x = from_samples(np.kron(bm, bm)).reshape(4 * quad, NL, NL)
    lin = np.zeros((4 * quad, 384))
    for c, (p, q) in enumerate(CLASSES):
        lin[:, c * wide : (c + 1) * wide] = lin_x[:, p::2, q::2].reshape(4 * quad, wide)
    lin[:, 256:320] = from_samples(np.kron(fine[picks], bm))[:, order]
    big["lin"] = lin
    k1 = [(s_n @ u_n.T / 2)[p::2, p * half : (p + 1) * half] for p in (0, 1)]
    for c, (p, q) in enumerate(CLASSES):
        big["near%d" % c] = np.kron(k1[p], k1[q]).T
    r1 = [(u_n @ s_n / 2)[p * half : (p + 1) * half, p::2] for p in (0, 1)]
    for c, (p, q) in enumerate(CLASSES):
        big["far%d" % c] = np.kron(r1[p], r1[q]).T

    second = 2 * np.eye(blocks) - np.eye(blocks, k=1) - np.eye(blocks, k=-1)
    s_y, s_z = sine_table(ny), sine_table(nz)
    proj_z = np.zeros((nz, blocks))
    proj_z[:, margin : margin + cells] = s_z
    edge = interp_table(-1, n + 2, -1, cells + 2, Q)
    depth = interp_table(0, n, 0, cells, Q)
    lateral = edge[1 : n + 1]
    s_ext = np.zeros((ny + 2, ny))
    s_ext[1:-1] = s_y
    sp = np.concatenate([s_n[0::2], s_n[1::2]])
    deep = sp @ depth @ s_z

    def by_class(first, second_table):
        parts = []
        for p, q in CLASSES:
            parts.append(
                np.kron(first[p * half : (p + 1) * half], second_table[q * half : (q + 1) * half])
            )
        return np.concatenate(parts).T

    factor = (2.0 / (ny + 1)) * (2.0 / (nz + 1))
    spread, drop = [], []
    for b in range(n_gy):
        proj_y = np.zeros((ny, blocks))
        for j in range(blocks):
            at = j + b * cells - margin
            if 0 <= at < ny:
                proj_y[:, j] = s_y[:, at]
        flat = np.kron(proj_y, proj_z)
        curved = np.kron(proj_y @ second, proj_z) + np.kron(proj_y, proj_z @ second)
        spread.append(
            factor * np.concatenate([from_samples(curved), from_samples(flat)], axis=1)
        )
        local_s = s_ext[b * cells : b * cells + cells + 2]
        rim = np.outer(sp[:, 0], edge[0] @ local_s) + np.outer(sp[:, n - 1], edge[n + 1] @ local_s)
        drop.append(
            np.concatenate([by_class(sp @ lateral @ local_s, deep), by_class(rim, deep)])
        )
    big["spread"] = np.stack(spread)
    big["drop"] = np.stack(drop)
    sb = s_n @ basis
    sbp = np.concatenate([sb[0::2], sb[1::2]])
    facex = np.zeros((4 * wide, n * n))
    for c, (p, q) in enumerate(CLASSES):
        facex[c * wide : (c + 1) * wide, c * 256 : c * 256 + 256] = np.kron(
            sb[p::2, p::2], sb[q::2, q::2]
        ).T
    big["facex"] = facex
    ends = np.stack([sp[:, 0], sp[:, n - 1], sp[:, 0], sp[:, n - 1]], axis=1)
    big["facey"] = by_class(ends, sbp)[order]

    mu_y, mu_z = eigen_values(ny), eigen_values(nz)
    theta = np.arccosh(1.0 + (mu_y[:, None] + mu_z[None, :]).reshape(1, modes) / 2)
    below = 2 * np.sinh(theta) * (1.0 - np.exp(-2 * theta * (nx + 1)))
    apart = np.abs(np.arange(48) - 20)[:, None]
    toep = (np.exp(-theta * apart) + np.exp(-theta * np.maximum(2 * (nx + 1) - apart, 0))) / below
    total = (np.arange(2 * nx + 32) - 13)[:, None]
    hank = np.exp(-theta * np.maximum(total + 2, 0)) + np.exp(-theta * np.maximum(2 * nx - total, 0))
    hank = hank / below

    u12 = np.zeros((64, 16))
    u12[:32, :10] = np.outer(s_n[:, 0], edge[0]) + np.outer(s_n[:, n - 1], edge[n + 1])
    u12[32:, :10] = s_n @ lateral
    place = np.arange(n_gx)
    mine = []
    for a in range(n_gx):
        rank = np.arange(16)[:, None]
        at = cells * a - margin + rank
        inside = (at >= 0) & (at < nx)
        rightward = inside * np.exp(-theta * (15 - rank)) * (1 - np.exp(-2 * theta * (at + 1) * inside))
        leftward = inside * np.exp(-theta * rank) * (1 - np.exp(-2 * theta * (nx - at) * inside))
        row = np.arange(16)[:, None]
        x = cells * a - 1 + row
        used = row < cells + 2
        falling = used * np.exp(-theta * row) * (1 - np.exp(-2 * theta * np.maximum(nx - x, 0))) / below
        rising = (
            used
            * np.exp(-theta * np.maximum(cells + 1 - row, 0))
            * (1 - np.exp(-2 * theta * (x + 1)))
            / below
        )
        away = (a - place)[:, None]
        before = (away >= 2) * np.exp(-theta * np.maximum(cells * away - 12, 0))
        after = (away <= -2) * np.exp(-theta * np.maximum(-cells * away - 12, 0))
        mine.append(
            np.concatenate(
                [
                    rightward,
                    leftward,
                    u12 @ falling,
                    u12 @ rising,
                    toep,
                    hank[2 * cells * a : 2 * cells * a + 48],
                    before,
                    after,
                ]
            )
        )
    mu_l, mu_n = eigen_values(length), eigen_values(n)
    reciprocal = []
    for q in (0, 1):
        for p in (0, 1):
            pair_sum = (mu_l[p::2][:, None] + mu_l[q::2][None, :]).reshape(1, hl * hl)
            table = 1.0 / (mu_l[:, None] + pair_sum)
            reciprocal.append(table.reshape(length, 4, 256).transpose(1, 0, 2).reshape(-1, 256))
    for p, q in CLASSES:
        pair_sum = (mu_n[p::2][:, None] + mu_n[q::2][None, :]).reshape(1, 256)
        reciprocal.append((2.0 / (n + 1)) ** 3 / (mu_n[:, None] + pair_sum))
    ends = np.zeros((n, 256))
    ends[:, :2] = s_n[:, [0, n - 1]]
    reciprocal.append(ends)

    scale = (2.0 / (length + 1)) ** 3
    blank = np.zeros((12, length))
    lefts = {
        "sl": s_l[:, W : W + n],
        "means": a_full * scale,
        "flat": np.concatenate([fine[picks], blank[:, :blocks], bm]),
        "picks": np.concatenate([s_l[picks], blank, b_full]) * scale,
        "sn": s_n,
        "u12": u12,
        "sb": sb,
    }
    for name, value in lefts.items():
        high, low = split(value)
        plain[name] = np.concatenate([high, high, low], axis=1)
    singles = {
        "mine": np.stack(mine).astype(np.float32),
        "recip": np.concatenate(reciprocal).astype(np.float32),
        "compact": np.concatenate(compact),
    }
    places = {}
    for group, names in GROUPS.items():
        packs, row = [], 0
        for name in names:
            if name in plain:
                parts = [plain[name].astype(ml_dtypes.bfloat16)]
            else:
                parts = split(big[name])
            depth, width = parts[0].shape[-2:]
            place = {"left": (row, depth, width)}
            step = 256
            tiles = []
            for part in parts:
                for at in range(0, width, step):
                    tile = np.zeros(part.shape[:-1] + (256,), ml_dtypes.bfloat16)
                    piece = part[..., at : at + step]
                    tile[..., : piece.shape[-1]] = piece
                    packs.append(tile)
                    tiles.append((row, depth))
                    row += depth
            count = len(tiles) // len(parts)
            place["tiles"] = [tiles[k * count : (k + 1) * count] for k in range(len(parts))]
            places[name] = (group, place)
        most = max(tile.ndim for tile in packs)
        if most == 3:
            packs = [np.broadcast_to(tile, (n_gy,) + tile.shape[-2:]) for tile in packs]
        singles[group] = np.concatenate(packs, axis=-2)
    return singles, places


GROUPS = {
    "upz": ["fz0", "gz0", "fz1", "gz1", "sl", "means", "bz0", "bz1"],
    "downy": ["by0", "by1"],
    "spread": ["spread"],
    "side": ["picks", "flat", "sn", "sb", "u12", "lin", "cy0", "cy1"]
    + ["near%d" % c for c in range(4)]
    + ["facex", "facey"],
    "drop": ["drop"],
    "last": ["far%d" % c for c in range(4)] + ["unfold"],
}
NAMES = [
    "charge", "compact", "upz", "recip", "downy", "spread", "mine", "side", "drop", "last",
]
WAITS = [
    ["charge"], ["compact"], ["upz"], ["recip"], ["downy", "spread"], ["mine"],
    ["side", "drop", "last"],
]
CUTS = {"charge": 4, "compact": 4}


def halves(value):
    high = value.astype(jnp.bfloat16)
    return high, (value - high.astype(jnp.float32)).astype(jnp.bfloat16)


def mm(left, right):
    return jnp.dot(left, right, preferred_element_type=jnp.float32)


def window(name, shape):
    return shape[1:] if name in ("spread", "drop", "mine") else shape


def kernel(places, n_gx, n_gy, *refs):
    count = len(NAMES)
    hbm = dict(zip(NAMES, refs[:count]))
    out_ref = refs[count]
    charge_ref, compact_ref, recip_ref, mine_ref, tables_ref = refs[count + 1 : count + 6]
    vmem = {"charge": charge_ref, "compact": compact_ref, "recip": recip_ref, "mine": mine_ref}
    (
        sign_ref, grow_ref, fold_ref, w_ref, z_ref, x_ref, s_ref, b_ref, y_ref, c_ref, d_ref,
        mom_ref, far_ref, near_ref, cx_ref, cy_ref, rx_ref, ry_ref, tally_ref,
        load_sem, f_send, f_recv, p_send, p_recv,
    ) = refs[count + 6 :]
    ndev = n_gx * n_gy
    a = lax.axis_index("gx")
    b = lax.axis_index("gy")
    me = a * n_gy + b
    n, cells = P_SIZE, P_SIZE // Q
    half = n + 2 * W
    modes = near_ref.shape[-1]

    loads, base = {}, 0
    for i, names in enumerate(WAITS):
        start = base
        for name in names:
            source = hbm[name]
            if name in ("spread", "drop"):
                source = source.at[b]
            if name == "mine":
                source = source.at[a]
            if name in GROUPS:
                rows = source.shape[0]
                vmem[name] = tables_ref.at[pl.ds(base, rows)]
                base += rows
            cuts = CUTS.get(name, 1)
            each = source.shape[0] // cuts
            for k in range(cuts):
                part = pl.ds(k * each, each)
                pltpu.make_async_copy(
                    source.at[part], vmem[name].at[part], load_sem.at[i]
                ).start()
        target = tables_ref.at[pl.ds(start, base - start)] if base > start else vmem[names[0]]
        loads[names[0]] = pltpu.make_async_copy(target, target, load_sem.at[i])

    barrier = pltpu.get_barrier_semaphore()

    def greet(r, carry):
        peer = lax.rem(me + r, ndev)
        pl.semaphore_signal(
            barrier, inc=1, device_id=(peer // n_gy, lax.rem(peer, n_gy)), device_id_type=MESH
        )
        return carry

    with jax.named_scope("greet"):
        lax.fori_loop(1, ndev, greet, 0)

    def tile(name, part, i):
        group, place = places[name]
        row, depth = place["tiles"][part][i]
        return vmem[group][row : row + depth, :]

    def table(name, part):
        count = len(places[name][1]["tiles"][part])
        return jnp.concatenate([tile(name, part, i) for i in range(count)], axis=1)

    def right_mul(high, low, name):
        rows = high.shape[0]
        both = mm(jnp.concatenate([high, low], axis=0), table(name, 0))
        return both[:rows] + both[rows:] + mm(high, table(name, 1))

    def left_mul(name, high, low):
        group, place = places[name]
        row, rows, cols = place["left"]
        return mm(vmem[group][row : row + rows, 0:cols], jnp.concatenate([high, low, high], axis=0))

    groups = [[0, 1, 7, 6], [2, 3, 5, 4]]
    with jax.named_scope("signs"):
        z = lax.broadcasted_iota(jnp.int32, (n, 512), 0)
        at = lax.broadcasted_iota(jnp.int32, (n, 512), 1)
        odd = jnp.where((at // 128) % 2 == 1, -1.0, 1.0)
        base = jnp.where(z == at % 16, 1.0, 0.0) + jnp.where(z == 31 - at % 16, odd, 0.0)
        turned = jnp.where(at >= 256, -base, base)
        spot = (at // 16) % 8
        for side, value in ((0, base), (1, turned)):
            for y in range(8):
                rows = (side * 8 + y) * n
                match = spot == ((3 - y) % 8 if side else y)
                sign_ref[rows : rows + n] = jnp.where(match, value, 0.0).astype(jnp.bfloat16)

    with jax.named_scope("w_charge"):
        loads["charge"].wait()
    with jax.named_scope("fold"):
        charge = vmem["charge"]
        sides = [
            jnp.concatenate([charge[:, v * 128 : (v + 1) * 128] for v in group], axis=1)
            for group in groups
        ]
        high, low = halves(jnp.concatenate(sides, axis=0))
        both = mm(jnp.concatenate([high, low], axis=0), sign_ref[...])
        parts = halves(both[: 2 * n] + both[2 * n :])
        lane = lax.broadcasted_iota(jnp.int32, (half, 128), 1)
        for k, part in enumerate(parts):
            for c in range(4):
                for side in range(2):
                    piece = part[side * n : (side + 1) * n, c * 128 : (c + 1) * 128]
                    at = c * 256 + side * 128
                    fold_ref[k, :, at : at + 128] = piece
                    rows = (2 * k + c % 2) * n
                    w_ref[c // 2, rows : rows + n, side * 128 : (side + 1) * 128] = piece
    with jax.named_scope("grow"):
        loads["compact"].wait()
        same = lax.broadcasted_iota(jnp.int32, (16, 512), 0)
        same = jnp.where(lax.broadcasted_iota(jnp.int32, (16, 512), 1) % 16 == same, 1.0, 0.0)
        same = same.astype(jnp.bfloat16)
        for t in range(4):
            for i in range(16):
                line = jnp.broadcast_to(compact_ref[t * 16 + i : t * 16 + i + 1], (16, 512))
                grow_ref[t, i * 16 : (i + 1) * 16] = line.astype(jnp.bfloat16) * same
    with jax.named_scope("upy"):
        for p in range(2):
            both = mm(w_ref[p], grow_ref[2 * p])
            lift = both[: 2 * n] + both[2 * n :] + mm(w_ref[p, 0 : 2 * n], grow_ref[2 * p + 1])
            high, low = halves(lift)
            for q in range(2):
                for k in range(4):
                    at = (4 * p + k) * n
                    rows, lanes = slice(q * n, (q + 1) * n), slice(k * 128, (k + 1) * 128)
                    z_ref[q, at : at + n, 0:128] = high[rows, lanes]
                    z_ref[q, at : at + n, 128:256] = low[rows, lanes]
    with jax.named_scope("w_upz"):
        loads["upz"].wait()
    with jax.named_scope("upz"):
        for q in range(2):
            up = mm(z_ref[q], tile("fz%d" % q, 0, 0)) + mm(z_ref[q, :, 0:128], tile("gz%d" % q, 0, 0))
            high, low = halves(up)
            for k in range(8):
                rows, lanes = slice(k * n, (k + 1) * n), slice((8 * q + k) * 256, (8 * q + k + 1) * 256)
                x_ref[0:n, lanes] = high[rows]
                x_ref[n : 2 * n, lanes] = low[rows]
    with jax.named_scope("w_recip"):
        loads["recip"].wait()
    with jax.named_scope("upx"):
        group, place = places["sl"]
        row, rows, cols = place["left"]
        weights = vmem[group][row : row + rows, 0:cols]
        for q in range(2):
            lanes = slice(q * 2048, (q + 1) * 2048)
            spectrum = mm(
                weights, jnp.concatenate([x_ref[:, lanes], x_ref[0:n, lanes]], axis=0)
            )
            divisor = [
                vmem["recip"][(8 * q + k) * half : (8 * q + k + 1) * half] for k in range(8)
            ]
            high, low = halves(spectrum * jnp.concatenate(divisor, axis=1))
            s_ref[0:half, lanes] = high
            s_ref[half : 2 * half, lanes] = low

    def down(name, rows, b_ref, y_ref, finish):
        group, place = places[name]
        row, _, cols = place["left"]
        weights = vmem[group][row : row + rows, 0:cols]
        for q in range(2):
            lanes = slice(q * 2048, (q + 1) * 2048)
            stacked = jnp.concatenate([weights[:, 0:half], weights[:, 2 * half : 3 * half]], axis=0)
            short = mm(stacked, s_ref[0:half, lanes])
            short = short[:rows] + short[rows:] + mm(weights[:, 0:half], s_ref[half:, lanes])
            high, low = halves(short)
            for k in range(8):
                lanes = slice(k * 256, (k + 1) * 256)
                b_ref[q, k * rows : (k + 1) * rows] = high[:, lanes]
                b_ref[q, (8 + k) * rows : (9 + k) * rows] = low[:, lanes]
        for q in range(2):
            both = mm(b_ref[q], tile("bz%d" % q, 0, 0))
            block = 8 * rows
            high, low = halves(both[:block, :128] + both[block:, :128] + both[:block, 128:])
            for p in range(2):
                for k in range(4):
                    at, lanes = (4 * p + k) * rows, slice(k * 128, (k + 1) * 128)
                    y_ref[p, q * rows : (q + 1) * rows, lanes] = high[at : at + rows]
                    y_ref[p, (2 + q) * rows : (3 + q) * rows, lanes] = low[at : at + rows]
        ys = []
        finish()
        for p in range(2):
            both = mm(y_ref[p], tile("%sy%d" % ("b" if name == "means" else "c", p), 0, 0))
            both = both[: 2 * rows, :128] + both[2 * rows :, :128] + both[: 2 * rows, 128:]
            ys += [both[:rows], both[rows:]]
        return ys

    def arrive():
        loads["downy"].wait()
        loads["mine"].wait()

    with jax.named_scope("down"):
        y0, y1, y2, y3 = down("means", 16, b_ref, y_ref, arrive)
    with jax.named_scope("spread"):
        sample = jnp.concatenate(
            [jnp.where(lane[0:16] < 64, u, v) for u, v in ((y0, y1), (y2, y3))], axis=1
        )
        sample = halves(sample)
        spread = right_mul(*sample, "spread")
        bend = spread[:, modes:]
        gap = jnp.zeros((1, modes), jnp.float32)
        packet = spread[:, :modes] + 2.0 * bend
        packet = packet - jnp.concatenate([gap, bend[:-1]]) - jnp.concatenate([bend[1:], gap])
        mine = vmem["mine"]
        near_ref[n_gy + b] = packet
        rightward = jnp.sum(packet * mine[0:16], axis=0, keepdims=True)
        leftward = jnp.sum(packet * mine[16:32], axis=0, keepdims=True)
        for g in range(modes // 128):
            mom_ref[g, 0:1] = rightward[:, g * 128 : (g + 1) * 128]
            mom_ref[g, 1:2] = leftward[:, g * 128 : (g + 1) * 128]

    with jax.named_scope("barrier"):
        pl.semaphore_wait(barrier, ndev - 1)

    def remote(source, target, send, recv, device):
        return pltpu.make_async_remote_copy(
            src_ref=source,
            dst_ref=target,
            send_sem=send,
            recv_sem=recv,
            device_id=device,
            device_id_type=MESH,
        )

    def start_far(r, carry):
        d = n_gx - r
        for j in range(n_gy):
            for row, other, fine in ((0, a + d, a + d < n_gx), (1, a - d, a >= d)):

                @pl.when(fine)
                def _():
                    remote(
                        mom_ref.at[:, pl.ds(row, 1)],
                        far_ref.at[b, :, pl.ds(a, 1)],
                        f_send,
                        f_recv,
                        (other, j),
                    ).start()

        return carry

    with jax.named_scope("send"):
        lax.fori_loop(1, n_gx - 1, start_far, 0)
        for step in (0, 1, 2):
            for j in range(n_gy):
                other = a + step - 1
                fine = (other >= 0) & (other < n_gx)
                if step == 1:
                    fine = b != j

                @pl.when(fine)
                def _():
                    remote(
                        near_ref.at[n_gy + b],
                        near_ref.at[(2 - step) * n_gy + b],
                        p_send,
                        p_recv,
                        (other, j),
                    ).start()

    with jax.named_scope("w_side"):
        loads["side"].wait()
    with jax.named_scope("lin"):
        y0, y1, y2, y3 = down("picks", 32, c_ref, d_ref, lambda: None)
        flat = right_mul(*halves(left_mul("flat", *sample)), "lin")
        cx = jnp.concatenate(
            [
                jnp.where(lane[0:8] < 64, pltpu.roll(u[0:8], 64, 1), v[0:8])
                for u, v in ((y0, y1), (y2, y3))
            ],
            axis=1,
        )
        cx = cx - flat[0:8, 0:256]
        cy = jnp.where(lane[0:16] < 32, y0[16:] + y2[16:], y1[16:] + y3[16:])
        cy = cy - flat[16:32, 256:384]
        cx_ref[...] = cx
        cy_ref[...] = cy

    upper, lower = lax.rem(b + 1, n_gy), lax.rem(b + n_gy - 1, n_gy)
    with jax.named_scope("sendc"):

        @pl.when(a < n_gx - 1)
        def _():
            remote(
                cx_ref.at[pl.ds(2, 1)], rx_ref.at[pl.ds(0, 1)], p_send, p_recv, (a + 1, b)
            ).start()

        @pl.when(a > 0)
        def _():
            remote(
                cx_ref.at[pl.ds(1, 1)], rx_ref.at[pl.ds(1, 1)], p_send, p_recv, (a - 1, b)
            ).start()

        remote(cy_ref, ry_ref.at[0], p_send, p_recv, (a, upper)).start()
        remote(cy_ref, ry_ref.at[1], p_send, p_recv, (a, lower)).start()

    with jax.named_scope("near"):
        narrow = halves(left_mul("sn", fold_ref[0], fold_ref[1]))
        spectrum = []
        for c in range(4):
            at = slice(c * 256, (c + 1) * 256)
            spectrum.append(right_mul(narrow[0][:, at], narrow[1][:, at], "near%d" % c))
        spectrum = jnp.concatenate(spectrum, axis=1)

    edge = (a == 0) | (a == n_gx - 1)
    inner = jnp.logical_not(edge)

    def settle_near(sides):
        lines = 16 * (modes // 128) * ((1 + sides) * n_gy - 1) + 2 * sides + 32
        block = tally_ref.at[pl.ds(0, lines)]
        remote(block, block, p_send, p_recv, (a, b)).wait()

    with jax.named_scope("wait_p"):

        @pl.when(edge)
        def _():
            settle_near(1)

        @pl.when(inner)
        def _():
            settle_near(2)

    with jax.named_scope("face"):
        from_left = jnp.where(a > 0, rx_ref[0:1], 0.0)
        from_right = jnp.where(a < n_gx - 1, rx_ref[1:2], 0.0)
        ends = jnp.concatenate(
            [cx[0:1] + from_left, cx[3:4] + from_right, jnp.zeros((14, cx.shape[1]), jnp.float32)]
        )
        ends = right_mul(*halves(ends), "facex")
        fine = 16 * half
        column = vmem["recip"][fine + 4 * n : fine + 5 * n, 0:2]
        spectrum = spectrum + column[:, 0:1] * ends[0:1] + column[:, 1:2] * ends[1:2]
        group = jnp.where(lane[0:16] < 64, lax.rem(lane[0:16], 32) // 8, 4)
        total = jnp.where((group == 0) | (group == 3), cy, 0.0)
        total = total + jnp.where((group == 2) & (b > 0), ry_ref[0], 0.0)
        total = total + jnp.where((group == 1) & (b < n_gy - 1), ry_ref[1], 0.0)
        total = left_mul("sb", *halves(total))[:, 0:64]
        spectrum = spectrum + right_mul(*halves(total), "facey")
    with jax.named_scope("green"):
        row = lax.broadcasted_iota(jnp.int32, (8, modes), 0)

        def gathered(step):
            value = near_ref[step * n_gy]
            for j in range(1, n_gy):
                value = value + near_ref[step * n_gy + j]
            return value

        past = jnp.where(a > 0, gathered(0), 0.0)
        here = gathered(1)
        next_ = jnp.where(a < n_gx - 1, gathered(2), 0.0)
        source = jnp.concatenate(
            [
                jnp.where((row >= 4) | (a > 1), past[0:8], 0.0),
                past[8:16] + jnp.where((row >= 4) | (a > 0), here[0:8], 0.0),
                jnp.where((row < 4) | (a < n_gx - 1), here[8:16] + next_[0:8], 0.0),
                jnp.where((row < 4) | (a < n_gx - 2), next_[8:16], 0.0),
            ]
        )
        values = []
        for i in range(cells + 2):
            influence = mine[169 - i : 201 - i] - mine[208 + i : 240 + i]
            values.append(jnp.sum(influence * source, axis=0, keepdims=True))
        values.append(jnp.zeros((16 - len(values), modes), jnp.float32))
        lifted = left_mul("u12", *halves(jnp.concatenate(values, axis=0)))

    def settle_far(each):
        block = far_ref.at[:, :, pl.ds(0, each)]
        remote(block, block, f_send, f_recv, (a, b)).wait()

    with jax.named_scope("wait_f"):

        @pl.when(edge)
        def _():
            settle_far(n_gx - 2)

        @pl.when(inner)
        def _():
            settle_far(n_gx - 3)

    with jax.named_scope("final"):
        origin = lax.broadcasted_iota(jnp.int32, (n_gx, modes), 0)
        before = jnp.zeros((n_gx, modes), jnp.float32)
        after = before
        for j in range(n_gy):
            sent = jnp.concatenate([far_ref[j, g] for g in range(modes // 128)], axis=1)
            before = before + jnp.where(origin <= a - 2, sent, 0.0)
            after = after + jnp.where(origin >= a + 2, sent, 0.0)
        before = jnp.sum(before * mine[256 : 256 + n_gx], axis=0, keepdims=True)
        after = jnp.sum(after * mine[256 + n_gx : 256 + 2 * n_gx], axis=0, keepdims=True)
        lifted = lifted + mine[32:96] * before + mine[96:160] * after
        lifted = halves(jnp.concatenate([lifted[:n], lifted[n:]], axis=1))
        inverse = jnp.concatenate(
            [vmem["recip"][fine + c * n : fine + (c + 1) * n] for c in range(4)], axis=1
        )
        spectrum = (spectrum + right_mul(*lifted, "drop")) * inverse
        high, low = halves(left_mul("sn", *halves(spectrum)))
        parts = []
        for c in range(4):
            at = slice(c * 256, (c + 1) * 256)
            parts.append(right_mul(high[:, at], low[:, at], "far%d" % c))
    with jax.named_scope("unfold"):
        sides = [
            jnp.concatenate([part[:, s * 128 : (s + 1) * 128] for part in parts], axis=1)
            for s in range(2)
        ]
        high, low = halves(jnp.concatenate(sides, axis=0))
        stacked = jnp.concatenate([high, low], axis=0)
        both = mm(stacked, table("unfold", 0))
        both = both[: 2 * n] + both[2 * n :]
        for s, group in enumerate(groups):
            for i, v in enumerate(group):
                out_ref[:, v * 128 : (v + 1) * 128] = both[
                    s * n : (s + 1) * n, i * 128 : (i + 1) * 128
                ]


def emit(in_ref, out_ref, sem):
    copy = pltpu.make_async_copy(in_ref, out_ref, sem)
    copy.start()
    copy.wait()


def body(n_gx, n_gy, charge):
    singles, places = tables(n_gx, n_gy)
    arrays = [charge] + [jnp.asarray(singles[name]) for name in NAMES[1:]]
    shapes = {name: window(name, array.shape) for name, array in zip(NAMES, arrays)}
    total = sum(shapes[name][0] for name in GROUPS)
    scratch = [pltpu.VMEM(shapes[name], jnp.float32) for name in ("charge", "compact", "recip", "mine")]
    scratch.append(pltpu.VMEM((total, 256), jnp.bfloat16))
    modes = n_gy * (P_SIZE // Q) ** 2
    half = P_SIZE + 2 * W
    scratch += [
        pltpu.VMEM((512, 512), jnp.bfloat16),
        pltpu.VMEM((4, 256, 512), jnp.bfloat16),
        pltpu.VMEM((2, P_SIZE, 1024), jnp.bfloat16),
        pltpu.VMEM((2, 4 * P_SIZE, 256), jnp.bfloat16),
        pltpu.VMEM((2, 8 * P_SIZE, 256), jnp.bfloat16),
        pltpu.VMEM((2 * P_SIZE, 4096), jnp.bfloat16),
        pltpu.VMEM((2 * half, 4096), jnp.bfloat16),
        pltpu.VMEM((2, 256, 256), jnp.bfloat16),
        pltpu.VMEM((2, 64, 512), jnp.bfloat16),
        pltpu.VMEM((2, 512, 256), jnp.bfloat16),
        pltpu.VMEM((2, 128, 512), jnp.bfloat16),
        pltpu.VMEM((modes // 128, 8, 128), jnp.float32),
        pltpu.VMEM((n_gy, modes // 128, n_gx, 128), jnp.float32),
        pltpu.VMEM((3 * n_gy, 16, modes), jnp.float32),
        pltpu.VMEM((8, 256), jnp.float32),
        pltpu.VMEM((16, 128), jnp.float32),
        pltpu.VMEM((8, 256), jnp.float32),
        pltpu.VMEM((2, 16, 128), jnp.float32),
        pltpu.VMEM((16 * (modes // 128) * (3 * n_gy - 1) + 40, 128), jnp.float32),
        pltpu.SemaphoreType.DMA((len(WAITS),)),
        pltpu.SemaphoreType.DMA,
        pltpu.SemaphoreType.DMA,
        pltpu.SemaphoreType.DMA,
        pltpu.SemaphoreType.DMA,
    ]
    hbm = pl.BlockSpec(memory_space=pl.ANY)
    vm = pl.BlockSpec(memory_space=pltpu.VMEM)
    solved = pl.pallas_call(
        functools.partial(kernel, places, n_gx, n_gy),
        out_shape=pltpu.VMEM(charge.shape, charge.dtype),
        in_specs=[hbm] * len(NAMES),
        out_specs=vm,
        scratch_shapes=scratch,
        name="mlc",
        compiler_params=pltpu.CompilerParams(
            collective_id=0, has_side_effects=True, vmem_limit_bytes=60 * 1024 * 1024
        ),
    )(*arrays)
    return pl.pallas_call(
        emit,
        out_shape=jax.ShapeDtypeStruct(charge.shape, charge.dtype),
        in_specs=[vm],
        out_specs=hbm,
        scratch_shapes=[pltpu.SemaphoreType.DMA],
        name="emit",
        compiler_params=pltpu.CompilerParams(vmem_limit_bytes=1024 * 1024),
    )(solved)


def solution(mesh):
    run = functools.partial(body, mesh.shape["gx"], mesh.shape["gy"])
    spec = P("gx", "gy")
    return jax.shard_map(run, mesh=mesh, in_specs=(spec,), out_specs=spec, check_vma=False)
```

```python
import functools

import jax
import jax.numpy as jnp
import ml_dtypes
import numpy as np
from jax import lax
from jax.experimental import pallas as pl
from jax.experimental.pallas import tpu as pltpu
from jax.sharding import PartitionSpec as P

P_SIZE = 32
W = 16
Q = 4
NL = 16
CLASSES = [(0, 0), (0, 1), (1, 0), (1, 1)]
MESH = pl.DeviceIdType.MESH


def sine_table(length):
    counter = np.arange(length) + 1
    return np.sin(np.pi * np.outer(counter, counter) / (length + 1))


def eigen_values(length):
    return 2.0 - 2.0 * np.cos(np.pi * (np.arange(length) + 1) / (length + 1))


def interp_table(fine_start, fine_count, coarse_start, coarse_count, ratio):
    fine_pos = np.arange(fine_count) + fine_start
    coarse_pos = np.arange(coarse_count) + coarse_start
    numerator = 2 * fine_pos - (ratio - 1)
    lower = numerator // (2 * ratio)
    weight = ((numerator - 2 * ratio * lower) / (2 * ratio))[:, None]
    below = coarse_pos[None, :] == lower[:, None]
    above = coarse_pos[None, :] == lower[:, None] + 1
    return below * (1.0 - weight) + above * weight


def legendre_basis(length, count):
    points = (2.0 * np.arange(length) + 1.0) / length - 1.0
    columns = [np.ones_like(points), points]
    for degree in range(2, count):
        columns.append(
            ((2 * degree - 1) * points * columns[-1] - (degree - 1) * columns[-2]) / degree
        )
    result = []
    for vector in columns[:count]:
        for passes in range(2):
            for earlier in result:
                vector = vector - np.sum(earlier * vector) * earlier
        result.append(vector / np.sqrt(np.sum(vector * vector)))
    return np.stack(result, axis=1)


def fold(length):
    half = length // 2
    eye = np.eye(length)
    return np.concatenate([eye[:half] + eye[::-1][:half], eye[:half] - eye[::-1][:half]])


def split(table):
    high = table.astype(ml_dtypes.bfloat16)
    low = (table - high.astype(np.float64)).astype(ml_dtypes.bfloat16)
    return high, low


@functools.lru_cache(maxsize=None)
def tables(n_gx, n_gy):
    n, length, cells = P_SIZE, P_SIZE + 2 * W, P_SIZE // Q
    blocks, margin = length // Q, W // Q
    half, hl, hb, hn = n // 2, length // 2, blocks // 2, NL // 2
    quad, wide = hb * hb, hn * hn
    nx, ny, nz = n_gx * cells, n_gy * cells, cells
    modes = ny * nz
    s_l, s_n = sine_table(length), sine_table(n)
    u_n, u_b = fold(n), fold(blocks)
    basis = legendre_basis(n, NL)
    average = np.kron(np.eye(blocks), np.full((1, Q), 1.0 / Q))
    fine = interp_table(0, length, 0, blocks, Q)
    middle = fine[W : W + n]
    picks = [W - 1, W, W + n - 1, W + n]
    a_full = average @ s_l
    b_full = basis.T @ s_l[W : W + n]
    order = np.arange(4 * NL).reshape(4, hn, 2).transpose(2, 0, 1).ravel()
    big = {}

    folding = np.zeros((4, 4, n, 4, 2 * 4, half))
    for c, (p, q) in enumerate(CLASSES):
        for vi in range(4):
            for y4 in range(4):
                il = [y4, 4 + y4, 3 - y4, 7 - y4][vi]
                sign = -1.0 if vi > 1 and p == 1 else 1.0
                folding[vi, y4, :, c, il, :] = sign * u_n[q * half : (q + 1) * half].T
    folding = folding.reshape(4 * 128, 4 * 128)
    plain = {"unfold": folding.T}

    inner = s_l[:, W : W + n] @ u_n.T / 2
    f1 = [inner[p::2, p * half : (p + 1) * half] for p in (0, 1)]
    a1 = [(u_b @ a_full)[p * hb : (p + 1) * hb, p::2] for p in (0, 1)]
    b1 = [b_full[p::2, p::2] for p in (0, 1)]
    keep, pick = np.eye(hb), np.concatenate([np.zeros((hn, hb)), np.eye(hn)], axis=1)
    keep = np.concatenate([keep, np.zeros((hb, hn))], axis=1)
    compact = []
    for p in (0, 1):
        for part in split(np.repeat(f1[p].T, half, axis=1)):
            compact.append(part.astype(np.float32))
        high, low = split(np.kron(np.eye(8), f1[p].T))
        plain["fz%d" % p] = np.concatenate([high, high])
        plain["gz%d" % p] = low
        plain["bz%d" % p] = np.concatenate(
            split(np.kron(np.eye(8), np.concatenate([a1[p], b1[p]]).T)), axis=1
        )
        sample = np.kron(a1[p], keep).T
        slab = np.kron(s_l[picks][:, p::2], pick).T
        plain["by%d" % p] = np.concatenate(split(np.concatenate([sample, sample], axis=1)), axis=1)
        plain["cy%d" % p] = np.concatenate(
            split(np.concatenate([slab, slab, np.kron(b1[p], pick).T], axis=1)), axis=1
        )

    unfold = u_b.T / 2
    pair = np.kron(unfold, unfold).reshape(blocks * blocks, 2, hb, 2, hb)

    def from_samples(table):
        folded = np.einsum("os,spaqb->pqabo", table, pair)
        return folded.reshape(4 * quad, table.shape[0])

    bm = basis.T @ middle
    lin_x = from_samples(np.kron(bm, bm)).reshape(4 * quad, NL, NL)
    lin = np.zeros((4 * quad, 384))
    for c, (p, q) in enumerate(CLASSES):
        lin[:, c * wide : (c + 1) * wide] = lin_x[:, p::2, q::2].reshape(4 * quad, wide)
    lin[:, 256:320] = from_samples(np.kron(fine[picks], bm))[:, order]
    big["lin"] = lin
    k1 = [(s_n @ u_n.T / 2)[p::2, p * half : (p + 1) * half] for p in (0, 1)]
    for c, (p, q) in enumerate(CLASSES):
        big["near%d" % c] = np.kron(k1[p], k1[q]).T
    r1 = [(u_n @ s_n / 2)[p * half : (p + 1) * half, p::2] for p in (0, 1)]
    for c, (p, q) in enumerate(CLASSES):
        big["far%d" % c] = np.kron(r1[p], r1[q]).T

    second = 2 * np.eye(blocks) - np.eye(blocks, k=1) - np.eye(blocks, k=-1)
    s_y, s_z = sine_table(ny), sine_table(nz)
    proj_z = np.zeros((nz, blocks))
    proj_z[:, margin : margin + cells] = s_z
    edge = interp_table(-1, n + 2, -1, cells + 2, Q)
    depth = interp_table(0, n, 0, cells, Q)
    lateral = edge[1 : n + 1]
    s_ext = np.zeros((ny + 2, ny))
    s_ext[1:-1] = s_y
    sp = np.concatenate([s_n[0::2], s_n[1::2]])
    deep = sp @ depth @ s_z

    def by_class(first, second_table):
        parts = []
        for p, q in CLASSES:
            parts.append(
                np.kron(first[p * half : (p + 1) * half], second_table[q * half : (q + 1) * half])
            )
        return np.concatenate(parts).T

    factor = (2.0 / (ny + 1)) * (2.0 / (nz + 1))
    spread, drop = [], []
    for b in range(n_gy):
        proj_y = np.zeros((ny, blocks))
        for j in range(blocks):
            at = j + b * cells - margin
            if 0 <= at < ny:
                proj_y[:, j] = s_y[:, at]
        flat = np.kron(proj_y, proj_z)
        curved = np.kron(proj_y @ second, proj_z) + np.kron(proj_y, proj_z @ second)
        spread.append(
            factor * np.concatenate([from_samples(curved), from_samples(flat)], axis=1)
        )
        local_s = s_ext[b * cells : b * cells + cells + 2]
        rim = np.outer(sp[:, 0], edge[0] @ local_s) + np.outer(sp[:, n - 1], edge[n + 1] @ local_s)
        drop.append(
            np.concatenate([by_class(sp @ lateral @ local_s, deep), by_class(rim, deep)])
        )
    big["spread"] = np.stack(spread)
    big["drop"] = np.stack(drop)
    sb = s_n @ basis
    sbp = np.concatenate([sb[0::2], sb[1::2]])
    facex = np.zeros((4 * wide, n * n))
    for c, (p, q) in enumerate(CLASSES):
        facex[c * wide : (c + 1) * wide, c * 256 : c * 256 + 256] = np.kron(
            sb[p::2, p::2], sb[q::2, q::2]
        ).T
    big["facex"] = facex
    ends = np.stack([sp[:, 0], sp[:, n - 1], sp[:, 0], sp[:, n - 1]], axis=1)
    big["facey"] = by_class(ends, sbp)[order]

    mu_y, mu_z = eigen_values(ny), eigen_values(nz)
    theta = np.arccosh(1.0 + (mu_y[:, None] + mu_z[None, :]).reshape(1, modes) / 2)
    below = 2 * np.sinh(theta) * (1.0 - np.exp(-2 * theta * (nx + 1)))
    apart = np.abs(np.arange(48) - 20)[:, None]
    toep = (np.exp(-theta * apart) + np.exp(-theta * np.maximum(2 * (nx + 1) - apart, 0))) / below
    total = (np.arange(2 * nx + 32) - 13)[:, None]
    hank = np.exp(-theta * np.maximum(total + 2, 0)) + np.exp(-theta * np.maximum(2 * nx - total, 0))
    hank = hank / below

    u12 = np.zeros((64, 16))
    u12[:32, :10] = np.outer(s_n[:, 0], edge[0]) + np.outer(s_n[:, n - 1], edge[n + 1])
    u12[32:, :10] = s_n @ lateral
    place = np.arange(n_gx)
    mine = []
    for a in range(n_gx):
        rank = np.arange(16)[:, None]
        at = cells * a - margin + rank
        inside = (at >= 0) & (at < nx)
        rightward = inside * np.exp(-theta * (15 - rank)) * (1 - np.exp(-2 * theta * (at + 1) * inside))
        leftward = inside * np.exp(-theta * rank) * (1 - np.exp(-2 * theta * (nx - at) * inside))
        row = np.arange(16)[:, None]
        x = cells * a - 1 + row
        used = row < cells + 2
        falling = used * np.exp(-theta * row) * (1 - np.exp(-2 * theta * np.maximum(nx - x, 0))) / below
        rising = (
            used
            * np.exp(-theta * np.maximum(cells + 1 - row, 0))
            * (1 - np.exp(-2 * theta * (x + 1)))
            / below
        )
        away = (a - place)[:, None]
        before = (away >= 2) * np.exp(-theta * np.maximum(cells * away - 12, 0))
        after = (away <= -2) * np.exp(-theta * np.maximum(-cells * away - 12, 0))
        mine.append(
            np.concatenate(
                [
                    rightward,
                    leftward,
                    u12 @ falling,
                    u12 @ rising,
                    toep,
                    hank[2 * cells * a : 2 * cells * a + 48],
                    before,
                    after,
                ]
            )
        )
    mu_l, mu_n = eigen_values(length), eigen_values(n)
    reciprocal = []
    for q in (0, 1):
        for p in (0, 1):
            pair_sum = (mu_l[p::2][:, None] + mu_l[q::2][None, :]).reshape(1, hl * hl)
            table = 1.0 / (mu_l[:, None] + pair_sum)
            reciprocal.append(table.reshape(length, 4, 256).transpose(1, 0, 2).reshape(-1, 256))
    for p, q in CLASSES:
        pair_sum = (mu_n[p::2][:, None] + mu_n[q::2][None, :]).reshape(1, 256)
        reciprocal.append((2.0 / (n + 1)) ** 3 / (mu_n[:, None] + pair_sum))
    ends = np.zeros((n, 256))
    ends[:, :2] = s_n[:, [0, n - 1]]
    reciprocal.append(ends)

    scale = (2.0 / (length + 1)) ** 3
    blank = np.zeros((12, length))
    lefts = {
        "sl": s_l[:, W : W + n],
        "means": a_full * scale,
        "flat": np.concatenate([fine[picks], blank[:, :blocks], bm]),
        "picks": np.concatenate([s_l[picks], blank, b_full]) * scale,
        "sn": s_n,
        "u12": u12,
        "sb": sb,
    }
    for name, value in lefts.items():
        high, low = split(value)
        plain[name] = np.concatenate([high, high, low], axis=1)
    singles = {
        "mine": np.stack(mine).astype(np.float32),
        "recip": np.concatenate(reciprocal).astype(np.float32),
        "compact": np.concatenate(compact),
    }
    places = {}
    for group, names in GROUPS.items():
        packs, row = [], 0
        for name in names:
            if name in plain:
                parts = [plain[name].astype(ml_dtypes.bfloat16)]
            else:
                parts = split(big[name])
            depth, width = parts[0].shape[-2:]
            place = {"left": (row, depth, width)}
            step = 256
            tiles = []
            for part in parts:
                for at in range(0, width, step):
                    tile = np.zeros(part.shape[:-1] + (256,), ml_dtypes.bfloat16)
                    piece = part[..., at : at + step]
                    tile[..., : piece.shape[-1]] = piece
                    packs.append(tile)
                    tiles.append((row, depth))
                    row += depth
            count = len(tiles) // len(parts)
            place["tiles"] = [tiles[k * count : (k + 1) * count] for k in range(len(parts))]
            places[name] = (group, place)
        most = max(tile.ndim for tile in packs)
        if most == 3:
            packs = [np.broadcast_to(tile, (n_gy,) + tile.shape[-2:]) for tile in packs]
        singles[group] = np.concatenate(packs, axis=-2)
    return singles, places


GROUPS = {
    "upz": ["fz0", "gz0", "fz1", "gz1", "sl", "means", "bz0", "bz1"],
    "downy": ["by0", "by1"],
    "spread": ["spread"],
    "side": ["picks", "flat", "sn", "sb", "u12", "lin", "cy0", "cy1"]
    + ["near%d" % c for c in range(4)]
    + ["facex", "facey"],
    "drop": ["drop"],
    "last": ["far%d" % c for c in range(4)] + ["unfold"],
}
NAMES = [
    "charge", "compact", "upz", "recip", "downy", "spread", "mine", "side", "drop", "last",
]
WAITS = [
    ["charge"], ["compact"], ["upz"], ["recip"], ["downy", "spread"], ["mine"],
    ["side", "drop", "last"],
]
CUTS = {"charge": 4, "compact": 4}


def halves(value):
    high = value.astype(jnp.bfloat16)
    return high, (value - high.astype(jnp.float32)).astype(jnp.bfloat16)


def mm(left, right):
    return jnp.dot(left, right, preferred_element_type=jnp.float32)


def window(name, shape):
    return shape[1:] if name in ("spread", "drop", "mine") else shape


def kernel(places, n_gx, n_gy, *refs):
    count = len(NAMES)
    hbm = dict(zip(NAMES, refs[:count]))
    out_ref = refs[count]
    charge_ref, compact_ref, recip_ref, mine_ref, tables_ref = refs[count + 1 : count + 6]
    vmem = {"charge": charge_ref, "compact": compact_ref, "recip": recip_ref, "mine": mine_ref}
    (
        sign_ref, grow_ref, sample_ref, spec_ref, fold_ref, w_ref, z_ref, x_ref, s_ref, b_ref, y_ref, c_ref, d_ref,
        mom_ref, far_ref, near_ref, cx_ref, cy_ref, rx_ref, ry_ref, tally_ref,
        load_sem, f_send, f_recv, p_send, p_recv,
    ) = refs[count + 6 :]
    ndev = n_gx * n_gy
    a = lax.axis_index("gx")
    b = lax.axis_index("gy")
    me = a * n_gy + b
    n, cells = P_SIZE, P_SIZE // Q
    half = n + 2 * W
    modes = near_ref.shape[-1]

    loads, base = {}, 0
    for i, names in enumerate(WAITS):
        start = base
        for name in names:
            source = hbm[name]
            if name in ("spread", "drop"):
                source = source.at[b]
            if name == "mine":
                source = source.at[a]
            if name in GROUPS:
                rows = source.shape[0]
                vmem[name] = tables_ref.at[pl.ds(base, rows)]
                base += rows
            cuts = CUTS.get(name, 1)
            each = source.shape[0] // cuts
            for k in range(cuts):
                part = pl.ds(k * each, each)
                pltpu.make_async_copy(
                    source.at[part], vmem[name].at[part], load_sem.at[i]
                ).start()
        target = tables_ref.at[pl.ds(start, base - start)] if base > start else vmem[names[0]]
        loads[names[0]] = pltpu.make_async_copy(target, target, load_sem.at[i])

    barrier = pltpu.get_barrier_semaphore()

    def greet(r, carry):
        peer = lax.rem(me + r, ndev)
        pl.semaphore_signal(
            barrier, inc=1, device_id=(peer // n_gy, lax.rem(peer, n_gy)), device_id_type=MESH
        )
        return carry

    with jax.named_scope("greet"):
        lax.fori_loop(1, ndev, greet, 0)

    def tile(name, part, i):
        group, place = places[name]
        row, depth = place["tiles"][part][i]
        return vmem[group][row : row + depth, :]

    def table(name, part):
        count = len(places[name][1]["tiles"][part])
        return jnp.concatenate([tile(name, part, i) for i in range(count)], axis=1)

    def right_mul(high, low, name):
        rows = high.shape[0]
        both = mm(jnp.concatenate([high, low], axis=0), table(name, 0))
        return both[:rows] + both[rows:] + mm(high, table(name, 1))

    def left_mul(name, high, low):
        group, place = places[name]
        row, rows, cols = place["left"]
        return mm(vmem[group][row : row + rows, 0:cols], jnp.concatenate([high, low, high], axis=0))

    groups = [[0, 1, 7, 6], [2, 3, 5, 4]]
    with jax.named_scope("signs"):
        z = lax.broadcasted_iota(jnp.int32, (n, 512), 0)
        at = lax.broadcasted_iota(jnp.int32, (n, 512), 1)
        odd = jnp.where((at // 128) % 2 == 1, -1.0, 1.0)
        base = jnp.where(z == at % 16, 1.0, 0.0) + jnp.where(z == 31 - at % 16, odd, 0.0)
        turned = jnp.where(at >= 256, -base, base)
        spot = (at // 16) % 8
        for side, value in ((0, base), (1, turned)):
            for y in range(8):
                rows = (side * 8 + y) * n
                match = spot == ((3 - y) % 8 if side else y)
                sign_ref[rows : rows + n] = jnp.where(match, value, 0.0).astype(jnp.bfloat16)

    with jax.named_scope("w_charge"):
        loads["charge"].wait()
    with jax.named_scope("fold"):
        charge = vmem["charge"]
        sides = [
            jnp.concatenate([charge[:, v * 128 : (v + 1) * 128] for v in group], axis=1)
            for group in groups
        ]
        high, low = halves(jnp.concatenate(sides, axis=0))
        both = mm(jnp.concatenate([high, low], axis=0), sign_ref[...])
        parts = halves(both[: 2 * n] + both[2 * n :])
        lane = lax.broadcasted_iota(jnp.int32, (half, 128), 1)
        for k, part in enumerate(parts):
            for c in range(4):
                for side in range(2):
                    piece = part[side * n : (side + 1) * n, c * 128 : (c + 1) * 128]
                    at = c * 256 + side * 128
                    fold_ref[k, :, at : at + 128] = piece
                    rows = (2 * k + c % 2) * n
                    w_ref[c // 2, rows : rows + n, side * 128 : (side + 1) * 128] = piece
    with jax.named_scope("grow"):
        loads["compact"].wait()
        same = lax.broadcasted_iota(jnp.int32, (16, 512), 0)
        same = jnp.where(lax.broadcasted_iota(jnp.int32, (16, 512), 1) % 16 == same, 1.0, 0.0)
        same = same.astype(jnp.bfloat16)
        for t in range(4):
            for i in range(16):
                line = jnp.broadcast_to(compact_ref[t * 16 + i : t * 16 + i + 1], (16, 512))
                grow_ref[t, i * 16 : (i + 1) * 16] = line.astype(jnp.bfloat16) * same
    with jax.named_scope("upy"):
        for p in range(2):
            both = mm(w_ref[p], grow_ref[2 * p])
            lift = both[: 2 * n] + both[2 * n :] + mm(w_ref[p, 0 : 2 * n], grow_ref[2 * p + 1])
            high, low = halves(lift)
            for q in range(2):
                for k in range(4):
                    at = (4 * p + k) * n
                    rows, lanes = slice(q * n, (q + 1) * n), slice(k * 128, (k + 1) * 128)
                    z_ref[q, at : at + n, 0:128] = high[rows, lanes]
                    z_ref[q, at : at + n, 128:256] = low[rows, lanes]
    with jax.named_scope("w_upz"):
        loads["upz"].wait()
    with jax.named_scope("upz"):
        for q in range(2):
            up = mm(z_ref[q], tile("fz%d" % q, 0, 0)) + mm(z_ref[q, :, 0:128], tile("gz%d" % q, 0, 0))
            high, low = halves(up)
            for k in range(8):
                rows, lanes = slice(k * n, (k + 1) * n), slice((8 * q + k) * 256, (8 * q + k + 1) * 256)
                x_ref[0:n, lanes] = high[rows]
                x_ref[n : 2 * n, lanes] = low[rows]
    with jax.named_scope("w_recip"):
        loads["recip"].wait()
    with jax.named_scope("upx"):
        group, place = places["sl"]
        row, rows, cols = place["left"]
        weights = vmem[group][row : row + rows, 0:cols]
        for q in range(2):
            lanes = slice(q * 2048, (q + 1) * 2048)
            spectrum = mm(
                weights, jnp.concatenate([x_ref[:, lanes], x_ref[0:n, lanes]], axis=0)
            )
            divisor = [
                vmem["recip"][(8 * q + k) * half : (8 * q + k + 1) * half] for k in range(8)
            ]
            high, low = halves(spectrum * jnp.concatenate(divisor, axis=1))
            s_ref[0:half, lanes] = high
            s_ref[half : 2 * half, lanes] = low

    def down(name, rows, b_ref, y_ref, finish):
        group, place = places[name]
        row, _, cols = place["left"]
        weights = vmem[group][row : row + rows, 0:cols]
        for q in range(2):
            lanes = slice(q * 2048, (q + 1) * 2048)
            stacked = jnp.concatenate([weights[:, 0:half], weights[:, 2 * half : 3 * half]], axis=0)
            short = mm(stacked, s_ref[0:half, lanes])
            short = short[:rows] + short[rows:] + mm(weights[:, 0:half], s_ref[half:, lanes])
            high, low = halves(short)
            for k in range(8):
                lanes = slice(k * 256, (k + 1) * 256)
                b_ref[q, k * rows : (k + 1) * rows] = high[:, lanes]
                b_ref[q, (8 + k) * rows : (9 + k) * rows] = low[:, lanes]
        for q in range(2):
            both = mm(b_ref[q], tile("bz%d" % q, 0, 0))
            block = 8 * rows
            high, low = halves(both[:block, :128] + both[block:, :128] + both[:block, 128:])
            for p in range(2):
                for k in range(4):
                    at, lanes = (4 * p + k) * rows, slice(k * 128, (k + 1) * 128)
                    y_ref[p, q * rows : (q + 1) * rows, lanes] = high[at : at + rows]
                    y_ref[p, (2 + q) * rows : (3 + q) * rows, lanes] = low[at : at + rows]
        ys = []
        finish()
        for p in range(2):
            both = mm(y_ref[p], tile("%sy%d" % ("b" if name == "means" else "c", p), 0, 0))
            both = both[: 2 * rows, :128] + both[2 * rows :, :128] + both[: 2 * rows, 128:]
            ys += [both[:rows], both[rows:]]
        return ys

    def arrive():
        loads["downy"].wait()
        loads["mine"].wait()

    with jax.named_scope("down"):
        y0, y1, y2, y3 = down("means", 16, b_ref, y_ref, arrive)
    with jax.named_scope("spread"):
        sample = jnp.concatenate(
            [jnp.where(lane[0:16] < 64, u, v) for u, v in ((y0, y1), (y2, y3))], axis=1
        )
        sample = halves(sample)
        sample_ref[0] = sample[0]
        sample_ref[1] = sample[1]
        spread = right_mul(*sample, "spread")
        bend = spread[:, modes:]
        gap = jnp.zeros((1, modes), jnp.float32)
        packet = spread[:, :modes] + 2.0 * bend
        packet = packet - jnp.concatenate([gap, bend[:-1]]) - jnp.concatenate([bend[1:], gap])
        mine = vmem["mine"]
        near_ref[n_gy + b] = packet
        rightward = jnp.sum(packet * mine[0:16], axis=0, keepdims=True)
        leftward = jnp.sum(packet * mine[16:32], axis=0, keepdims=True)
        for g in range(modes // 128):
            mom_ref[g, 0:1] = rightward[:, g * 128 : (g + 1) * 128]
            mom_ref[g, 1:2] = leftward[:, g * 128 : (g + 1) * 128]

    def remote(source, target, send, recv, device):
        return pltpu.make_async_remote_copy(
            src_ref=source,
            dst_ref=target,
            send_sem=send,
            recv_sem=recv,
            device_id=device,
            device_id_type=MESH,
        )

    def start_far(r, carry):
        d = n_gx - r
        for j in range(n_gy):
            for row, other, fine in ((0, a + d, a + d < n_gx), (1, a - d, a >= d)):

                @pl.when(fine)
                def _():
                    remote(
                        mom_ref.at[:, pl.ds(row, 1)],
                        far_ref.at[b, :, pl.ds(a, 1)],
                        f_send,
                        f_recv,
                        (other, j),
                    ).start()

        return carry

    early = a < n_gx // 4

    def send_far():
        with jax.named_scope("sendf"):
            lax.fori_loop(1, n_gx - 1, start_far, 0)

    def send_near():
        with jax.named_scope("send"):
            for step in (0, 1, 2):
                for j in range(n_gy):
                    other = a + step - 1
                    fine = (other >= 0) & (other < n_gx)
                    if step == 1:
                        fine = b != j

                    @pl.when(fine)
                    def _():
                        remote(
                            near_ref.at[n_gy + b],
                            near_ref.at[(2 - step) * n_gy + b],
                            p_send,
                            p_recv,
                            (other, j),
                        ).start()

    upper, lower = lax.rem(b + 1, n_gy), lax.rem(b + n_gy - 1, n_gy)
    def send_faces():
        with jax.named_scope("sendc"):

            @pl.when(a < n_gx - 1)
            def _():
                remote(
                    cx_ref.at[pl.ds(2, 1)], rx_ref.at[pl.ds(0, 1)], p_send, p_recv, (a + 1, b)
                ).start()

            @pl.when(a > 0)
            def _():
                remote(
                    cx_ref.at[pl.ds(1, 1)], rx_ref.at[pl.ds(1, 1)], p_send, p_recv, (a - 1, b)
                ).start()

            remote(cy_ref, ry_ref.at[0], p_send, p_recv, (a, upper)).start()
            remote(cy_ref, ry_ref.at[1], p_send, p_recv, (a, lower)).start()

    def turn(step, carry):
        @pl.when(step == last)
        def _():
            with jax.named_scope("barrier"):
                pl.semaphore_wait(barrier, ndev - 1)

            @pl.when(early)
            def _():
                send_faces()
                send_near()
                send_far()

            @pl.when(jnp.logical_not(early))
            def _():
                send_far()
                send_near()

        @pl.when(step != last)
        def _():
            with jax.named_scope("w_side"):
                loads["side"].wait()
            with jax.named_scope("lin"):
                y0, y1, y2, y3 = down("picks", 32, c_ref, d_ref, lambda: None)
                flat = right_mul(*halves(left_mul("flat", sample_ref[0], sample_ref[1])), "lin")
                cx = jnp.concatenate(
                    [
                        jnp.where(lane[0:8] < 64, pltpu.roll(u[0:8], 64, 1), v[0:8])
                        for u, v in ((y0, y1), (y2, y3))
                    ],
                    axis=1,
                )
                cx = cx - flat[0:8, 0:256]
                cy = jnp.where(lane[0:16] < 32, y0[16:] + y2[16:], y1[16:] + y3[16:])
                cy = cy - flat[16:32, 256:384]
                cx_ref[...] = cx
                cy_ref[...] = cy

            with jax.named_scope("near"):
                narrow = halves(left_mul("sn", fold_ref[0], fold_ref[1]))
                spectrum = []
                for c in range(4):
                    at = slice(c * 256, (c + 1) * 256)
                    spectrum.append(right_mul(narrow[0][:, at], narrow[1][:, at], "near%d" % c))
                spec_ref[...] = jnp.concatenate(spectrum, axis=1)

        return carry

    last = jnp.where(early, 1, 0)
    lax.fori_loop(0, 2, turn, 0)

    @pl.when(jnp.logical_not(early))
    def _():
        send_faces()

    edge = (a == 0) | (a == n_gx - 1)
    inner = jnp.logical_not(edge)

    def settle_near(sides):
        lines = 16 * (modes // 128) * ((1 + sides) * n_gy - 1) + 2 * sides + 32
        block = tally_ref.at[pl.ds(0, lines)]
        remote(block, block, p_send, p_recv, (a, b)).wait()

    with jax.named_scope("wait_p"):

        @pl.when(edge)
        def _():
            settle_near(1)

        @pl.when(inner)
        def _():
            settle_near(2)

    with jax.named_scope("face"):
        cx, cy, spectrum = cx_ref[...], cy_ref[...], spec_ref[...]
        from_left = jnp.where(a > 0, rx_ref[0:1], 0.0)
        from_right = jnp.where(a < n_gx - 1, rx_ref[1:2], 0.0)
        ends = jnp.concatenate(
            [cx[0:1] + from_left, cx[3:4] + from_right, jnp.zeros((14, cx.shape[1]), jnp.float32)]
        )
        ends = right_mul(*halves(ends), "facex")
        fine = 16 * half
        column = vmem["recip"][fine + 4 * n : fine + 5 * n, 0:2]
        spectrum = spectrum + column[:, 0:1] * ends[0:1] + column[:, 1:2] * ends[1:2]
        group = jnp.where(lane[0:16] < 64, lax.rem(lane[0:16], 32) // 8, 4)
        total = jnp.where((group == 0) | (group == 3), cy, 0.0)
        total = total + jnp.where((group == 2) & (b > 0), ry_ref[0], 0.0)
        total = total + jnp.where((group == 1) & (b < n_gy - 1), ry_ref[1], 0.0)
        total = left_mul("sb", *halves(total))[:, 0:64]
        spectrum = spectrum + right_mul(*halves(total), "facey")
    with jax.named_scope("green"):
        row = lax.broadcasted_iota(jnp.int32, (8, modes), 0)

        def gathered(step):
            value = near_ref[step * n_gy]
            for j in range(1, n_gy):
                value = value + near_ref[step * n_gy + j]
            return value

        past = jnp.where(a > 0, gathered(0), 0.0)
        here = gathered(1)
        next_ = jnp.where(a < n_gx - 1, gathered(2), 0.0)
        source = jnp.concatenate(
            [
                jnp.where((row >= 4) | (a > 1), past[0:8], 0.0),
                past[8:16] + jnp.where((row >= 4) | (a > 0), here[0:8], 0.0),
                jnp.where((row < 4) | (a < n_gx - 1), here[8:16] + next_[0:8], 0.0),
                jnp.where((row < 4) | (a < n_gx - 2), next_[8:16], 0.0),
            ]
        )
        values = []
        for i in range(cells + 2):
            influence = mine[169 - i : 201 - i] - mine[208 + i : 240 + i]
            values.append(jnp.sum(influence * source, axis=0, keepdims=True))
        values.append(jnp.zeros((16 - len(values), modes), jnp.float32))
        lifted = left_mul("u12", *halves(jnp.concatenate(values, axis=0)))

    inverse = jnp.concatenate(
        [vmem["recip"][fine + c * n : fine + (c + 1) * n] for c in range(4)], axis=1
    )

    def unfolded(parts):
        sides = [
            jnp.concatenate([part[:, s * 128 : (s + 1) * 128] for part in parts], axis=1)
            for s in range(2)
        ]
        return jnp.concatenate(sides, axis=0)

    def cells_of(both):
        for s, group in enumerate(groups):
            for i, v in enumerate(group):
                yield v, both[s * n : (s + 1) * n, i * 128 : (i + 1) * 128]

    with jax.named_scope("base"):
        lifted = halves(jnp.concatenate([lifted[:n], lifted[n:]], axis=1))
        spectrum = (spectrum + right_mul(*lifted, "drop")) * inverse
        high, low = halves(left_mul("sn", *halves(spectrum)))
        parts = []
        for c in range(4):
            at = slice(c * 256, (c + 1) * 256)
            parts.append(right_mul(high[:, at], low[:, at], "far%d" % c))
        high, low = halves(unfolded(parts))
        both = mm(jnp.concatenate([high, low], axis=0), table("unfold", 0))
        for v, value in cells_of(both[: 2 * n] + both[2 * n :]):
            out_ref[:, v * 128 : (v + 1) * 128] = value

    def settle_far(each):
        block = far_ref.at[:, :, pl.ds(0, each)]
        remote(block, block, f_send, f_recv, (a, b)).wait()

    with jax.named_scope("wait_f"):

        @pl.when(edge)
        def _():
            settle_far(n_gx - 2)

        @pl.when(inner)
        def _():
            settle_far(n_gx - 3)

    with jax.named_scope("final"):
        origin = lax.broadcasted_iota(jnp.int32, (n_gx, modes), 0)
        before = jnp.zeros((n_gx, modes), jnp.float32)
        after = before
        for j in range(n_gy):
            sent = jnp.concatenate([far_ref[j, g] for g in range(modes // 128)], axis=1)
            before = before + jnp.where(origin <= a - 2, sent, 0.0)
            after = after + jnp.where(origin >= a + 2, sent, 0.0)
        before = jnp.sum(before * mine[256 : 256 + n_gx], axis=0, keepdims=True)
        after = jnp.sum(after * mine[256 + n_gx : 256 + 2 * n_gx], axis=0, keepdims=True)
        lifted = mine[32:96] * before + mine[96:160] * after
        lifted = jnp.concatenate([lifted[:n], lifted[n:]], axis=1).astype(jnp.bfloat16)
        spectrum = (mm(lifted, table("drop", 0)) * inverse).astype(jnp.bfloat16)
        group, place = places["sn"]
        row, rows, _ = place["left"]
        spectrum = mm(vmem[group][row : row + rows, 0:n], spectrum).astype(jnp.bfloat16)
        parts = [mm(spectrum[:, c * 256 : (c + 1) * 256], tile("far%d" % c, 0, 0)) for c in range(4)]
    with jax.named_scope("unfold"):
        both = mm(unfolded(parts).astype(jnp.bfloat16), table("unfold", 0))
        for v, value in cells_of(both):
            at = slice(v * 128, (v + 1) * 128)
            out_ref[:, at] = out_ref[:, at] + value


def emit(in_ref, out_ref, sem):
    copy = pltpu.make_async_copy(in_ref, out_ref, sem)
    copy.start()
    copy.wait()


def body(n_gx, n_gy, charge):
    singles, places = tables(n_gx, n_gy)
    arrays = [charge] + [jnp.asarray(singles[name]) for name in NAMES[1:]]
    shapes = {name: window(name, array.shape) for name, array in zip(NAMES, arrays)}
    total = sum(shapes[name][0] for name in GROUPS)
    scratch = [pltpu.VMEM(shapes[name], jnp.float32) for name in ("charge", "compact", "recip", "mine")]
    scratch.append(pltpu.VMEM((total, 256), jnp.bfloat16))
    modes = n_gy * (P_SIZE // Q) ** 2
    half = P_SIZE + 2 * W
    scratch += [
        pltpu.VMEM((512, 512), jnp.bfloat16),
        pltpu.VMEM((4, 256, 512), jnp.bfloat16),
        pltpu.VMEM((2, 16, 256), jnp.bfloat16),
        pltpu.VMEM((P_SIZE, 1024), jnp.float32),
        pltpu.VMEM((2, P_SIZE, 1024), jnp.bfloat16),
        pltpu.VMEM((2, 4 * P_SIZE, 256), jnp.bfloat16),
        pltpu.VMEM((2, 8 * P_SIZE, 256), jnp.bfloat16),
        pltpu.VMEM((2 * P_SIZE, 4096), jnp.bfloat16),
        pltpu.VMEM((2 * half, 4096), jnp.bfloat16),
        pltpu.VMEM((2, 256, 256), jnp.bfloat16),
        pltpu.VMEM((2, 64, 512), jnp.bfloat16),
        pltpu.VMEM((2, 512, 256), jnp.bfloat16),
        pltpu.VMEM((2, 128, 512), jnp.bfloat16),
        pltpu.VMEM((modes // 128, 8, 128), jnp.float32),
        pltpu.VMEM((n_gy, modes // 128, n_gx, 128), jnp.float32),
        pltpu.VMEM((3 * n_gy, 16, modes), jnp.float32),
        pltpu.VMEM((8, 256), jnp.float32),
        pltpu.VMEM((16, 128), jnp.float32),
        pltpu.VMEM((8, 256), jnp.float32),
        pltpu.VMEM((2, 16, 128), jnp.float32),
        pltpu.VMEM((16 * (modes // 128) * (3 * n_gy - 1) + 40, 128), jnp.float32),
        pltpu.SemaphoreType.DMA((len(WAITS),)),
        pltpu.SemaphoreType.DMA,
        pltpu.SemaphoreType.DMA,
        pltpu.SemaphoreType.DMA,
        pltpu.SemaphoreType.DMA,
    ]
    hbm = pl.BlockSpec(memory_space=pl.ANY)
    vm = pl.BlockSpec(memory_space=pltpu.VMEM)
    solved = pl.pallas_call(
        functools.partial(kernel, places, n_gx, n_gy),
        out_shape=pltpu.VMEM(charge.shape, charge.dtype),
        in_specs=[hbm] * len(NAMES),
        out_specs=vm,
        scratch_shapes=scratch,
        name="mlc",
        compiler_params=pltpu.CompilerParams(
            collective_id=0, has_side_effects=True, vmem_limit_bytes=60 * 1024 * 1024
        ),
    )(*arrays)
    return pl.pallas_call(
        emit,
        out_shape=jax.ShapeDtypeStruct(charge.shape, charge.dtype),
        in_specs=[vm],
        out_specs=hbm,
        scratch_shapes=[pltpu.SemaphoreType.DMA],
        name="emit",
        compiler_params=pltpu.CompilerParams(vmem_limit_bytes=1024 * 1024),
    )(solved)


def solution(mesh):
    run = functools.partial(body, mesh.shape["gx"], mesh.shape["gy"])
    spec = P("gx", "gy")
    return jax.shard_map(run, mesh=mesh, in_specs=(spec,), out_specs=spec, check_vma=False)
```

```python
import functools

import jax
import jax.numpy as jnp
import ml_dtypes
import numpy as np
from jax import lax
from jax.experimental import pallas as pl
from jax.experimental.pallas import tpu as pltpu
from jax.sharding import PartitionSpec as P

P_SIZE = 32
W = 16
Q = 4
NL = 16
CLASSES = [(0, 0), (0, 1), (1, 0), (1, 1)]
MESH = pl.DeviceIdType.MESH


def sine_table(length):
    counter = np.arange(length) + 1
    return np.sin(np.pi * np.outer(counter, counter) / (length + 1))


def eigen_values(length):
    return 2.0 - 2.0 * np.cos(np.pi * (np.arange(length) + 1) / (length + 1))


def interp_table(fine_start, fine_count, coarse_start, coarse_count, ratio):
    fine_pos = np.arange(fine_count) + fine_start
    coarse_pos = np.arange(coarse_count) + coarse_start
    numerator = 2 * fine_pos - (ratio - 1)
    lower = numerator // (2 * ratio)
    weight = ((numerator - 2 * ratio * lower) / (2 * ratio))[:, None]
    below = coarse_pos[None, :] == lower[:, None]
    above = coarse_pos[None, :] == lower[:, None] + 1
    return below * (1.0 - weight) + above * weight


def legendre_basis(length, count):
    points = (2.0 * np.arange(length) + 1.0) / length - 1.0
    columns = [np.ones_like(points), points]
    for degree in range(2, count):
        columns.append(
            ((2 * degree - 1) * points * columns[-1] - (degree - 1) * columns[-2]) / degree
        )
    result = []
    for vector in columns[:count]:
        for passes in range(2):
            for earlier in result:
                vector = vector - np.sum(earlier * vector) * earlier
        result.append(vector / np.sqrt(np.sum(vector * vector)))
    return np.stack(result, axis=1)


def fold(length):
    half = length // 2
    eye = np.eye(length)
    return np.concatenate([eye[:half] + eye[::-1][:half], eye[:half] - eye[::-1][:half]])


def split(table):
    high = table.astype(ml_dtypes.bfloat16)
    low = (table - high.astype(np.float64)).astype(ml_dtypes.bfloat16)
    return high, low


@functools.lru_cache(maxsize=None)
def tables(n_gx, n_gy):
    n, length, cells = P_SIZE, P_SIZE + 2 * W, P_SIZE // Q
    blocks, margin = length // Q, W // Q
    half, hl, hb, hn = n // 2, length // 2, blocks // 2, NL // 2
    quad, wide = hb * hb, hn * hn
    nx, ny, nz = n_gx * cells, n_gy * cells, cells
    modes = ny * nz
    s_l, s_n = sine_table(length), sine_table(n)
    u_n, u_b = fold(n), fold(blocks)
    basis = legendre_basis(n, NL)
    average = np.kron(np.eye(blocks), np.full((1, Q), 1.0 / Q))
    fine = interp_table(0, length, 0, blocks, Q)
    middle = fine[W : W + n]
    picks = [W - 1, W, W + n - 1, W + n]
    a_full = average @ s_l
    b_full = basis.T @ s_l[W : W + n]
    order = np.arange(4 * NL).reshape(4, hn, 2).transpose(2, 0, 1).ravel()
    big = {}

    folding = np.zeros((4, 4, n, 4, 2 * 4, half))
    for c, (p, q) in enumerate(CLASSES):
        for vi in range(4):
            for y4 in range(4):
                il = [y4, 4 + y4, 3 - y4, 7 - y4][vi]
                sign = -1.0 if vi > 1 and p == 1 else 1.0
                folding[vi, y4, :, c, il, :] = sign * u_n[q * half : (q + 1) * half].T
    folding = folding.reshape(4 * 128, 4 * 128)
    plain = {"unfold": folding.T}

    inner = s_l[:, W : W + n] @ u_n.T / 2
    f1 = [inner[p::2, p * half : (p + 1) * half] for p in (0, 1)]
    a1 = [(u_b @ a_full)[p * hb : (p + 1) * hb, p::2] for p in (0, 1)]
    b1 = [b_full[p::2, p::2] for p in (0, 1)]
    keep, pick = np.eye(hb), np.concatenate([np.zeros((hn, hb)), np.eye(hn)], axis=1)
    keep = np.concatenate([keep, np.zeros((hb, hn))], axis=1)
    compact = []
    for p in (0, 1):
        for part in split(np.repeat(f1[p].T, half, axis=1)):
            compact.append(part.astype(np.float32))
        high, low = split(np.kron(np.eye(8), f1[p].T))
        plain["fz%d" % p] = np.concatenate([high, high])
        plain["gz%d" % p] = low
        plain["bz%d" % p] = np.concatenate(
            split(np.kron(np.eye(8), np.concatenate([a1[p], b1[p]]).T)), axis=1
        )
        sample = np.kron(a1[p], keep).T
        slab = np.kron(s_l[picks][:, p::2], pick).T
        plain["by%d" % p] = np.concatenate(split(np.concatenate([sample, sample], axis=1)), axis=1)
        plain["cy%d" % p] = np.concatenate(
            split(np.concatenate([slab, slab, np.kron(b1[p], pick).T], axis=1)), axis=1
        )

    unfold = u_b.T / 2
    pair = np.kron(unfold, unfold).reshape(blocks * blocks, 2, hb, 2, hb)

    def from_samples(table):
        folded = np.einsum("os,spaqb->pqabo", table, pair)
        return folded.reshape(4 * quad, table.shape[0])

    bm = basis.T @ middle
    lin_x = from_samples(np.kron(bm, bm)).reshape(4 * quad, NL, NL)
    lin = np.zeros((4 * quad, 384))
    for c, (p, q) in enumerate(CLASSES):
        lin[:, c * wide : (c + 1) * wide] = lin_x[:, p::2, q::2].reshape(4 * quad, wide)
    lin[:, 256:320] = from_samples(np.kron(fine[picks], bm))[:, order]
    big["lin"] = lin
    k1 = [(s_n @ u_n.T / 2)[p::2, p * half : (p + 1) * half] for p in (0, 1)]
    for c, (p, q) in enumerate(CLASSES):
        big["near%d" % c] = np.kron(k1[p], k1[q]).T
    r1 = [(u_n @ s_n / 2)[p * half : (p + 1) * half, p::2] for p in (0, 1)]
    for c, (p, q) in enumerate(CLASSES):
        big["far%d" % c] = np.kron(r1[p], r1[q]).T

    second = 2 * np.eye(blocks) - np.eye(blocks, k=1) - np.eye(blocks, k=-1)
    s_y, s_z = sine_table(ny), sine_table(nz)
    proj_z = np.zeros((nz, blocks))
    proj_z[:, margin : margin + cells] = s_z
    edge = interp_table(-1, n + 2, -1, cells + 2, Q)
    depth = interp_table(0, n, 0, cells, Q)
    lateral = edge[1 : n + 1]
    s_ext = np.zeros((ny + 2, ny))
    s_ext[1:-1] = s_y
    sp = np.concatenate([s_n[0::2], s_n[1::2]])
    deep = sp @ depth @ s_z

    def by_class(first, second_table):
        parts = []
        for p, q in CLASSES:
            parts.append(
                np.kron(first[p * half : (p + 1) * half], second_table[q * half : (q + 1) * half])
            )
        return np.concatenate(parts).T

    factor = (2.0 / (ny + 1)) * (2.0 / (nz + 1))
    spread, drop = [], []
    for b in range(n_gy):
        proj_y = np.zeros((ny, blocks))
        for j in range(blocks):
            at = j + b * cells - margin
            if 0 <= at < ny:
                proj_y[:, j] = s_y[:, at]
        flat = np.kron(proj_y, proj_z)
        curved = np.kron(proj_y @ second, proj_z) + np.kron(proj_y, proj_z @ second)
        spread.append(
            factor * np.concatenate([from_samples(curved), from_samples(flat)], axis=1)
        )
        local_s = s_ext[b * cells : b * cells + cells + 2]
        rim = np.outer(sp[:, 0], edge[0] @ local_s) + np.outer(sp[:, n - 1], edge[n + 1] @ local_s)
        drop.append(
            np.concatenate([by_class(sp @ lateral @ local_s, deep), by_class(rim, deep)])
        )
    big["spread"] = np.stack(spread)
    big["drop"] = np.stack(drop)
    sb = s_n @ basis
    sbp = np.concatenate([sb[0::2], sb[1::2]])
    facex = np.zeros((4 * wide, n * n))
    for c, (p, q) in enumerate(CLASSES):
        facex[c * wide : (c + 1) * wide, c * 256 : c * 256 + 256] = np.kron(
            sb[p::2, p::2], sb[q::2, q::2]
        ).T
    big["facex"] = facex
    ends = np.stack([sp[:, 0], sp[:, n - 1], sp[:, 0], sp[:, n - 1]], axis=1)
    big["facey"] = by_class(ends, sbp)[order]

    mu_y, mu_z = eigen_values(ny), eigen_values(nz)
    theta = np.arccosh(1.0 + (mu_y[:, None] + mu_z[None, :]).reshape(1, modes) / 2)
    below = 2 * np.sinh(theta) * (1.0 - np.exp(-2 * theta * (nx + 1)))
    apart = np.abs(np.arange(48) - 20)[:, None]
    toep = (np.exp(-theta * apart) + np.exp(-theta * np.maximum(2 * (nx + 1) - apart, 0))) / below
    total = (np.arange(2 * nx + 32) - 13)[:, None]
    hank = np.exp(-theta * np.maximum(total + 2, 0)) + np.exp(-theta * np.maximum(2 * nx - total, 0))
    hank = hank / below

    u12 = np.zeros((64, 16))
    u12[:32, :10] = np.outer(s_n[:, 0], edge[0]) + np.outer(s_n[:, n - 1], edge[n + 1])
    u12[32:, :10] = s_n @ lateral
    place = np.arange(n_gx)
    mine = []
    for a in range(n_gx):
        rank = np.arange(16)[:, None]
        at = cells * a - margin + rank
        inside = (at >= 0) & (at < nx)
        rightward = inside * np.exp(-theta * (15 - rank)) * (1 - np.exp(-2 * theta * (at + 1) * inside))
        leftward = inside * np.exp(-theta * rank) * (1 - np.exp(-2 * theta * (nx - at) * inside))
        row = np.arange(16)[:, None]
        x = cells * a - 1 + row
        used = row < cells + 2
        falling = used * np.exp(-theta * row) * (1 - np.exp(-2 * theta * np.maximum(nx - x, 0))) / below
        rising = (
            used
            * np.exp(-theta * np.maximum(cells + 1 - row, 0))
            * (1 - np.exp(-2 * theta * (x + 1)))
            / below
        )
        away = (a - place)[:, None]
        before = (away >= 2) * np.exp(-theta * np.maximum(cells * away - 12, 0))
        after = (away <= -2) * np.exp(-theta * np.maximum(-cells * away - 12, 0))
        mine.append(
            np.concatenate(
                [
                    rightward,
                    leftward,
                    u12 @ falling,
                    u12 @ rising,
                    toep,
                    hank[2 * cells * a : 2 * cells * a + 48],
                    before,
                    after,
                ]
            )
        )
    mu_l, mu_n = eigen_values(length), eigen_values(n)
    reciprocal = []
    for q in (0, 1):
        for p in (0, 1):
            pair_sum = (mu_l[p::2][:, None] + mu_l[q::2][None, :]).reshape(1, hl * hl)
            table = 1.0 / (mu_l[:, None] + pair_sum)
            reciprocal.append(table.reshape(length, 4, 256).transpose(1, 0, 2).reshape(-1, 256))
    for p, q in CLASSES:
        pair_sum = (mu_n[p::2][:, None] + mu_n[q::2][None, :]).reshape(1, 256)
        reciprocal.append((2.0 / (n + 1)) ** 3 / (mu_n[:, None] + pair_sum))
    ends = np.zeros((n, 256))
    ends[:, :2] = s_n[:, [0, n - 1]]
    reciprocal.append(ends)

    scale = (2.0 / (length + 1)) ** 3
    blank = np.zeros((12, length))
    lefts = {
        "sl": s_l[:, W : W + n],
        "means": a_full * scale,
        "flat": np.concatenate([fine[picks], blank[:, :blocks], bm]),
        "picks": np.concatenate([s_l[picks], blank, b_full]) * scale,
        "sn": s_n,
        "u12": u12,
        "sb": sb,
    }
    for name, value in lefts.items():
        high, low = split(value)
        plain[name] = np.concatenate([high, high, low], axis=1)
    singles = {
        "mine": np.stack(mine).astype(np.float32),
        "recip": np.concatenate(reciprocal).astype(np.float32),
        "compact": np.concatenate(compact),
    }
    places = {}
    for group, names in GROUPS.items():
        packs, row = [], 0
        for name in names:
            if name in plain:
                parts = [plain[name].astype(ml_dtypes.bfloat16)]
            else:
                parts = split(big[name])
            depth, width = parts[0].shape[-2:]
            place = {"left": (row, depth, width)}
            step = 256
            tiles = []
            for part in parts:
                for at in range(0, width, step):
                    tile = np.zeros(part.shape[:-1] + (256,), ml_dtypes.bfloat16)
                    piece = part[..., at : at + step]
                    tile[..., : piece.shape[-1]] = piece
                    packs.append(tile)
                    tiles.append((row, depth))
                    row += depth
            count = len(tiles) // len(parts)
            place["tiles"] = [tiles[k * count : (k + 1) * count] for k in range(len(parts))]
            places[name] = (group, place)
        most = max(tile.ndim for tile in packs)
        if most == 3:
            packs = [np.broadcast_to(tile, (n_gy,) + tile.shape[-2:]) for tile in packs]
        singles[group] = np.concatenate(packs, axis=-2)
    return singles, places


GROUPS = {
    "upz": ["fz0", "gz0", "fz1", "gz1", "sl", "means", "bz0", "bz1"],
    "downy": ["by0", "by1"],
    "spread": ["spread"],
    "side": ["picks", "flat", "sn", "sb", "u12", "lin", "cy0", "cy1"]
    + ["near%d" % c for c in range(4)]
    + ["facex", "facey"],
    "drop": ["drop"],
    "last": ["far%d" % c for c in range(4)] + ["unfold"],
}
NAMES = [
    "charge", "compact", "upz", "recip", "downy", "spread", "mine", "side", "drop", "last",
]
WAITS = [
    ["charge"], ["compact"], ["upz"], ["recip"], ["downy", "spread"], ["mine"],
    ["side", "drop", "last"],
]
CUTS = {"charge": 4, "compact": 4}


def halves(value):
    high = value.astype(jnp.bfloat16)
    return high, (value - high.astype(jnp.float32)).astype(jnp.bfloat16)


def mm(left, right):
    return jnp.dot(left, right, preferred_element_type=jnp.float32)


def window(name, shape):
    return shape[1:] if name in ("spread", "drop", "mine") else shape


def kernel(places, n_gx, n_gy, *refs):
    count = len(NAMES)
    hbm = dict(zip(NAMES, refs[:count]))
    out_ref = refs[count]
    charge_ref, compact_ref, recip_ref, mine_ref, tables_ref = refs[count + 1 : count + 6]
    vmem = {"charge": charge_ref, "compact": compact_ref, "recip": recip_ref, "mine": mine_ref}
    (
        sign_ref, grow_ref, sample_ref, spec_ref, w_ref, z_ref, x_ref, s_ref, b_ref, y_ref, c_ref, d_ref,
        mom_ref, far_ref, near_ref, cx_ref, cy_ref, rx_ref, ry_ref, tally_ref,
        load_sem, f_send, f_recv, p_send, p_recv,
    ) = refs[count + 6 :]
    ndev = n_gx * n_gy
    a = lax.axis_index("gx")
    b = lax.axis_index("gy")
    me = a * n_gy + b
    n, cells = P_SIZE, P_SIZE // Q
    half = n + 2 * W
    modes = near_ref.shape[-1]

    loads, base = {}, 0
    for i, names in enumerate(WAITS):
        start = base
        for name in names:
            source = hbm[name]
            if name in ("spread", "drop"):
                source = source.at[b]
            if name == "mine":
                source = source.at[a]
            if name in GROUPS:
                rows = source.shape[0]
                vmem[name] = tables_ref.at[pl.ds(base, rows)]
                base += rows
            cuts = CUTS.get(name, 1)
            each = source.shape[0] // cuts
            for k in range(cuts):
                part = pl.ds(k * each, each)
                pltpu.make_async_copy(
                    source.at[part], vmem[name].at[part], load_sem.at[i]
                ).start()
        target = tables_ref.at[pl.ds(start, base - start)] if base > start else vmem[names[0]]
        loads[names[0]] = pltpu.make_async_copy(target, target, load_sem.at[i])

    barrier = pltpu.get_barrier_semaphore()

    def greet(r, carry):
        peer = lax.rem(me + r, ndev)
        pl.semaphore_signal(
            barrier, inc=1, device_id=(peer // n_gy, lax.rem(peer, n_gy)), device_id_type=MESH
        )
        return carry

    with jax.named_scope("greet"):
        lax.fori_loop(1, ndev, greet, 0)

    def tile(name, part, i):
        group, place = places[name]
        row, depth = place["tiles"][part][i]
        return vmem[group][row : row + depth, :]

    def table(name, part):
        count = len(places[name][1]["tiles"][part])
        return jnp.concatenate([tile(name, part, i) for i in range(count)], axis=1)

    def right_mul(high, low, name):
        rows = high.shape[0]
        both = mm(jnp.concatenate([high, low], axis=0), table(name, 0))
        return both[:rows] + both[rows:] + mm(high, table(name, 1))

    def left_mul(name, high, low):
        group, place = places[name]
        row, rows, cols = place["left"]
        return mm(vmem[group][row : row + rows, 0:cols], jnp.concatenate([high, low, high], axis=0))

    groups = [[0, 1, 7, 6], [2, 3, 5, 4]]
    with jax.named_scope("signs"):
        z = lax.broadcasted_iota(jnp.int32, (n, 512), 0)
        at = lax.broadcasted_iota(jnp.int32, (n, 512), 1)
        odd = jnp.where((at // 128) % 2 == 1, -1.0, 1.0)
        base = jnp.where(z == at % 16, 1.0, 0.0) + jnp.where(z == 31 - at % 16, odd, 0.0)
        turned = jnp.where(at >= 256, -base, base)
        spot = (at // 16) % 8
        for side, value in ((0, base), (1, turned)):
            for y in range(8):
                rows = (side * 8 + y) * n
                match = spot == ((3 - y) % 8 if side else y)
                sign_ref[rows : rows + n] = jnp.where(match, value, 0.0).astype(jnp.bfloat16)

    with jax.named_scope("w_charge"):
        loads["charge"].wait()
        loads["compact"].wait()
    with jax.named_scope("grow"):
        same = lax.broadcasted_iota(jnp.int32, (16, 512), 0)
        same = jnp.where(lax.broadcasted_iota(jnp.int32, (16, 512), 1) % 16 == same, 1.0, 0.0)
        same = same.astype(jnp.bfloat16)
        for t in range(4):
            for i in range(16):
                line = jnp.broadcast_to(compact_ref[t * 16 + i : t * 16 + i + 1], (16, 512))
                grow_ref[t, i * 16 : (i + 1) * 16] = line.astype(jnp.bfloat16) * same
    with jax.named_scope("fold"):
        charge = vmem["charge"]
        sides = [
            jnp.concatenate([charge[:, v * 128 : (v + 1) * 128] for v in group], axis=1)
            for group in groups
        ]
        high, low = halves(jnp.concatenate(sides, axis=0))
        both = mm(jnp.concatenate([high, low], axis=0), sign_ref[...])
        parts = halves(both[: 2 * n] + both[2 * n :])
        lane = lax.broadcasted_iota(jnp.int32, (half, 128), 1)
        for k, part in enumerate(parts):
            for c in range(4):
                for side in range(2):
                    piece = part[side * n : (side + 1) * n, c * 128 : (c + 1) * 128]
                    rows = (2 * k + c % 2) * n
                    w_ref[c // 2, rows : rows + n, side * 128 : (side + 1) * 128] = piece
    with jax.named_scope("upy"):
        for p in range(2):
            both = mm(w_ref[p], grow_ref[2 * p])
            lift = both[: 2 * n] + both[2 * n :] + mm(w_ref[p, 0 : 2 * n], grow_ref[2 * p + 1])
            high, low = halves(lift)
            for q in range(2):
                for k in range(4):
                    at = (4 * p + k) * n
                    rows, lanes = slice(q * n, (q + 1) * n), slice(k * 128, (k + 1) * 128)
                    z_ref[q, at : at + n, 0:128] = high[rows, lanes]
                    z_ref[q, at : at + n, 128:256] = low[rows, lanes]
    with jax.named_scope("w_upz"):
        loads["upz"].wait()
    with jax.named_scope("upz"):
        for q in range(2):
            up = mm(z_ref[q], tile("fz%d" % q, 0, 0)) + mm(z_ref[q, :, 0:128], tile("gz%d" % q, 0, 0))
            high, low = halves(up)
            for k in range(8):
                rows, lanes = slice(k * n, (k + 1) * n), slice((8 * q + k) * 256, (8 * q + k + 1) * 256)
                x_ref[0:n, lanes] = high[rows]
                x_ref[n : 2 * n, lanes] = low[rows]
    with jax.named_scope("w_recip"):
        loads["recip"].wait()
    with jax.named_scope("upx"):
        group, place = places["sl"]
        row, rows, cols = place["left"]
        weights = vmem[group][row : row + rows, 0:cols]
        for q in range(2):
            lanes = slice(q * 2048, (q + 1) * 2048)
            spectrum = mm(
                weights, jnp.concatenate([x_ref[:, lanes], x_ref[0:n, lanes]], axis=0)
            )
            divisor = [
                vmem["recip"][(8 * q + k) * half : (8 * q + k + 1) * half] for k in range(8)
            ]
            high, low = halves(spectrum * jnp.concatenate(divisor, axis=1))
            s_ref[0:half, lanes] = high
            s_ref[half : 2 * half, lanes] = low

    def down(name, rows, b_ref, y_ref, finish):
        group, place = places[name]
        row, _, cols = place["left"]
        weights = vmem[group][row : row + rows, 0:cols]
        for q in range(2):
            lanes = slice(q * 2048, (q + 1) * 2048)
            stacked = jnp.concatenate([weights[:, 0:half], weights[:, 2 * half : 3 * half]], axis=0)
            short = mm(stacked, s_ref[0:half, lanes])
            short = short[:rows] + short[rows:] + mm(weights[:, 0:half], s_ref[half:, lanes])
            high, low = halves(short)
            for k in range(8):
                lanes = slice(k * 256, (k + 1) * 256)
                b_ref[q, k * rows : (k + 1) * rows] = high[:, lanes]
                b_ref[q, (8 + k) * rows : (9 + k) * rows] = low[:, lanes]
        for q in range(2):
            both = mm(b_ref[q], tile("bz%d" % q, 0, 0))
            block = 8 * rows
            high, low = halves(both[:block, :128] + both[block:, :128] + both[:block, 128:])
            for p in range(2):
                for k in range(4):
                    at, lanes = (4 * p + k) * rows, slice(k * 128, (k + 1) * 128)
                    y_ref[p, q * rows : (q + 1) * rows, lanes] = high[at : at + rows]
                    y_ref[p, (2 + q) * rows : (3 + q) * rows, lanes] = low[at : at + rows]
        ys = []
        finish()
        for p in range(2):
            both = mm(y_ref[p], tile("%sy%d" % ("b" if name == "means" else "c", p), 0, 0))
            both = both[: 2 * rows, :128] + both[2 * rows :, :128] + both[: 2 * rows, 128:]
            ys += [both[:rows], both[rows:]]
        return ys

    def arrive():
        loads["downy"].wait()
        loads["mine"].wait()

    with jax.named_scope("down"):
        y0, y1, y2, y3 = down("means", 16, b_ref, y_ref, arrive)
    with jax.named_scope("spread"):
        sample = jnp.concatenate(
            [jnp.where(lane[0:16] < 64, u, v) for u, v in ((y0, y1), (y2, y3))], axis=1
        )
        sample = halves(sample)
        sample_ref[0] = sample[0]
        sample_ref[1] = sample[1]
        spread = right_mul(*sample, "spread")
        bend = spread[:, modes:]
        gap = jnp.zeros((1, modes), jnp.float32)
        packet = spread[:, :modes] + 2.0 * bend
        packet = packet - jnp.concatenate([gap, bend[:-1]]) - jnp.concatenate([bend[1:], gap])
        mine = vmem["mine"]
        near_ref[n_gy + b] = packet
        rightward = jnp.sum(packet * mine[0:16], axis=0, keepdims=True)
        leftward = jnp.sum(packet * mine[16:32], axis=0, keepdims=True)
        for g in range(modes // 128):
            mom_ref[g, 0:1] = rightward[:, g * 128 : (g + 1) * 128]
            mom_ref[g, 1:2] = leftward[:, g * 128 : (g + 1) * 128]

    def remote(source, target, send, recv, device):
        return pltpu.make_async_remote_copy(
            src_ref=source,
            dst_ref=target,
            send_sem=send,
            recv_sem=recv,
            device_id=device,
            device_id_type=MESH,
        )

    def start_far(r, carry):
        d = n_gx - r
        for j in range(n_gy):
            for row, other, fine in ((0, a + d, a + d < n_gx), (1, a - d, a >= d)):

                @pl.when(fine)
                def _():
                    remote(
                        mom_ref.at[:, pl.ds(row, 1)],
                        far_ref.at[b, :, pl.ds(a, 1)],
                        f_send,
                        f_recv,
                        (other, j),
                    ).start()

        return carry

    early = a < n_gx // 8

    def send_far():
        with jax.named_scope("sendf"):
            lax.fori_loop(1, n_gx - 1, start_far, 0)

    def send_near():
        with jax.named_scope("send"):
            for step in (0, 1, 2):
                for j in range(n_gy):
                    other = a + step - 1
                    fine = (other >= 0) & (other < n_gx)
                    if step == 1:
                        fine = b != j

                    @pl.when(fine)
                    def _():
                        remote(
                            near_ref.at[n_gy + b],
                            near_ref.at[(2 - step) * n_gy + b],
                            p_send,
                            p_recv,
                            (other, j),
                        ).start()

    upper, lower = lax.rem(b + 1, n_gy), lax.rem(b + n_gy - 1, n_gy)
    def send_faces():
        with jax.named_scope("sendc"):

            @pl.when(a < n_gx - 1)
            def _():
                remote(
                    cx_ref.at[pl.ds(2, 1)], rx_ref.at[pl.ds(0, 1)], p_send, p_recv, (a + 1, b)
                ).start()

            @pl.when(a > 0)
            def _():
                remote(
                    cx_ref.at[pl.ds(1, 1)], rx_ref.at[pl.ds(1, 1)], p_send, p_recv, (a - 1, b)
                ).start()

            remote(cy_ref, ry_ref.at[0], p_send, p_recv, (a, upper)).start()
            remote(cy_ref, ry_ref.at[1], p_send, p_recv, (a, lower)).start()

    def turn(step, carry):
        @pl.when(step == last)
        def _():
            with jax.named_scope("barrier"):
                pl.semaphore_wait(barrier, ndev - 1)

            @pl.when(early)
            def _():
                send_faces()
                send_near()
                send_far()

            @pl.when(jnp.logical_not(early))
            def _():
                send_far()
                send_near()

        @pl.when(step != last)
        def _():
            with jax.named_scope("w_side"):
                loads["side"].wait()
            with jax.named_scope("lin"):
                y0, y1, y2, y3 = down("picks", 32, c_ref, d_ref, lambda: None)
                flat = right_mul(*halves(left_mul("flat", sample_ref[0], sample_ref[1])), "lin")
                cx = jnp.concatenate(
                    [
                        jnp.where(lane[0:8] < 64, pltpu.roll(u[0:8], 64, 1), v[0:8])
                        for u, v in ((y0, y1), (y2, y3))
                    ],
                    axis=1,
                )
                cx = cx - flat[0:8, 0:256]
                cy = jnp.where(lane[0:16] < 32, y0[16:] + y2[16:], y1[16:] + y3[16:])
                cy = cy - flat[16:32, 256:384]
                cx_ref[...] = cx
                cy_ref[...] = cy

            with jax.named_scope("near"):
                folded = [
                    jnp.concatenate(
                        [w_ref[c // 2, (2 * k + c % 2) * n : (2 * k + c % 2 + 1) * n] for c in range(4)],
                        axis=1,
                    )
                    for k in range(2)
                ]
                narrow = halves(left_mul("sn", *folded))
                spectrum = []
                for c in range(4):
                    at = slice(c * 256, (c + 1) * 256)
                    spectrum.append(right_mul(narrow[0][:, at], narrow[1][:, at], "near%d" % c))
                spec_ref[...] = jnp.concatenate(spectrum, axis=1)

        return carry

    last = jnp.where(early, 1, 0)
    lax.fori_loop(0, 2, turn, 0)

    @pl.when(jnp.logical_not(early))
    def _():
        send_faces()

    edge = (a == 0) | (a == n_gx - 1)
    inner = jnp.logical_not(edge)

    def settle_near(sides):
        lines = 16 * (modes // 128) * ((1 + sides) * n_gy - 1) + 2 * sides + 32
        block = tally_ref.at[pl.ds(0, lines)]
        remote(block, block, p_send, p_recv, (a, b)).wait()

    with jax.named_scope("wait_p"):

        @pl.when(edge)
        def _():
            settle_near(1)

        @pl.when(inner)
        def _():
            settle_near(2)

    with jax.named_scope("face"):
        cx, cy, spectrum = cx_ref[...], cy_ref[...], spec_ref[...]
        from_left = jnp.where(a > 0, rx_ref[0:1], 0.0)
        from_right = jnp.where(a < n_gx - 1, rx_ref[1:2], 0.0)
        ends = jnp.concatenate(
            [cx[0:1] + from_left, cx[3:4] + from_right, jnp.zeros((14, cx.shape[1]), jnp.float32)]
        )
        ends = right_mul(*halves(ends), "facex")
        fine = 16 * half
        column = vmem["recip"][fine + 4 * n : fine + 5 * n, 0:2]
        spectrum = spectrum + column[:, 0:1] * ends[0:1] + column[:, 1:2] * ends[1:2]
        group = jnp.where(lane[0:16] < 64, lax.rem(lane[0:16], 32) // 8, 4)
        total = jnp.where((group == 0) | (group == 3), cy, 0.0)
        total = total + jnp.where((group == 2) & (b > 0), ry_ref[0], 0.0)
        total = total + jnp.where((group == 1) & (b < n_gy - 1), ry_ref[1], 0.0)
        total = left_mul("sb", *halves(total))[:, 0:64]
        spectrum = spectrum + right_mul(*halves(total), "facey")
    with jax.named_scope("green"):
        row = lax.broadcasted_iota(jnp.int32, (8, modes), 0)

        def gathered(step):
            value = near_ref[step * n_gy]
            for j in range(1, n_gy):
                value = value + near_ref[step * n_gy + j]
            return value

        past = jnp.where(a > 0, gathered(0), 0.0)
        here = gathered(1)
        next_ = jnp.where(a < n_gx - 1, gathered(2), 0.0)
        source = jnp.concatenate(
            [
                jnp.where((row >= 4) | (a > 1), past[0:8], 0.0),
                past[8:16] + jnp.where((row >= 4) | (a > 0), here[0:8], 0.0),
                jnp.where((row < 4) | (a < n_gx - 1), here[8:16] + next_[0:8], 0.0),
                jnp.where((row < 4) | (a < n_gx - 2), next_[8:16], 0.0),
            ]
        )
        values = []
        for i in range(cells + 2):
            influence = mine[169 - i : 201 - i] - mine[208 + i : 240 + i]
            values.append(jnp.sum(influence * source, axis=0, keepdims=True))
        values.append(jnp.zeros((16 - len(values), modes), jnp.float32))
        lifted = left_mul("u12", *halves(jnp.concatenate(values, axis=0)))

    inverse = jnp.concatenate(
        [vmem["recip"][fine + c * n : fine + (c + 1) * n] for c in range(4)], axis=1
    )

    def unfolded(parts):
        sides = [
            jnp.concatenate([part[:, s * 128 : (s + 1) * 128] for part in parts], axis=1)
            for s in range(2)
        ]
        return jnp.concatenate(sides, axis=0)

    def cells_of(both):
        for s, group in enumerate(groups):
            for i, v in enumerate(group):
                yield v, both[s * n : (s + 1) * n, i * 128 : (i + 1) * 128]

    with jax.named_scope("base"):
        lifted = halves(jnp.concatenate([lifted[:n], lifted[n:]], axis=1))
        spectrum = (spectrum + right_mul(*lifted, "drop")) * inverse
        high, low = halves(left_mul("sn", *halves(spectrum)))
        parts = []
        for c in range(4):
            at = slice(c * 256, (c + 1) * 256)
            parts.append(right_mul(high[:, at], low[:, at], "far%d" % c))
        high, low = halves(unfolded(parts))
        both = mm(jnp.concatenate([high, low], axis=0), table("unfold", 0))
        for v, value in cells_of(both[: 2 * n] + both[2 * n :]):
            out_ref[:, v * 128 : (v + 1) * 128] = value

    def settle_far(each):
        block = far_ref.at[:, :, pl.ds(0, each)]
        remote(block, block, f_send, f_recv, (a, b)).wait()

    with jax.named_scope("wait_f"):

        @pl.when(edge)
        def _():
            settle_far(n_gx - 2)

        @pl.when(inner)
        def _():
            settle_far(n_gx - 3)

    with jax.named_scope("final"):
        origin = lax.broadcasted_iota(jnp.int32, (n_gx, modes), 0)
        before = jnp.zeros((n_gx, modes), jnp.float32)
        after = before
        for j in range(n_gy):
            sent = jnp.concatenate([far_ref[j, g] for g in range(modes // 128)], axis=1)
            before = before + jnp.where(origin <= a - 2, sent, 0.0)
            after = after + jnp.where(origin >= a + 2, sent, 0.0)
        before = jnp.sum(before * mine[256 : 256 + n_gx], axis=0, keepdims=True)
        after = jnp.sum(after * mine[256 + n_gx : 256 + 2 * n_gx], axis=0, keepdims=True)
        lifted = mine[32:96] * before + mine[96:160] * after
        lifted = jnp.concatenate([lifted[:n], lifted[n:]], axis=1).astype(jnp.bfloat16)
        spectrum = (mm(lifted, table("drop", 0)) * inverse).astype(jnp.bfloat16)
        group, place = places["sn"]
        row, rows, _ = place["left"]
        spectrum = mm(vmem[group][row : row + rows, 0:n], spectrum).astype(jnp.bfloat16)
        parts = [mm(spectrum[:, c * 256 : (c + 1) * 256], tile("far%d" % c, 0, 0)) for c in range(4)]
    with jax.named_scope("unfold"):
        both = mm(unfolded(parts).astype(jnp.bfloat16), table("unfold", 0))
        for v, value in cells_of(both):
            at = slice(v * 128, (v + 1) * 128)
            out_ref[:, at] = out_ref[:, at] + value


def emit(in_ref, out_ref, sem):
    copy = pltpu.make_async_copy(in_ref, out_ref, sem)
    copy.start()
    copy.wait()


def body(n_gx, n_gy, charge):
    singles, places = tables(n_gx, n_gy)
    arrays = [charge] + [jnp.asarray(singles[name]) for name in NAMES[1:]]
    shapes = {name: window(name, array.shape) for name, array in zip(NAMES, arrays)}
    total = sum(shapes[name][0] for name in GROUPS)
    scratch = [pltpu.VMEM(shapes[name], jnp.float32) for name in ("charge", "compact", "recip", "mine")]
    scratch.append(pltpu.VMEM((total, 256), jnp.bfloat16))
    modes = n_gy * (P_SIZE // Q) ** 2
    half = P_SIZE + 2 * W
    scratch += [
        pltpu.VMEM((512, 512), jnp.bfloat16),
        pltpu.VMEM((4, 256, 512), jnp.bfloat16),
        pltpu.VMEM((2, 16, 256), jnp.bfloat16),
        pltpu.VMEM((P_SIZE, 1024), jnp.float32),
        pltpu.VMEM((2, 4 * P_SIZE, 256), jnp.bfloat16),
        pltpu.VMEM((2, 8 * P_SIZE, 256), jnp.bfloat16),
        pltpu.VMEM((2 * P_SIZE, 4096), jnp.bfloat16),
        pltpu.VMEM((2 * half, 4096), jnp.bfloat16),
        pltpu.VMEM((2, 256, 256), jnp.bfloat16),
        pltpu.VMEM((2, 64, 512), jnp.bfloat16),
        pltpu.VMEM((2, 512, 256), jnp.bfloat16),
        pltpu.VMEM((2, 128, 512), jnp.bfloat16),
        pltpu.VMEM((modes // 128, 8, 128), jnp.float32),
        pltpu.VMEM((n_gy, modes // 128, n_gx, 128), jnp.float32),
        pltpu.VMEM((3 * n_gy, 16, modes), jnp.float32),
        pltpu.VMEM((8, 256), jnp.float32),
        pltpu.VMEM((16, 128), jnp.float32),
        pltpu.VMEM((8, 256), jnp.float32),
        pltpu.VMEM((2, 16, 128), jnp.float32),
        pltpu.VMEM((16 * (modes // 128) * (3 * n_gy - 1) + 40, 128), jnp.float32),
        pltpu.SemaphoreType.DMA((len(WAITS),)),
        pltpu.SemaphoreType.DMA,
        pltpu.SemaphoreType.DMA,
        pltpu.SemaphoreType.DMA,
        pltpu.SemaphoreType.DMA,
    ]
    hbm = pl.BlockSpec(memory_space=pl.ANY)
    vm = pl.BlockSpec(memory_space=pltpu.VMEM)
    solved = pl.pallas_call(
        functools.partial(kernel, places, n_gx, n_gy),
        out_shape=pltpu.VMEM(charge.shape, charge.dtype),
        in_specs=[hbm] * len(NAMES),
        out_specs=vm,
        scratch_shapes=scratch,
        name="mlc",
        compiler_params=pltpu.CompilerParams(
            collective_id=0, has_side_effects=True, vmem_limit_bytes=60 * 1024 * 1024
        ),
    )(*arrays)
    return pl.pallas_call(
        emit,
        out_shape=jax.ShapeDtypeStruct(charge.shape, charge.dtype),
        in_specs=[vm],
        out_specs=hbm,
        scratch_shapes=[pltpu.SemaphoreType.DMA],
        name="emit",
        compiler_params=pltpu.CompilerParams(vmem_limit_bytes=1024 * 1024),
    )(solved)


def solution(mesh):
    run = functools.partial(body, mesh.shape["gx"], mesh.shape["gy"])
    spec = P("gx", "gy")
    return jax.shard_map(run, mesh=mesh, in_specs=(spec,), out_specs=spec, check_vma=False)
```

```python
import functools

import jax
import jax.numpy as jnp
import ml_dtypes
import numpy as np
from jax import lax
from jax.experimental import pallas as pl
from jax.experimental.pallas import tpu as pltpu
from jax.sharding import PartitionSpec as P

P_SIZE = 32
W = 16
Q = 4
NL = 16
CLASSES = [(0, 0), (0, 1), (1, 0), (1, 1)]
MESH = pl.DeviceIdType.MESH


def sine_table(length):
    counter = np.arange(length) + 1
    return np.sin(np.pi * np.outer(counter, counter) / (length + 1))


def eigen_values(length):
    return 2.0 - 2.0 * np.cos(np.pi * (np.arange(length) + 1) / (length + 1))


def interp_table(fine_start, fine_count, coarse_start, coarse_count, ratio):
    fine_pos = np.arange(fine_count) + fine_start
    coarse_pos = np.arange(coarse_count) + coarse_start
    numerator = 2 * fine_pos - (ratio - 1)
    lower = numerator // (2 * ratio)
    weight = ((numerator - 2 * ratio * lower) / (2 * ratio))[:, None]
    below = coarse_pos[None, :] == lower[:, None]
    above = coarse_pos[None, :] == lower[:, None] + 1
    return below * (1.0 - weight) + above * weight


def legendre_basis(length, count):
    points = (2.0 * np.arange(length) + 1.0) / length - 1.0
    columns = [np.ones_like(points), points]
    for degree in range(2, count):
        columns.append(
            ((2 * degree - 1) * points * columns[-1] - (degree - 1) * columns[-2]) / degree
        )
    result = []
    for vector in columns[:count]:
        for passes in range(2):
            for earlier in result:
                vector = vector - np.sum(earlier * vector) * earlier
        result.append(vector / np.sqrt(np.sum(vector * vector)))
    return np.stack(result, axis=1)


def fold(length):
    half = length // 2
    eye = np.eye(length)
    return np.concatenate([eye[:half] + eye[::-1][:half], eye[:half] - eye[::-1][:half]])


def split(table):
    high = table.astype(ml_dtypes.bfloat16)
    low = (table - high.astype(np.float64)).astype(ml_dtypes.bfloat16)
    return high, low


@functools.lru_cache(maxsize=None)
def tables(n_gx, n_gy):
    n, length, cells = P_SIZE, P_SIZE + 2 * W, P_SIZE // Q
    blocks, margin = length // Q, W // Q
    half, hl, hb, hn = n // 2, length // 2, blocks // 2, NL // 2
    quad, wide = hb * hb, hn * hn
    nx, ny, nz = n_gx * cells, n_gy * cells, cells
    modes = ny * nz
    s_l, s_n = sine_table(length), sine_table(n)
    u_n, u_b = fold(n), fold(blocks)
    basis = legendre_basis(n, NL)
    average = np.kron(np.eye(blocks), np.full((1, Q), 1.0 / Q))
    fine = interp_table(0, length, 0, blocks, Q)
    middle = fine[W : W + n]
    picks = [W - 1, W, W + n - 1, W + n]
    a_full = average @ s_l
    b_full = basis.T @ s_l[W : W + n]
    order = np.arange(4 * NL).reshape(4, hn, 2).transpose(2, 0, 1).ravel()
    big = {}

    folding = np.zeros((4, 4, n, 4, 2 * 4, half))
    for c, (p, q) in enumerate(CLASSES):
        for vi in range(4):
            for y4 in range(4):
                il = [y4, 4 + y4, 3 - y4, 7 - y4][vi]
                sign = -1.0 if vi > 1 and p == 1 else 1.0
                folding[vi, y4, :, c, il, :] = sign * u_n[q * half : (q + 1) * half].T
    folding = folding.reshape(4 * 128, 4 * 128)
    plain = {"unfold": folding.T}

    inner = s_l[:, W : W + n] @ u_n.T / 2
    f1 = [inner[p::2, p * half : (p + 1) * half] for p in (0, 1)]
    a1 = [(u_b @ a_full)[p * hb : (p + 1) * hb, p::2] for p in (0, 1)]
    b1 = [b_full[p::2, p::2] for p in (0, 1)]
    keep, pick = np.eye(hb), np.concatenate([np.zeros((hn, hb)), np.eye(hn)], axis=1)
    keep = np.concatenate([keep, np.zeros((hb, hn))], axis=1)
    compact = []
    for p in (0, 1):
        for part in split(np.repeat(f1[p].T, half, axis=1)):
            compact.append(part.astype(np.float32))
        high, low = split(np.kron(np.eye(8), f1[p].T))
        plain["fz%d" % p] = np.concatenate([high, high])
        plain["gz%d" % p] = low
        plain["bz%d" % p] = np.concatenate(
            split(np.kron(np.eye(8), np.concatenate([a1[p], b1[p]]).T)), axis=1
        )
        sample = np.kron(a1[p], keep).T
        slab = np.kron(s_l[picks][:, p::2], pick).T
        plain["by%d" % p] = np.concatenate(split(np.concatenate([sample, sample], axis=1)), axis=1)
        plain["cy%d" % p] = np.concatenate(
            split(np.concatenate([slab, slab, np.kron(b1[p], pick).T], axis=1)), axis=1
        )

    unfold = u_b.T / 2
    pair = np.kron(unfold, unfold).reshape(blocks * blocks, 2, hb, 2, hb)

    def from_samples(table):
        folded = np.einsum("os,spaqb->pqabo", table, pair)
        return folded.reshape(4 * quad, table.shape[0])

    bm = basis.T @ middle
    lin_x = from_samples(np.kron(bm, bm)).reshape(4 * quad, NL, NL)
    lin = np.zeros((4 * quad, 384))
    for c, (p, q) in enumerate(CLASSES):
        lin[:, c * wide : (c + 1) * wide] = lin_x[:, p::2, q::2].reshape(4 * quad, wide)
    lin[:, 256:320] = from_samples(np.kron(fine[picks], bm))[:, order]
    big["lin"] = lin
    k1 = [(s_n @ u_n.T / 2)[p::2, p * half : (p + 1) * half] for p in (0, 1)]
    for c, (p, q) in enumerate(CLASSES):
        big["near%d" % c] = np.kron(k1[p], k1[q]).T
    r1 = [(u_n @ s_n / 2)[p * half : (p + 1) * half, p::2] for p in (0, 1)]
    for c, (p, q) in enumerate(CLASSES):
        big["far%d" % c] = np.kron(r1[p], r1[q]).T

    second = 2 * np.eye(blocks) - np.eye(blocks, k=1) - np.eye(blocks, k=-1)
    s_y, s_z = sine_table(ny), sine_table(nz)
    proj_z = np.zeros((nz, blocks))
    proj_z[:, margin : margin + cells] = s_z
    edge = interp_table(-1, n + 2, -1, cells + 2, Q)
    depth = interp_table(0, n, 0, cells, Q)
    lateral = edge[1 : n + 1]
    s_ext = np.zeros((ny + 2, ny))
    s_ext[1:-1] = s_y
    sp = np.concatenate([s_n[0::2], s_n[1::2]])
    deep = sp @ depth @ s_z

    def by_class(first, second_table):
        parts = []
        for p, q in CLASSES:
            parts.append(
                np.kron(first[p * half : (p + 1) * half], second_table[q * half : (q + 1) * half])
            )
        return np.concatenate(parts).T

    factor = (2.0 / (ny + 1)) * (2.0 / (nz + 1))
    spread, drop = [], []
    for b in range(n_gy):
        proj_y = np.zeros((ny, blocks))
        for j in range(blocks):
            at = j + b * cells - margin
            if 0 <= at < ny:
                proj_y[:, j] = s_y[:, at]
        flat = np.kron(proj_y, proj_z)
        curved = np.kron(proj_y @ second, proj_z) + np.kron(proj_y, proj_z @ second)
        spread.append(
            factor * np.concatenate([from_samples(curved), from_samples(flat)], axis=1)
        )
        local_s = s_ext[b * cells : b * cells + cells + 2]
        rim = np.outer(sp[:, 0], edge[0] @ local_s) + np.outer(sp[:, n - 1], edge[n + 1] @ local_s)
        drop.append(
            np.concatenate([by_class(sp @ lateral @ local_s, deep), by_class(rim, deep)])
        )
    big["spread"] = np.stack(spread)
    big["drop"] = np.stack(drop)
    sb = s_n @ basis
    sbp = np.concatenate([sb[0::2], sb[1::2]])
    facex = np.zeros((4 * wide, n * n))
    for c, (p, q) in enumerate(CLASSES):
        facex[c * wide : (c + 1) * wide, c * 256 : c * 256 + 256] = np.kron(
            sb[p::2, p::2], sb[q::2, q::2]
        ).T
    big["facex"] = facex
    ends = np.stack([sp[:, 0], sp[:, n - 1], sp[:, 0], sp[:, n - 1]], axis=1)
    big["facey"] = by_class(ends, sbp)[order]

    mu_y, mu_z = eigen_values(ny), eigen_values(nz)
    theta = np.arccosh(1.0 + (mu_y[:, None] + mu_z[None, :]).reshape(1, modes) / 2)
    below = 2 * np.sinh(theta) * (1.0 - np.exp(-2 * theta * (nx + 1)))
    apart = np.abs(np.arange(48) - 20)[:, None]
    toep = (np.exp(-theta * apart) + np.exp(-theta * np.maximum(2 * (nx + 1) - apart, 0))) / below
    total = (np.arange(2 * nx + 32) - 13)[:, None]
    hank = np.exp(-theta * np.maximum(total + 2, 0)) + np.exp(-theta * np.maximum(2 * nx - total, 0))
    hank = hank / below

    u12 = np.zeros((64, 16))
    u12[:32, :10] = np.outer(s_n[:, 0], edge[0]) + np.outer(s_n[:, n - 1], edge[n + 1])
    u12[32:, :10] = s_n @ lateral
    place = np.arange(n_gx)
    mine = []
    for a in range(n_gx):
        rank = np.arange(16)[:, None]
        at = cells * a - margin + rank
        inside = (at >= 0) & (at < nx)
        rightward = inside * np.exp(-theta * (15 - rank)) * (1 - np.exp(-2 * theta * (at + 1) * inside))
        leftward = inside * np.exp(-theta * rank) * (1 - np.exp(-2 * theta * (nx - at) * inside))
        row = np.arange(16)[:, None]
        x = cells * a - 1 + row
        used = row < cells + 2
        falling = used * np.exp(-theta * row) * (1 - np.exp(-2 * theta * np.maximum(nx - x, 0))) / below
        rising = (
            used
            * np.exp(-theta * np.maximum(cells + 1 - row, 0))
            * (1 - np.exp(-2 * theta * (x + 1)))
            / below
        )
        away = (a - place)[:, None]
        before = (away >= 2) * np.exp(-theta * np.maximum(cells * away - 12, 0))
        after = (away <= -2) * np.exp(-theta * np.maximum(-cells * away - 12, 0))
        mine.append(
            np.concatenate(
                [
                    rightward,
                    leftward,
                    u12 @ falling,
                    u12 @ rising,
                    toep,
                    hank[2 * cells * a : 2 * cells * a + 48],
                    before,
                    after,
                ]
            )
        )
    mu_l, mu_n = eigen_values(length), eigen_values(n)
    reciprocal = []
    for q in (0, 1):
        for p in (0, 1):
            pair_sum = (mu_l[p::2][:, None] + mu_l[q::2][None, :]).reshape(1, hl * hl)
            table = 1.0 / (mu_l[:, None] + pair_sum)
            reciprocal.append(table.reshape(length, 4, 256).transpose(1, 0, 2).reshape(-1, 256))
    for p, q in CLASSES:
        pair_sum = (mu_n[p::2][:, None] + mu_n[q::2][None, :]).reshape(1, 256)
        reciprocal.append((2.0 / (n + 1)) ** 3 / (mu_n[:, None] + pair_sum))
    ends = np.zeros((n, 256))
    ends[:, :2] = s_n[:, [0, n - 1]]
    reciprocal.append(ends)

    scale = (2.0 / (length + 1)) ** 3
    blank = np.zeros((12, length))
    lefts = {
        "sl": s_l[:, W : W + n],
        "means": a_full * scale,
        "flat": np.concatenate([fine[picks], blank[:, :blocks], bm]),
        "picks": np.concatenate([s_l[picks], blank, b_full]) * scale,
        "sn": s_n,
        "u12": u12,
        "sb": sb,
    }
    for name, value in lefts.items():
        high, low = split(value)
        plain[name] = np.concatenate([high, high, low], axis=1)
    singles = {
        "mine": np.stack(mine).astype(np.float32),
        "recip": np.concatenate(reciprocal).astype(np.float32),
        "compact": np.concatenate(compact),
    }
    places = {}
    for group, names in GROUPS.items():
        packs, row = [], 0
        for name in names:
            if name in plain:
                parts = [plain[name].astype(ml_dtypes.bfloat16)]
            else:
                parts = split(big[name])
            depth, width = parts[0].shape[-2:]
            place = {"left": (row, depth, width)}
            step = 256
            tiles = []
            for part in parts:
                for at in range(0, width, step):
                    tile = np.zeros(part.shape[:-1] + (256,), ml_dtypes.bfloat16)
                    piece = part[..., at : at + step]
                    tile[..., : piece.shape[-1]] = piece
                    packs.append(tile)
                    tiles.append((row, depth))
                    row += depth
            count = len(tiles) // len(parts)
            place["tiles"] = [tiles[k * count : (k + 1) * count] for k in range(len(parts))]
            places[name] = (group, place)
        most = max(tile.ndim for tile in packs)
        if most == 3:
            packs = [np.broadcast_to(tile, (n_gy,) + tile.shape[-2:]) for tile in packs]
        singles[group] = np.concatenate(packs, axis=-2)
    return singles, places


GROUPS = {
    "upz": ["fz0", "gz0", "fz1", "gz1", "sl", "means", "bz0", "bz1"],
    "downy": ["by0", "by1"],
    "spread": ["spread"],
    "side": ["picks", "flat", "sn", "sb", "u12", "lin", "cy0", "cy1"]
    + ["near%d" % c for c in range(4)]
    + ["facex", "facey"],
    "drop": ["drop"],
    "last": ["far%d" % c for c in range(4)] + ["unfold"],
}
NAMES = [
    "charge", "compact", "upz", "recip", "downy", "spread", "mine", "side", "drop", "last",
]
WAITS = [
    ["charge"], ["compact"], ["upz"], ["recip"], ["downy", "spread", "mine"],
    ["side", "drop", "last"],
]
CUTS = {"charge": 4, "compact": 4}


def halves(value):
    high = value.astype(jnp.bfloat16)
    return high, (value - high.astype(jnp.float32)).astype(jnp.bfloat16)


def mm(left, right):
    return jnp.dot(left, right, preferred_element_type=jnp.float32)


def window(name, shape):
    return shape[1:] if name in ("spread", "drop", "mine") else shape


def kernel(places, n_gx, n_gy, *refs):
    count = len(NAMES)
    hbm = dict(zip(NAMES, refs[:count]))
    out_ref = refs[count]
    charge_ref, compact_ref, recip_ref, mine_ref, tables_ref = refs[count + 1 : count + 6]
    vmem = {"charge": charge_ref, "compact": compact_ref, "recip": recip_ref, "mine": mine_ref}
    (
        sign_ref, grow_ref, sample_ref, spec_ref, w_ref, z_ref, x_ref, s_ref, b_ref, y_ref, c_ref, d_ref,
        mom_ref, far_ref, near_ref, cx_ref, cy_ref, rx_ref, ry_ref, tally_ref,
        load_sem, f_send, f_recv, p_send, p_recv,
    ) = refs[count + 6 :]
    ndev = n_gx * n_gy
    a = lax.axis_index("gx")
    b = lax.axis_index("gy")
    me = a * n_gy + b
    n, cells = P_SIZE, P_SIZE // Q
    half = n + 2 * W
    modes = near_ref.shape[-1]

    loads, base = {}, 0
    for i, names in enumerate(WAITS):
        start = base
        for name in names:
            source = hbm[name]
            if name in ("spread", "drop"):
                source = source.at[b]
            if name == "mine":
                source = source.at[a]
            if name in GROUPS:
                rows = source.shape[0]
                vmem[name] = tables_ref.at[pl.ds(base, rows)]
                base += rows
            cuts = CUTS.get(name, 1)
            each = source.shape[0] // cuts
            for k in range(cuts):
                part = pl.ds(k * each, each)
                pltpu.make_async_copy(
                    source.at[part], vmem[name].at[part], load_sem.at[i]
                ).start()
        extra = 2 * vmem["mine"].shape[0] * modes // 256 if "mine" in names else 0
        target = tables_ref.at[pl.ds(start, base - start + extra)] if base > start else vmem[names[0]]
        loads[names[0]] = pltpu.make_async_copy(target, target, load_sem.at[i])

    barrier = pltpu.get_barrier_semaphore()

    def greet(r, carry):
        peer = lax.rem(me + r, ndev)
        pl.semaphore_signal(
            barrier, inc=1, device_id=(peer // n_gy, lax.rem(peer, n_gy)), device_id_type=MESH
        )
        return carry

    with jax.named_scope("greet"):
        lax.fori_loop(1, ndev, greet, 0)

    def tile(name, part, i):
        group, place = places[name]
        row, depth = place["tiles"][part][i]
        return vmem[group][row : row + depth, :]

    def table(name, part):
        count = len(places[name][1]["tiles"][part])
        return jnp.concatenate([tile(name, part, i) for i in range(count)], axis=1)

    def right_mul(high, low, name):
        rows = high.shape[0]
        both = mm(jnp.concatenate([high, low], axis=0), table(name, 0))
        return both[:rows] + both[rows:] + mm(high, table(name, 1))

    def left_mul(name, high, low):
        group, place = places[name]
        row, rows, cols = place["left"]
        return mm(vmem[group][row : row + rows, 0:cols], jnp.concatenate([high, low, high], axis=0))

    groups = [[0, 1, 7, 6], [2, 3, 5, 4]]
    with jax.named_scope("signs"):
        z = lax.broadcasted_iota(jnp.int32, (n, 512), 0)
        at = lax.broadcasted_iota(jnp.int32, (n, 512), 1)
        odd = jnp.where((at // 128) % 2 == 1, -1.0, 1.0)
        base = jnp.where(z == at % 16, 1.0, 0.0) + jnp.where(z == 31 - at % 16, odd, 0.0)
        turned = jnp.where(at >= 256, -base, base)
        spot = (at // 16) % 8
        for side, value in ((0, base), (1, turned)):
            for y in range(8):
                rows = (side * 8 + y) * n
                match = spot == ((3 - y) % 8 if side else y)
                sign_ref[rows : rows + n] = jnp.where(match, value, 0.0).astype(jnp.bfloat16)

    with jax.named_scope("w_charge"):
        loads["charge"].wait()
        loads["compact"].wait()
    with jax.named_scope("grow"):
        same = lax.broadcasted_iota(jnp.int32, (16, 512), 0)
        same = jnp.where(lax.broadcasted_iota(jnp.int32, (16, 512), 1) % 16 == same, 1.0, 0.0)
        same = same.astype(jnp.bfloat16)
        for t in range(4):
            for i in range(16):
                line = jnp.broadcast_to(compact_ref[t * 16 + i : t * 16 + i + 1], (16, 512))
                grow_ref[t, i * 16 : (i + 1) * 16] = line.astype(jnp.bfloat16) * same
    with jax.named_scope("fold"):
        charge = vmem["charge"]
        sides = [
            jnp.concatenate([charge[:, v * 128 : (v + 1) * 128] for v in group], axis=1)
            for group in groups
        ]
        high, low = halves(jnp.concatenate(sides, axis=0))
        both = mm(jnp.concatenate([high, low], axis=0), sign_ref[...])
        parts = halves(both[: 2 * n] + both[2 * n :])
        lane = lax.broadcasted_iota(jnp.int32, (half, 128), 1)
        for k, part in enumerate(parts):
            for c in range(4):
                for side in range(2):
                    piece = part[side * n : (side + 1) * n, c * 128 : (c + 1) * 128]
                    rows = (2 * k + c % 2) * n
                    w_ref[c // 2, rows : rows + n, side * 128 : (side + 1) * 128] = piece
    with jax.named_scope("upy"):
        for p in range(2):
            both = mm(w_ref[p], grow_ref[2 * p])
            lift = both[: 2 * n] + both[2 * n :] + mm(w_ref[p, 0 : 2 * n], grow_ref[2 * p + 1])
            high, low = halves(lift)
            for q in range(2):
                for k in range(4):
                    at = (4 * p + k) * n
                    rows, lanes = slice(q * n, (q + 1) * n), slice(k * 128, (k + 1) * 128)
                    z_ref[q, at : at + n, 0:128] = high[rows, lanes]
                    z_ref[q, at : at + n, 128:256] = low[rows, lanes]
    with jax.named_scope("w_upz"):
        loads["upz"].wait()
    with jax.named_scope("upz"):
        for q in range(2):
            up = mm(z_ref[q], tile("fz%d" % q, 0, 0)) + mm(z_ref[q, :, 0:128], tile("gz%d" % q, 0, 0))
            high, low = halves(up)
            for k in range(8):
                rows, lanes = slice(k * n, (k + 1) * n), slice((8 * q + k) * 256, (8 * q + k + 1) * 256)
                x_ref[0:n, lanes] = high[rows]
                x_ref[n : 2 * n, lanes] = low[rows]
    with jax.named_scope("w_recip"):
        loads["recip"].wait()
    with jax.named_scope("upx"):
        group, place = places["sl"]
        row, rows, cols = place["left"]
        weights = vmem[group][row : row + rows, 0:cols]
        for q in range(2):
            lanes = slice(q * 2048, (q + 1) * 2048)
            spectrum = mm(
                weights, jnp.concatenate([x_ref[:, lanes], x_ref[0:n, lanes]], axis=0)
            )
            divisor = [
                vmem["recip"][(8 * q + k) * half : (8 * q + k + 1) * half] for k in range(8)
            ]
            high, low = halves(spectrum * jnp.concatenate(divisor, axis=1))
            s_ref[0:half, lanes] = high
            s_ref[half : 2 * half, lanes] = low

    def down(name, rows, b_ref, y_ref, finish):
        group, place = places[name]
        row, _, cols = place["left"]
        weights = vmem[group][row : row + rows, 0:cols]
        for q in range(2):
            lanes = slice(q * 2048, (q + 1) * 2048)
            stacked = jnp.concatenate([weights[:, 0:half], weights[:, 2 * half : 3 * half]], axis=0)
            short = mm(stacked, s_ref[0:half, lanes])
            short = short[:rows] + short[rows:] + mm(weights[:, 0:half], s_ref[half:, lanes])
            high, low = halves(short)
            for k in range(8):
                lanes = slice(k * 256, (k + 1) * 256)
                b_ref[q, k * rows : (k + 1) * rows] = high[:, lanes]
                b_ref[q, (8 + k) * rows : (9 + k) * rows] = low[:, lanes]
        for q in range(2):
            both = mm(b_ref[q], tile("bz%d" % q, 0, 0))
            block = 8 * rows
            high, low = halves(both[:block, :128] + both[block:, :128] + both[:block, 128:])
            for p in range(2):
                for k in range(4):
                    at, lanes = (4 * p + k) * rows, slice(k * 128, (k + 1) * 128)
                    y_ref[p, q * rows : (q + 1) * rows, lanes] = high[at : at + rows]
                    y_ref[p, (2 + q) * rows : (3 + q) * rows, lanes] = low[at : at + rows]
        ys = []
        finish()
        for p in range(2):
            both = mm(y_ref[p], tile("%sy%d" % ("b" if name == "means" else "c", p), 0, 0))
            both = both[: 2 * rows, :128] + both[2 * rows :, :128] + both[: 2 * rows, 128:]
            ys += [both[:rows], both[rows:]]
        return ys

    def arrive():
        loads["downy"].wait()

    with jax.named_scope("down"):
        y0, y1, y2, y3 = down("means", 16, b_ref, y_ref, arrive)
    with jax.named_scope("spread"):
        sample = jnp.concatenate(
            [jnp.where(lane[0:16] < 64, u, v) for u, v in ((y0, y1), (y2, y3))], axis=1
        )
        sample = halves(sample)
        sample_ref[0] = sample[0]
        sample_ref[1] = sample[1]
        spread = right_mul(*sample, "spread")
        bend = spread[:, modes:]
        gap = jnp.zeros((1, modes), jnp.float32)
        packet = spread[:, :modes] + 2.0 * bend
        packet = packet - jnp.concatenate([gap, bend[:-1]]) - jnp.concatenate([bend[1:], gap])
        mine = vmem["mine"]
        near_ref[n_gy + b] = packet
        rightward = jnp.sum(packet * mine[0:16], axis=0, keepdims=True)
        leftward = jnp.sum(packet * mine[16:32], axis=0, keepdims=True)
        for g in range(modes // 128):
            mom_ref[g, 0:1] = rightward[:, g * 128 : (g + 1) * 128]
            mom_ref[g, 1:2] = leftward[:, g * 128 : (g + 1) * 128]

    def remote(source, target, send, recv, device):
        return pltpu.make_async_remote_copy(
            src_ref=source,
            dst_ref=target,
            send_sem=send,
            recv_sem=recv,
            device_id=device,
            device_id_type=MESH,
        )

    def start_far(r, carry):
        d = n_gx - r
        for j in range(n_gy):
            for row, other, fine in ((0, a + d, a + d < n_gx), (1, a - d, a >= d)):

                @pl.when(fine)
                def _():
                    remote(
                        mom_ref.at[:, pl.ds(row, 1)],
                        far_ref.at[b, :, pl.ds(a, 1)],
                        f_send,
                        f_recv,
                        (other, j),
                    ).start()

        return carry

    early = a < n_gx // 8

    def send_far():
        with jax.named_scope("sendf"):
            lax.fori_loop(1, n_gx - 1, start_far, 0)

    def send_near():
        with jax.named_scope("send"):
            for step in (0, 1, 2):
                for j in range(n_gy):
                    other = a + step - 1
                    fine = (other >= 0) & (other < n_gx)
                    if step == 1:
                        fine = b != j

                    @pl.when(fine)
                    def _():
                        remote(
                            near_ref.at[n_gy + b],
                            near_ref.at[(2 - step) * n_gy + b],
                            p_send,
                            p_recv,
                            (other, j),
                        ).start()

    upper, lower = lax.rem(b + 1, n_gy), lax.rem(b + n_gy - 1, n_gy)
    def send_faces():
        with jax.named_scope("sendc"):

            @pl.when(a < n_gx - 1)
            def _():
                remote(
                    cx_ref.at[pl.ds(2, 1)], rx_ref.at[pl.ds(0, 1)], p_send, p_recv, (a + 1, b)
                ).start()

            @pl.when(a > 0)
            def _():
                remote(
                    cx_ref.at[pl.ds(1, 1)], rx_ref.at[pl.ds(1, 1)], p_send, p_recv, (a - 1, b)
                ).start()

            remote(cy_ref, ry_ref.at[0], p_send, p_recv, (a, upper)).start()
            remote(cy_ref, ry_ref.at[1], p_send, p_recv, (a, lower)).start()

    def turn(step, carry):
        @pl.when(step == last)
        def _():
            with jax.named_scope("barrier"):
                pl.semaphore_wait(barrier, ndev - 1)

            @pl.when(early)
            def _():
                send_faces()
                send_near()
                send_far()

            @pl.when(jnp.logical_not(early))
            def _():
                send_far()
                send_near()

        @pl.when(step != last)
        def _():
            with jax.named_scope("w_side"):
                loads["side"].wait()
            with jax.named_scope("lin"):
                y0, y1, y2, y3 = down("picks", 32, c_ref, d_ref, lambda: None)
                flat = right_mul(*halves(left_mul("flat", sample_ref[0], sample_ref[1])), "lin")
                cx = jnp.concatenate(
                    [
                        jnp.where(lane[0:8] < 64, pltpu.roll(u[0:8], 64, 1), v[0:8])
                        for u, v in ((y0, y1), (y2, y3))
                    ],
                    axis=1,
                )
                cx = cx - flat[0:8, 0:256]
                cy = jnp.where(lane[0:16] < 32, y0[16:] + y2[16:], y1[16:] + y3[16:])
                cy = cy - flat[16:32, 256:384]
                cx_ref[...] = cx
                cy_ref[...] = cy

            with jax.named_scope("near"):
                folded = [
                    jnp.concatenate(
                        [w_ref[c // 2, (2 * k + c % 2) * n : (2 * k + c % 2 + 1) * n] for c in range(4)],
                        axis=1,
                    )
                    for k in range(2)
                ]
                narrow = halves(left_mul("sn", *folded))
                spectrum = []
                for c in range(4):
                    at = slice(c * 256, (c + 1) * 256)
                    spectrum.append(right_mul(narrow[0][:, at], narrow[1][:, at], "near%d" % c))
                spec_ref[...] = jnp.concatenate(spectrum, axis=1)

        return carry

    last = jnp.where(early, 1, 0)
    lax.fori_loop(0, 2, turn, 0)

    @pl.when(jnp.logical_not(early))
    def _():
        send_faces()

    edge = (a == 0) | (a == n_gx - 1)
    inner = jnp.logical_not(edge)

    def settle_near(sides):
        lines = 16 * (modes // 128) * ((1 + sides) * n_gy - 1) + 2 * sides + 32
        block = tally_ref.at[pl.ds(0, lines)]
        remote(block, block, p_send, p_recv, (a, b)).wait()

    with jax.named_scope("wait_p"):

        @pl.when(edge)
        def _():
            settle_near(1)

        @pl.when(inner)
        def _():
            settle_near(2)

    with jax.named_scope("face"):
        cx, cy, spectrum = cx_ref[...], cy_ref[...], spec_ref[...]
        from_left = jnp.where(a > 0, rx_ref[0:1], 0.0)
        from_right = jnp.where(a < n_gx - 1, rx_ref[1:2], 0.0)
        ends = jnp.concatenate(
            [cx[0:1] + from_left, cx[3:4] + from_right, jnp.zeros((14, cx.shape[1]), jnp.float32)]
        )
        ends = right_mul(*halves(ends), "facex")
        fine = 16 * half
        column = vmem["recip"][fine + 4 * n : fine + 5 * n, 0:2]
        spectrum = spectrum + column[:, 0:1] * ends[0:1] + column[:, 1:2] * ends[1:2]
        group = jnp.where(lane[0:16] < 64, lax.rem(lane[0:16], 32) // 8, 4)
        total = jnp.where((group == 0) | (group == 3), cy, 0.0)
        total = total + jnp.where((group == 2) & (b > 0), ry_ref[0], 0.0)
        total = total + jnp.where((group == 1) & (b < n_gy - 1), ry_ref[1], 0.0)
        total = left_mul("sb", *halves(total))[:, 0:64]
        spectrum = spectrum + right_mul(*halves(total), "facey")
    with jax.named_scope("green"):
        row = lax.broadcasted_iota(jnp.int32, (8, modes), 0)

        def gathered(step):
            value = near_ref[step * n_gy]
            for j in range(1, n_gy):
                value = value + near_ref[step * n_gy + j]
            return value

        past = jnp.where(a > 0, gathered(0), 0.0)
        here = gathered(1)
        next_ = jnp.where(a < n_gx - 1, gathered(2), 0.0)
        source = jnp.concatenate(
            [
                jnp.where((row >= 4) | (a > 1), past[0:8], 0.0),
                past[8:16] + jnp.where((row >= 4) | (a > 0), here[0:8], 0.0),
                jnp.where((row < 4) | (a < n_gx - 1), here[8:16] + next_[0:8], 0.0),
                jnp.where((row < 4) | (a < n_gx - 2), next_[8:16], 0.0),
            ]
        )
        values = []
        for i in range(cells + 2):
            influence = mine[169 - i : 201 - i] - mine[208 + i : 240 + i]
            values.append(jnp.sum(influence * source, axis=0, keepdims=True))
        values.append(jnp.zeros((16 - len(values), modes), jnp.float32))
        lifted = left_mul("u12", *halves(jnp.concatenate(values, axis=0)))

    inverse = jnp.concatenate(
        [vmem["recip"][fine + c * n : fine + (c + 1) * n] for c in range(4)], axis=1
    )

    def unfolded(parts):
        sides = [
            jnp.concatenate([part[:, s * 128 : (s + 1) * 128] for part in parts], axis=1)
            for s in range(2)
        ]
        return jnp.concatenate(sides, axis=0)

    def cells_of(both):
        for s, group in enumerate(groups):
            for i, v in enumerate(group):
                yield v, both[s * n : (s + 1) * n, i * 128 : (i + 1) * 128]

    with jax.named_scope("base"):
        lifted = halves(jnp.concatenate([lifted[:n], lifted[n:]], axis=1))
        spectrum = (spectrum + right_mul(*lifted, "drop")) * inverse
        high, low = halves(left_mul("sn", *halves(spectrum)))
        parts = []
        for c in range(4):
            at = slice(c * 256, (c + 1) * 256)
            parts.append(right_mul(high[:, at], low[:, at], "far%d" % c))
        high, low = halves(unfolded(parts))
        both = mm(jnp.concatenate([high, low], axis=0), table("unfold", 0))
        for v, value in cells_of(both[: 2 * n] + both[2 * n :]):
            out_ref[:, v * 128 : (v + 1) * 128] = value

    def settle_far(each):
        block = far_ref.at[:, :, pl.ds(0, each)]
        remote(block, block, f_send, f_recv, (a, b)).wait()

    with jax.named_scope("wait_f"):

        @pl.when(edge)
        def _():
            settle_far(n_gx - 2)

        @pl.when(inner)
        def _():
            settle_far(n_gx - 3)

    with jax.named_scope("final"):
        origin = lax.broadcasted_iota(jnp.int32, (n_gx, modes), 0)
        before = jnp.zeros((n_gx, modes), jnp.float32)
        after = before
        for j in range(n_gy):
            sent = jnp.concatenate([far_ref[j, g] for g in range(modes // 128)], axis=1)
            before = before + jnp.where(origin <= a - 2, sent, 0.0)
            after = after + jnp.where(origin >= a + 2, sent, 0.0)
        before = jnp.sum(before * mine[256 : 256 + n_gx], axis=0, keepdims=True)
        after = jnp.sum(after * mine[256 + n_gx : 256 + 2 * n_gx], axis=0, keepdims=True)
        lifted = mine[32:96] * before + mine[96:160] * after
        lifted = jnp.concatenate([lifted[:n], lifted[n:]], axis=1).astype(jnp.bfloat16)
        spectrum = (mm(lifted, table("drop", 0)) * inverse).astype(jnp.bfloat16)
        group, place = places["sn"]
        row, rows, _ = place["left"]
        spectrum = mm(vmem[group][row : row + rows, 0:n], spectrum).astype(jnp.bfloat16)
        parts = [mm(spectrum[:, c * 256 : (c + 1) * 256], tile("far%d" % c, 0, 0)) for c in range(4)]
    with jax.named_scope("unfold"):
        both = mm(unfolded(parts).astype(jnp.bfloat16), table("unfold", 0))
        for v, value in cells_of(both):
            at = slice(v * 128, (v + 1) * 128)
            out_ref[:, at] = out_ref[:, at] + value


def emit(in_ref, out_ref, sem):
    copy = pltpu.make_async_copy(in_ref, out_ref, sem)
    copy.start()
    copy.wait()


def body(n_gx, n_gy, charge):
    singles, places = tables(n_gx, n_gy)
    arrays = [charge] + [jnp.asarray(singles[name]) for name in NAMES[1:]]
    shapes = {name: window(name, array.shape) for name, array in zip(NAMES, arrays)}
    total = sum(shapes[name][0] for name in GROUPS)
    scratch = [pltpu.VMEM(shapes[name], jnp.float32) for name in ("charge", "compact", "recip", "mine")]
    scratch.append(pltpu.VMEM((total, 256), jnp.bfloat16))
    modes = n_gy * (P_SIZE // Q) ** 2
    half = P_SIZE + 2 * W
    scratch += [
        pltpu.VMEM((512, 512), jnp.bfloat16),
        pltpu.VMEM((4, 256, 512), jnp.bfloat16),
        pltpu.VMEM((2, 16, 256), jnp.bfloat16),
        pltpu.VMEM((P_SIZE, 1024), jnp.float32),
        pltpu.VMEM((2, 4 * P_SIZE, 256), jnp.bfloat16),
        pltpu.VMEM((2, 8 * P_SIZE, 256), jnp.bfloat16),
        pltpu.VMEM((2 * P_SIZE, 4096), jnp.bfloat16),
        pltpu.VMEM((2 * half, 4096), jnp.bfloat16),
        pltpu.VMEM((2, 256, 256), jnp.bfloat16),
        pltpu.VMEM((2, 64, 512), jnp.bfloat16),
        pltpu.VMEM((2, 512, 256), jnp.bfloat16),
        pltpu.VMEM((2, 128, 512), jnp.bfloat16),
        pltpu.VMEM((modes // 128, 8, 128), jnp.float32),
        pltpu.VMEM((n_gy, modes // 128, n_gx, 128), jnp.float32),
        pltpu.VMEM((3 * n_gy, 16, modes), jnp.float32),
        pltpu.VMEM((8, 256), jnp.float32),
        pltpu.VMEM((16, 128), jnp.float32),
        pltpu.VMEM((8, 256), jnp.float32),
        pltpu.VMEM((2, 16, 128), jnp.float32),
        pltpu.VMEM((16 * (modes // 128) * (3 * n_gy - 1) + 40, 128), jnp.float32),
        pltpu.SemaphoreType.DMA((len(WAITS),)),
        pltpu.SemaphoreType.DMA,
        pltpu.SemaphoreType.DMA,
        pltpu.SemaphoreType.DMA,
        pltpu.SemaphoreType.DMA,
    ]
    hbm = pl.BlockSpec(memory_space=pl.ANY)
    vm = pl.BlockSpec(memory_space=pltpu.VMEM)
    solved = pl.pallas_call(
        functools.partial(kernel, places, n_gx, n_gy),
        out_shape=pltpu.VMEM(charge.shape, charge.dtype),
        in_specs=[hbm] * len(NAMES),
        out_specs=vm,
        scratch_shapes=scratch,
        name="mlc",
        compiler_params=pltpu.CompilerParams(
            collective_id=0, has_side_effects=True, vmem_limit_bytes=60 * 1024 * 1024
        ),
    )(*arrays)
    return pl.pallas_call(
        emit,
        out_shape=jax.ShapeDtypeStruct(charge.shape, charge.dtype),
        in_specs=[vm],
        out_specs=hbm,
        scratch_shapes=[pltpu.SemaphoreType.DMA],
        name="emit",
        compiler_params=pltpu.CompilerParams(vmem_limit_bytes=1024 * 1024),
    )(solved)


def solution(mesh):
    run = functools.partial(body, mesh.shape["gx"], mesh.shape["gy"])
    spec = P("gx", "gy")
    return jax.shard_map(run, mesh=mesh, in_specs=(spec,), out_specs=spec, check_vma=False)
```

```python
import functools

import jax
import jax.numpy as jnp
import ml_dtypes
import numpy as np
from jax import lax
from jax.experimental import pallas as pl
from jax.experimental.pallas import tpu as pltpu
from jax.sharding import PartitionSpec as P

P_SIZE = 32
W = 16
Q = 4
NL = 16
CLASSES = [(0, 0), (0, 1), (1, 0), (1, 1)]
MESH = pl.DeviceIdType.MESH


def sine_table(length):
    counter = np.arange(length) + 1
    return np.sin(np.pi * np.outer(counter, counter) / (length + 1))


def eigen_values(length):
    return 2.0 - 2.0 * np.cos(np.pi * (np.arange(length) + 1) / (length + 1))


def interp_table(fine_start, fine_count, coarse_start, coarse_count, ratio):
    fine_pos = np.arange(fine_count) + fine_start
    coarse_pos = np.arange(coarse_count) + coarse_start
    numerator = 2 * fine_pos - (ratio - 1)
    lower = numerator // (2 * ratio)
    weight = ((numerator - 2 * ratio * lower) / (2 * ratio))[:, None]
    below = coarse_pos[None, :] == lower[:, None]
    above = coarse_pos[None, :] == lower[:, None] + 1
    return below * (1.0 - weight) + above * weight


def legendre_basis(length, count):
    points = (2.0 * np.arange(length) + 1.0) / length - 1.0
    columns = [np.ones_like(points), points]
    for degree in range(2, count):
        columns.append(
            ((2 * degree - 1) * points * columns[-1] - (degree - 1) * columns[-2]) / degree
        )
    result = []
    for vector in columns[:count]:
        for passes in range(2):
            for earlier in result:
                vector = vector - np.sum(earlier * vector) * earlier
        result.append(vector / np.sqrt(np.sum(vector * vector)))
    return np.stack(result, axis=1)


def fold(length):
    half = length // 2
    eye = np.eye(length)
    return np.concatenate([eye[:half] + eye[::-1][:half], eye[:half] - eye[::-1][:half]])


def split(table):
    high = table.astype(ml_dtypes.bfloat16)
    low = (table - high.astype(np.float64)).astype(ml_dtypes.bfloat16)
    return high, low


@functools.lru_cache(maxsize=None)
def tables(n_gx, n_gy):
    n, length, cells = P_SIZE, P_SIZE + 2 * W, P_SIZE // Q
    blocks, margin = length // Q, W // Q
    half, hl, hb, hn = n // 2, length // 2, blocks // 2, NL // 2
    quad, wide = hb * hb, hn * hn
    nx, ny, nz = n_gx * cells, n_gy * cells, cells
    modes = ny * nz
    s_l, s_n = sine_table(length), sine_table(n)
    u_n, u_b = fold(n), fold(blocks)
    basis = legendre_basis(n, NL)
    average = np.kron(np.eye(blocks), np.full((1, Q), 1.0 / Q))
    fine = interp_table(0, length, 0, blocks, Q)
    middle = fine[W : W + n]
    picks = [W - 1, W, W + n - 1, W + n]
    a_full = average @ s_l
    b_full = basis.T @ s_l[W : W + n]
    order = np.arange(4 * NL).reshape(4, hn, 2).transpose(2, 0, 1).ravel()
    big = {}

    folding = np.zeros((4, 4, n, 4, 2 * 4, half))
    for c, (p, q) in enumerate(CLASSES):
        for vi in range(4):
            for y4 in range(4):
                il = [y4, 4 + y4, 3 - y4, 7 - y4][vi]
                sign = -1.0 if vi > 1 and p == 1 else 1.0
                folding[vi, y4, :, c, il, :] = sign * u_n[q * half : (q + 1) * half].T
    folding = folding.reshape(4 * 128, 4 * 128)
    plain = {"unfold": folding.T}

    inner = s_l[:, W : W + n] @ u_n.T / 2
    f1 = [inner[p::2, p * half : (p + 1) * half] for p in (0, 1)]
    a1 = [(u_b @ a_full)[p * hb : (p + 1) * hb, p::2] for p in (0, 1)]
    b1 = [b_full[p::2, p::2] for p in (0, 1)]
    keep, pick = np.eye(hb), np.concatenate([np.zeros((hn, hb)), np.eye(hn)], axis=1)
    keep = np.concatenate([keep, np.zeros((hb, hn))], axis=1)
    compact = []
    for p in (0, 1):
        for part in split(np.repeat(f1[p].T, half, axis=1)):
            compact.append(part.astype(np.float32))
        high, low = split(np.kron(np.eye(8), f1[p].T))
        plain["fz%d" % p] = np.concatenate([high, high])
        plain["gz%d" % p] = low
        plain["bz%d" % p] = np.concatenate(
            split(np.kron(np.eye(8), np.concatenate([a1[p], b1[p]]).T)), axis=1
        )
        sample = np.kron(a1[p], keep).T
        slab = np.kron(s_l[picks][:, p::2], pick).T
        plain["by%d" % p] = np.concatenate(split(np.concatenate([sample, sample], axis=1)), axis=1)
        plain["cy%d" % p] = np.concatenate(
            split(np.concatenate([slab, slab, np.kron(b1[p], pick).T], axis=1)), axis=1
        )

    unfold = u_b.T / 2
    pair = np.kron(unfold, unfold).reshape(blocks * blocks, 2, hb, 2, hb)

    def from_samples(table):
        folded = np.einsum("os,spaqb->pqabo", table, pair)
        return folded.reshape(4 * quad, table.shape[0])

    bm = basis.T @ middle
    lin_x = from_samples(np.kron(bm, bm)).reshape(4 * quad, NL, NL)
    lin = np.zeros((4 * quad, 384))
    for c, (p, q) in enumerate(CLASSES):
        lin[:, c * wide : (c + 1) * wide] = lin_x[:, p::2, q::2].reshape(4 * quad, wide)
    lin[:, 256:320] = from_samples(np.kron(fine[picks], bm))[:, order]
    big["lin"] = lin
    k1 = [(s_n @ u_n.T / 2)[p::2, p * half : (p + 1) * half] for p in (0, 1)]
    for c, (p, q) in enumerate(CLASSES):
        big["near%d" % c] = np.kron(k1[p], k1[q]).T
    r1 = [(u_n @ s_n / 2)[p * half : (p + 1) * half, p::2] for p in (0, 1)]
    for c, (p, q) in enumerate(CLASSES):
        big["far%d" % c] = np.kron(r1[p], r1[q]).T

    second = 2 * np.eye(blocks) - np.eye(blocks, k=1) - np.eye(blocks, k=-1)
    s_y, s_z = sine_table(ny), sine_table(nz)
    proj_z = np.zeros((nz, blocks))
    proj_z[:, margin : margin + cells] = s_z
    edge = interp_table(-1, n + 2, -1, cells + 2, Q)
    depth = interp_table(0, n, 0, cells, Q)
    lateral = edge[1 : n + 1]
    s_ext = np.zeros((ny + 2, ny))
    s_ext[1:-1] = s_y
    sp = np.concatenate([s_n[0::2], s_n[1::2]])
    deep = sp @ depth @ s_z

    def by_class(first, second_table):
        parts = []
        for p, q in CLASSES:
            parts.append(
                np.kron(first[p * half : (p + 1) * half], second_table[q * half : (q + 1) * half])
            )
        return np.concatenate(parts).T

    factor = (2.0 / (ny + 1)) * (2.0 / (nz + 1))
    spread, drop = [], []
    for b in range(n_gy):
        proj_y = np.zeros((ny, blocks))
        for j in range(blocks):
            at = j + b * cells - margin
            if 0 <= at < ny:
                proj_y[:, j] = s_y[:, at]
        flat = np.kron(proj_y, proj_z)
        curved = np.kron(proj_y @ second, proj_z) + np.kron(proj_y, proj_z @ second)
        spread.append(
            factor * np.concatenate([from_samples(curved), from_samples(flat)], axis=1)
        )
        local_s = s_ext[b * cells : b * cells + cells + 2]
        rim = np.outer(sp[:, 0], edge[0] @ local_s) + np.outer(sp[:, n - 1], edge[n + 1] @ local_s)
        drop.append(
            np.concatenate([by_class(sp @ lateral @ local_s, deep), by_class(rim, deep)])
        )
    big["spread"] = np.stack(spread)
    big["drop"] = np.stack(drop)
    sb = s_n @ basis
    sbp = np.concatenate([sb[0::2], sb[1::2]])
    facex = np.zeros((4 * wide, n * n))
    for c, (p, q) in enumerate(CLASSES):
        facex[c * wide : (c + 1) * wide, c * 256 : c * 256 + 256] = np.kron(
            sb[p::2, p::2], sb[q::2, q::2]
        ).T
    big["facex"] = facex
    ends = np.stack([sp[:, 0], sp[:, n - 1], sp[:, 0], sp[:, n - 1]], axis=1)
    big["facey"] = by_class(ends, sbp)[order]

    mu_y, mu_z = eigen_values(ny), eigen_values(nz)
    theta = np.arccosh(1.0 + (mu_y[:, None] + mu_z[None, :]).reshape(1, modes) / 2)
    below = 2 * np.sinh(theta) * (1.0 - np.exp(-2 * theta * (nx + 1)))
    apart = np.abs(np.arange(48) - 20)[:, None]
    toep = (np.exp(-theta * apart) + np.exp(-theta * np.maximum(2 * (nx + 1) - apart, 0))) / below
    total = (np.arange(2 * nx + 32) - 13)[:, None]
    hank = np.exp(-theta * np.maximum(total + 2, 0)) + np.exp(-theta * np.maximum(2 * nx - total, 0))
    hank = hank / below

    u12 = np.zeros((64, 16))
    u12[:32, :10] = np.outer(s_n[:, 0], edge[0]) + np.outer(s_n[:, n - 1], edge[n + 1])
    u12[32:, :10] = s_n @ lateral
    place = np.arange(n_gx)
    mine = []
    for a in range(n_gx):
        rank = np.arange(16)[:, None]
        at = cells * a - margin + rank
        inside = (at >= 0) & (at < nx)
        rightward = inside * np.exp(-theta * (15 - rank)) * (1 - np.exp(-2 * theta * (at + 1) * inside))
        leftward = inside * np.exp(-theta * rank) * (1 - np.exp(-2 * theta * (nx - at) * inside))
        row = np.arange(16)[:, None]
        x = cells * a - 1 + row
        used = row < cells + 2
        falling = used * np.exp(-theta * row) * (1 - np.exp(-2 * theta * np.maximum(nx - x, 0))) / below
        rising = (
            used
            * np.exp(-theta * np.maximum(cells + 1 - row, 0))
            * (1 - np.exp(-2 * theta * (x + 1)))
            / below
        )
        away = (a - place)[:, None]
        before = (away >= 2) * np.exp(-theta * np.maximum(cells * away - 12, 0))
        after = (away <= -2) * np.exp(-theta * np.maximum(-cells * away - 12, 0))
        mine.append(
            np.concatenate(
                [
                    rightward,
                    leftward,
                    u12 @ falling,
                    u12 @ rising,
                    toep,
                    hank[2 * cells * a : 2 * cells * a + 48],
                    before,
                    after,
                ]
            )
        )
    mu_l, mu_n = eigen_values(length), eigen_values(n)
    reciprocal = []
    for q in (0, 1):
        for p in (0, 1):
            pair_sum = (mu_l[p::2][:, None] + mu_l[q::2][None, :]).reshape(1, hl * hl)
            table = 1.0 / (mu_l[:, None] + pair_sum)
            reciprocal.append(table.reshape(length, 4, 256).transpose(1, 0, 2).reshape(-1, 256))
    for p, q in CLASSES:
        pair_sum = (mu_n[p::2][:, None] + mu_n[q::2][None, :]).reshape(1, 256)
        reciprocal.append((2.0 / (n + 1)) ** 3 / (mu_n[:, None] + pair_sum))
    ends = np.zeros((n, 256))
    ends[:, :2] = s_n[:, [0, n - 1]]
    reciprocal.append(ends)

    scale = (2.0 / (length + 1)) ** 3
    blank = np.zeros((12, length))
    lefts = {
        "sl": s_l[:, W : W + n],
        "means": a_full * scale,
        "flat": np.concatenate([fine[picks], blank[:, :blocks], bm]),
        "picks": np.concatenate([s_l[picks], blank, b_full]) * scale,
        "sn": s_n,
        "u12": u12,
        "sb": sb,
    }
    for name, value in lefts.items():
        high, low = split(value)
        plain[name] = np.concatenate([high, high, low], axis=1)
    singles = {
        "mine": np.stack(mine).astype(np.float32),
        "recip": np.concatenate(reciprocal).astype(np.float32),
        "compact": np.concatenate(compact),
    }
    places = {}
    for group, names in GROUPS.items():
        packs, row = [], 0
        for name in names:
            if name in plain:
                parts = [plain[name].astype(ml_dtypes.bfloat16)]
            else:
                parts = split(big[name])
            depth, width = parts[0].shape[-2:]
            place = {"left": (row, depth, width)}
            step = 256
            tiles = []
            for part in parts:
                for at in range(0, width, step):
                    tile = np.zeros(part.shape[:-1] + (256,), ml_dtypes.bfloat16)
                    piece = part[..., at : at + step]
                    tile[..., : piece.shape[-1]] = piece
                    packs.append(tile)
                    tiles.append((row, depth))
                    row += depth
            count = len(tiles) // len(parts)
            place["tiles"] = [tiles[k * count : (k + 1) * count] for k in range(len(parts))]
            places[name] = (group, place)
        most = max(tile.ndim for tile in packs)
        if most == 3:
            packs = [np.broadcast_to(tile, (n_gy,) + tile.shape[-2:]) for tile in packs]
        singles[group] = np.concatenate(packs, axis=-2)
    return singles, places


GROUPS = {
    "upz": ["fz0", "gz0", "fz1", "gz1", "sl", "means", "bz0", "bz1"],
    "downy": ["by0", "by1"],
    "spread": ["spread"],
    "side": ["picks", "flat", "sn", "sb", "u12", "lin", "cy0", "cy1"]
    + ["near%d" % c for c in range(4)]
    + ["facex", "facey"],
    "drop": ["drop"],
    "last": ["far%d" % c for c in range(4)] + ["unfold"],
}
NAMES = [
    "charge", "compact", "upz", "recip", "downy", "spread", "mine", "side", "drop", "last",
]
WAITS = [
    ["charge"], ["compact"], ["upz"], ["recip"], ["downy", "spread", "mine"],
    ["side", "drop", "last"],
]
CUTS = {"charge": 4, "compact": 4}


def halves(value):
    high = value.astype(jnp.bfloat16)
    return high, (value - high.astype(jnp.float32)).astype(jnp.bfloat16)


def mm(left, right):
    return jnp.dot(left, right, preferred_element_type=jnp.float32)


def window(name, shape):
    return shape[1:] if name in ("spread", "drop", "mine") else shape


def kernel(places, n_gx, n_gy, *refs):
    count = len(NAMES)
    hbm = dict(zip(NAMES, refs[:count]))
    out_ref = refs[count]
    charge_ref, compact_ref, recip_ref, mine_ref, tables_ref = refs[count + 1 : count + 6]
    vmem = {"charge": charge_ref, "compact": compact_ref, "recip": recip_ref, "mine": mine_ref}
    (
        sign_ref, grow_ref, sample_ref, spec_ref, w_ref, z_ref, x_ref, s_ref, b_ref, y_ref, c_ref, d_ref,
        mom_ref, far_ref, near_ref, cx_ref, cy_ref, rx_ref, ry_ref, tally_ref,
        load_sem, f_send, f_recv, p_send, p_recv,
    ) = refs[count + 6 :]
    ndev = n_gx * n_gy
    a = lax.axis_index("gx")
    b = lax.axis_index("gy")
    me = a * n_gy + b
    n, cells = P_SIZE, P_SIZE // Q
    half = n + 2 * W
    modes = near_ref.shape[-1]

    loads, base = {}, 0
    for i, names in enumerate(WAITS):
        start = base
        for name in names:
            source = hbm[name]
            if name in ("spread", "drop"):
                source = source.at[b]
            if name == "mine":
                source = source.at[a]
            if name in GROUPS:
                rows = source.shape[0]
                vmem[name] = tables_ref.at[pl.ds(base, rows)]
                base += rows
            cuts = CUTS.get(name, 1)
            each = source.shape[0] // cuts
            for k in range(cuts):
                part = pl.ds(k * each, each)
                pltpu.make_async_copy(
                    source.at[part], vmem[name].at[part], load_sem.at[i]
                ).start()
        extra = 2 * vmem["mine"].shape[0] * modes // 256 if "mine" in names else 0
        target = tables_ref.at[pl.ds(start, base - start + extra)] if base > start else vmem[names[0]]
        loads[names[0]] = pltpu.make_async_copy(target, target, load_sem.at[i])

    barrier = pltpu.get_barrier_semaphore()

    def greet(r, carry):
        peer = lax.rem(me + r, ndev)
        pl.semaphore_signal(
            barrier, inc=1, device_id=(peer // n_gy, lax.rem(peer, n_gy)), device_id_type=MESH
        )
        return carry

    with jax.named_scope("greet"):
        lax.fori_loop(1, ndev, greet, 0)

    def tile(name, part, i):
        group, place = places[name]
        row, depth = place["tiles"][part][i]
        return vmem[group][row : row + depth, :]

    def table(name, part):
        count = len(places[name][1]["tiles"][part])
        return jnp.concatenate([tile(name, part, i) for i in range(count)], axis=1)

    def right_mul(high, low, name):
        rows = high.shape[0]
        both = mm(jnp.concatenate([high, low], axis=0), table(name, 0))
        return both[:rows] + both[rows:] + mm(high, table(name, 1))

    def left_mul(name, high, low):
        group, place = places[name]
        row, rows, cols = place["left"]
        return mm(vmem[group][row : row + rows, 0:cols], jnp.concatenate([high, low, high], axis=0))

    groups = [[0, 1, 7, 6], [2, 3, 5, 4]]
    with jax.named_scope("signs"):
        z = lax.broadcasted_iota(jnp.int32, (n, 512), 0)
        at = lax.broadcasted_iota(jnp.int32, (n, 512), 1)
        odd = jnp.where((at // 128) % 2 == 1, -1.0, 1.0)
        base = jnp.where(z == at % 16, 1.0, 0.0) + jnp.where(z == 31 - at % 16, odd, 0.0)
        turned = jnp.where(at >= 256, -base, base)
        spot = (at // 16) % 8
        for side, value in ((0, base), (1, turned)):
            for y in range(8):
                rows = (side * 8 + y) * n
                match = spot == ((3 - y) % 8 if side else y)
                sign_ref[rows : rows + n] = jnp.where(match, value, 0.0).astype(jnp.bfloat16)

    with jax.named_scope("w_charge"):
        loads["charge"].wait()
        loads["compact"].wait()
    with jax.named_scope("grow"):
        same = lax.broadcasted_iota(jnp.int32, (16, 512), 0)
        same = jnp.where(lax.broadcasted_iota(jnp.int32, (16, 512), 1) % 16 == same, 1.0, 0.0)
        same = same.astype(jnp.bfloat16)
        for t in range(4):
            for i in range(16):
                line = jnp.broadcast_to(compact_ref[t * 16 + i : t * 16 + i + 1], (16, 512))
                grow_ref[t, i * 16 : (i + 1) * 16] = line.astype(jnp.bfloat16) * same
    with jax.named_scope("fold"):
        charge = vmem["charge"]
        sides = [
            jnp.concatenate([charge[:, v * 128 : (v + 1) * 128] for v in group], axis=1)
            for group in groups
        ]
        high, low = halves(jnp.concatenate(sides, axis=0))
        both = mm(jnp.concatenate([high, low], axis=0), sign_ref[...])
        parts = halves(both[: 2 * n] + both[2 * n :])
        lane = lax.broadcasted_iota(jnp.int32, (half, 128), 1)
        for k, part in enumerate(parts):
            for c in range(4):
                for side in range(2):
                    piece = part[side * n : (side + 1) * n, c * 128 : (c + 1) * 128]
                    rows = (2 * k + c % 2) * n
                    w_ref[c // 2, rows : rows + n, side * 128 : (side + 1) * 128] = piece
    with jax.named_scope("upy"):
        for p in range(2):
            both = mm(w_ref[p], jnp.concatenate([grow_ref[2 * p], grow_ref[2 * p + 1]], axis=1))
            lift = both[: 2 * n, :512] + both[2 * n :, :512] + both[: 2 * n, 512:]
            high, low = halves(lift)
            for q in range(2):
                for k in range(4):
                    at = (4 * p + k) * n
                    rows, lanes = slice(q * n, (q + 1) * n), slice(k * 128, (k + 1) * 128)
                    z_ref[q, at : at + n, 0:128] = high[rows, lanes]
                    z_ref[q, at : at + n, 128:256] = low[rows, lanes]
    with jax.named_scope("w_upz"):
        loads["upz"].wait()
    with jax.named_scope("upz"):
        for q in range(2):
            up = mm(z_ref[q], tile("fz%d" % q, 0, 0)) + mm(z_ref[q, :, 0:128], tile("gz%d" % q, 0, 0))
            high, low = halves(up)
            for k in range(8):
                rows, lanes = slice(k * n, (k + 1) * n), slice((8 * q + k) * 256, (8 * q + k + 1) * 256)
                x_ref[0:n, lanes] = high[rows]
                x_ref[n : 2 * n, lanes] = low[rows]
    with jax.named_scope("w_recip"):
        loads["recip"].wait()
    with jax.named_scope("upx"):
        group, place = places["sl"]
        row, rows, cols = place["left"]
        weights = vmem[group][row : row + rows, 0:cols]
        for q in range(2):
            lanes = slice(q * 2048, (q + 1) * 2048)
            spectrum = mm(
                weights, jnp.concatenate([x_ref[:, lanes], x_ref[0:n, lanes]], axis=0)
            )
            divisor = [
                vmem["recip"][(8 * q + k) * half : (8 * q + k + 1) * half] for k in range(8)
            ]
            high, low = halves(spectrum * jnp.concatenate(divisor, axis=1))
            s_ref[0:half, lanes] = high
            s_ref[half : 2 * half, lanes] = low

    def down(name, rows, b_ref, y_ref, finish):
        group, place = places[name]
        row, _, cols = place["left"]
        weights = vmem[group][row : row + rows, 0:cols]
        for q in range(2):
            lanes = slice(q * 2048, (q + 1) * 2048)
            stacked = jnp.concatenate([weights[:, 0:half], weights[:, 2 * half : 3 * half]], axis=0)
            short = mm(stacked, s_ref[0:half, lanes])
            short = short[:rows] + short[rows:] + mm(weights[:, 0:half], s_ref[half:, lanes])
            high, low = halves(short)
            for k in range(8):
                lanes = slice(k * 256, (k + 1) * 256)
                b_ref[q, k * rows : (k + 1) * rows] = high[:, lanes]
                b_ref[q, (8 + k) * rows : (9 + k) * rows] = low[:, lanes]
        for q in range(2):
            both = mm(b_ref[q], tile("bz%d" % q, 0, 0))
            block = 8 * rows
            high, low = halves(both[:block, :128] + both[block:, :128] + both[:block, 128:])
            for p in range(2):
                for k in range(4):
                    at, lanes = (4 * p + k) * rows, slice(k * 128, (k + 1) * 128)
                    y_ref[p, q * rows : (q + 1) * rows, lanes] = high[at : at + rows]
                    y_ref[p, (2 + q) * rows : (3 + q) * rows, lanes] = low[at : at + rows]
        ys = []
        finish()
        for p in range(2):
            both = mm(y_ref[p], tile("%sy%d" % ("b" if name == "means" else "c", p), 0, 0))
            both = both[: 2 * rows, :128] + both[2 * rows :, :128] + both[: 2 * rows, 128:]
            ys += [both[:rows], both[rows:]]
        return ys

    def arrive():
        loads["downy"].wait()

    with jax.named_scope("down"):
        y0, y1, y2, y3 = down("means", 16, b_ref, y_ref, arrive)
    with jax.named_scope("spread"):
        sample = jnp.concatenate(
            [jnp.where(lane[0:16] < 64, u, v) for u, v in ((y0, y1), (y2, y3))], axis=1
        )
        sample = halves(sample)
        sample_ref[0] = sample[0]
        sample_ref[1] = sample[1]
        spread = right_mul(*sample, "spread")
        bend = spread[:, modes:]
        gap = jnp.zeros((1, modes), jnp.float32)
        packet = spread[:, :modes] + 2.0 * bend
        packet = packet - jnp.concatenate([gap, bend[:-1]]) - jnp.concatenate([bend[1:], gap])
        mine = vmem["mine"]
        rightward = jnp.sum(packet * mine[0:16], axis=0, keepdims=True)
        leftward = jnp.sum(packet * mine[16:32], axis=0, keepdims=True)
        for g in range(modes // 128):
            mom_ref[g, 0:1] = rightward[:, g * 128 : (g + 1) * 128]
            mom_ref[g, 1:2] = leftward[:, g * 128 : (g + 1) * 128]
        near_ref[n_gy + b] = packet

    def remote(source, target, send, recv, device):
        return pltpu.make_async_remote_copy(
            src_ref=source,
            dst_ref=target,
            send_sem=send,
            recv_sem=recv,
            device_id=device,
            device_id_type=MESH,
        )

    def start_far(r, carry):
        d = n_gx - r
        for j in range(n_gy):
            for row, other, fine in ((0, a + d, a + d < n_gx), (1, a - d, a >= d)):

                @pl.when(fine)
                def _():
                    remote(
                        mom_ref.at[:, pl.ds(row, 1)],
                        far_ref.at[b, :, pl.ds(a, 1)],
                        f_send,
                        f_recv,
                        (other, j),
                    ).start()

        return carry

    early = a < n_gx // 8

    def send_far():
        with jax.named_scope("sendf"):
            lax.fori_loop(1, n_gx - 1, start_far, 0)

    def send_near():
        with jax.named_scope("send"):
            for step in (0, 1, 2):
                for j in range(n_gy):
                    other = a + step - 1
                    fine = (other >= 0) & (other < n_gx)
                    if step == 1:
                        fine = b != j

                    @pl.when(fine)
                    def _():
                        remote(
                            near_ref.at[n_gy + b],
                            near_ref.at[(2 - step) * n_gy + b],
                            p_send,
                            p_recv,
                            (other, j),
                        ).start()

    upper, lower = lax.rem(b + 1, n_gy), lax.rem(b + n_gy - 1, n_gy)
    def send_faces():
        with jax.named_scope("sendc"):

            @pl.when(a < n_gx - 1)
            def _():
                remote(
                    cx_ref.at[pl.ds(2, 1)], rx_ref.at[pl.ds(0, 1)], p_send, p_recv, (a + 1, b)
                ).start()

            @pl.when(a > 0)
            def _():
                remote(
                    cx_ref.at[pl.ds(1, 1)], rx_ref.at[pl.ds(1, 1)], p_send, p_recv, (a - 1, b)
                ).start()

            remote(cy_ref, ry_ref.at[0], p_send, p_recv, (a, upper)).start()
            remote(cy_ref, ry_ref.at[1], p_send, p_recv, (a, lower)).start()

    def turn(step, carry):
        @pl.when(step == last)
        def _():
            with jax.named_scope("barrier"):
                pl.semaphore_wait(barrier, ndev - 1)

            @pl.when(early)
            def _():
                send_faces()
                send_near()
                send_far()

            @pl.when(jnp.logical_not(early))
            def _():
                send_far()
                send_near()

        @pl.when(step != last)
        def _():
            with jax.named_scope("w_side"):
                loads["side"].wait()
            with jax.named_scope("lin"):
                y0, y1, y2, y3 = down("picks", 32, c_ref, d_ref, lambda: None)
                flat = right_mul(*halves(left_mul("flat", sample_ref[0], sample_ref[1])), "lin")
                cx = jnp.concatenate(
                    [
                        jnp.where(lane[0:8] < 64, pltpu.roll(u[0:8], 64, 1), v[0:8])
                        for u, v in ((y0, y1), (y2, y3))
                    ],
                    axis=1,
                )
                cx = cx - flat[0:8, 0:256]
                cy = jnp.where(lane[0:16] < 32, y0[16:] + y2[16:], y1[16:] + y3[16:])
                cy = cy - flat[16:32, 256:384]
                cx_ref[...] = cx
                cy_ref[...] = cy

            with jax.named_scope("near"):
                folded = [
                    jnp.concatenate(
                        [w_ref[c // 2, (2 * k + c % 2) * n : (2 * k + c % 2 + 1) * n] for c in range(4)],
                        axis=1,
                    )
                    for k in range(2)
                ]
                narrow = halves(left_mul("sn", *folded))
                spectrum = []
                for c in range(4):
                    at = slice(c * 256, (c + 1) * 256)
                    spectrum.append(right_mul(narrow[0][:, at], narrow[1][:, at], "near%d" % c))
                spec_ref[...] = jnp.concatenate(spectrum, axis=1)

        return carry

    last = jnp.where(early, 1, 0)
    lax.fori_loop(0, 2, turn, 0)

    @pl.when(jnp.logical_not(early))
    def _():
        send_faces()

    edge = (a == 0) | (a == n_gx - 1)
    inner = jnp.logical_not(edge)

    def settle_near(sides):
        lines = 16 * (modes // 128) * ((1 + sides) * n_gy - 1) + 2 * sides + 32
        block = tally_ref.at[pl.ds(0, lines)]
        remote(block, block, p_send, p_recv, (a, b)).wait()

    with jax.named_scope("wait_p"):

        @pl.when(edge)
        def _():
            settle_near(1)

        @pl.when(inner)
        def _():
            settle_near(2)

    with jax.named_scope("face"):
        cx, cy, spectrum = cx_ref[...], cy_ref[...], spec_ref[...]
        from_left = jnp.where(a > 0, rx_ref[0:1], 0.0)
        from_right = jnp.where(a < n_gx - 1, rx_ref[1:2], 0.0)
        ends = jnp.concatenate(
            [cx[0:1] + from_left, cx[3:4] + from_right, jnp.zeros((14, cx.shape[1]), jnp.float32)]
        )
        ends = right_mul(*halves(ends), "facex")
        fine = 16 * half
        column = vmem["recip"][fine + 4 * n : fine + 5 * n, 0:2]
        spectrum = spectrum + column[:, 0:1] * ends[0:1] + column[:, 1:2] * ends[1:2]
        group = jnp.where(lane[0:16] < 64, lax.rem(lane[0:16], 32) // 8, 4)
        total = jnp.where((group == 0) | (group == 3), cy, 0.0)
        total = total + jnp.where((group == 2) & (b > 0), ry_ref[0], 0.0)
        total = total + jnp.where((group == 1) & (b < n_gy - 1), ry_ref[1], 0.0)
        total = left_mul("sb", *halves(total))[:, 0:64]
        spectrum = spectrum + right_mul(*halves(total), "facey")
    with jax.named_scope("green"):
        row = lax.broadcasted_iota(jnp.int32, (8, modes), 0)

        def gathered(step):
            value = near_ref[step * n_gy]
            for j in range(1, n_gy):
                value = value + near_ref[step * n_gy + j]
            return value

        past = jnp.where(a > 0, gathered(0), 0.0)
        here = gathered(1)
        next_ = jnp.where(a < n_gx - 1, gathered(2), 0.0)
        source = jnp.concatenate(
            [
                jnp.where((row >= 4) | (a > 1), past[0:8], 0.0),
                past[8:16] + jnp.where((row >= 4) | (a > 0), here[0:8], 0.0),
                jnp.where((row < 4) | (a < n_gx - 1), here[8:16] + next_[0:8], 0.0),
                jnp.where((row < 4) | (a < n_gx - 2), next_[8:16], 0.0),
            ]
        )
        values = []
        for i in range(cells + 2):
            influence = mine[169 - i : 201 - i] - mine[208 + i : 240 + i]
            values.append(jnp.sum(influence * source, axis=0, keepdims=True))
        values.append(jnp.zeros((16 - len(values), modes), jnp.float32))
        lifted = left_mul("u12", *halves(jnp.concatenate(values, axis=0)))

    inverse = jnp.concatenate(
        [vmem["recip"][fine + c * n : fine + (c + 1) * n] for c in range(4)], axis=1
    )

    def unfolded(parts):
        sides = [
            jnp.concatenate([part[:, s * 128 : (s + 1) * 128] for part in parts], axis=1)
            for s in range(2)
        ]
        return jnp.concatenate(sides, axis=0)

    def cells_of(both):
        for s, group in enumerate(groups):
            for i, v in enumerate(group):
                yield v, both[s * n : (s + 1) * n, i * 128 : (i + 1) * 128]

    with jax.named_scope("base"):
        lifted = halves(jnp.concatenate([lifted[:n], lifted[n:]], axis=1))
        spectrum = (spectrum + right_mul(*lifted, "drop")) * inverse
        high, low = halves(left_mul("sn", *halves(spectrum)))
        parts = []
        for c in range(4):
            at = slice(c * 256, (c + 1) * 256)
            parts.append(right_mul(high[:, at], low[:, at], "far%d" % c))
        high, low = halves(unfolded(parts))
        both = mm(jnp.concatenate([high, low], axis=0), table("unfold", 0))
        for v, value in cells_of(both[: 2 * n] + both[2 * n :]):
            out_ref[:, v * 128 : (v + 1) * 128] = value

    def settle_far(each):
        block = far_ref.at[:, :, pl.ds(0, each)]
        remote(block, block, f_send, f_recv, (a, b)).wait()

    with jax.named_scope("wait_f"):

        @pl.when(edge)
        def _():
            settle_far(n_gx - 2)

        @pl.when(inner)
        def _():
            settle_far(n_gx - 3)

    with jax.named_scope("final"):
        origin = lax.broadcasted_iota(jnp.int32, (n_gx, modes), 0)
        before = jnp.zeros((n_gx, modes), jnp.float32)
        after = before
        for j in range(n_gy):
            sent = jnp.concatenate([far_ref[j, g] for g in range(modes // 128)], axis=1)
            before = before + jnp.where(origin <= a - 2, sent, 0.0)
            after = after + jnp.where(origin >= a + 2, sent, 0.0)
        before = jnp.sum(before * mine[256 : 256 + n_gx], axis=0, keepdims=True)
        after = jnp.sum(after * mine[256 + n_gx : 256 + 2 * n_gx], axis=0, keepdims=True)
        lifted = mine[32:96] * before + mine[96:160] * after
        lifted = jnp.concatenate([lifted[:n], lifted[n:]], axis=1).astype(jnp.bfloat16)
        spectrum = (mm(lifted, table("drop", 0)) * inverse).astype(jnp.bfloat16)
        group, place = places["sn"]
        row, rows, _ = place["left"]
        spectrum = mm(vmem[group][row : row + rows, 0:n], spectrum).astype(jnp.bfloat16)
        parts = [mm(spectrum[:, c * 256 : (c + 1) * 256], tile("far%d" % c, 0, 0)) for c in range(4)]
    with jax.named_scope("unfold"):
        both = mm(unfolded(parts).astype(jnp.bfloat16), table("unfold", 0))
        for v, value in cells_of(both):
            at = slice(v * 128, (v + 1) * 128)
            out_ref[:, at] = out_ref[:, at] + value


def emit(in_ref, out_ref, sem):
    copy = pltpu.make_async_copy(in_ref, out_ref, sem)
    copy.start()
    copy.wait()


def body(n_gx, n_gy, charge):
    singles, places = tables(n_gx, n_gy)
    arrays = [charge] + [jnp.asarray(singles[name]) for name in NAMES[1:]]
    shapes = {name: window(name, array.shape) for name, array in zip(NAMES, arrays)}
    total = sum(shapes[name][0] for name in GROUPS)
    scratch = [pltpu.VMEM(shapes[name], jnp.float32) for name in ("charge", "compact", "recip", "mine")]
    scratch.append(pltpu.VMEM((total, 256), jnp.bfloat16))
    modes = n_gy * (P_SIZE // Q) ** 2
    half = P_SIZE + 2 * W
    scratch += [
        pltpu.VMEM((512, 512), jnp.bfloat16),
        pltpu.VMEM((4, 256, 512), jnp.bfloat16),
        pltpu.VMEM((2, 16, 256), jnp.bfloat16),
        pltpu.VMEM((P_SIZE, 1024), jnp.float32),
        pltpu.VMEM((2, 4 * P_SIZE, 256), jnp.bfloat16),
        pltpu.VMEM((2, 8 * P_SIZE, 256), jnp.bfloat16),
        pltpu.VMEM((2 * P_SIZE, 4096), jnp.bfloat16),
        pltpu.VMEM((2 * half, 4096), jnp.bfloat16),
        pltpu.VMEM((2, 256, 256), jnp.bfloat16),
        pltpu.VMEM((2, 64, 512), jnp.bfloat16),
        pltpu.VMEM((2, 512, 256), jnp.bfloat16),
        pltpu.VMEM((2, 128, 512), jnp.bfloat16),
        pltpu.VMEM((modes // 128, 8, 128), jnp.float32),
        pltpu.VMEM((n_gy, modes // 128, n_gx, 128), jnp.float32),
        pltpu.VMEM((3 * n_gy, 16, modes), jnp.float32),
        pltpu.VMEM((8, 256), jnp.float32),
        pltpu.VMEM((16, 128), jnp.float32),
        pltpu.VMEM((8, 256), jnp.float32),
        pltpu.VMEM((2, 16, 128), jnp.float32),
        pltpu.VMEM((16 * (modes // 128) * (3 * n_gy - 1) + 40, 128), jnp.float32),
        pltpu.SemaphoreType.DMA((len(WAITS),)),
        pltpu.SemaphoreType.DMA,
        pltpu.SemaphoreType.DMA,
        pltpu.SemaphoreType.DMA,
        pltpu.SemaphoreType.DMA,
    ]
    hbm = pl.BlockSpec(memory_space=pl.ANY)
    vm = pl.BlockSpec(memory_space=pltpu.VMEM)
    solved = pl.pallas_call(
        functools.partial(kernel, places, n_gx, n_gy),
        out_shape=pltpu.VMEM(charge.shape, charge.dtype),
        in_specs=[hbm] * len(NAMES),
        out_specs=vm,
        scratch_shapes=scratch,
        name="mlc",
        compiler_params=pltpu.CompilerParams(
            collective_id=0, has_side_effects=True, vmem_limit_bytes=60 * 1024 * 1024
        ),
    )(*arrays)
    return pl.pallas_call(
        emit,
        out_shape=jax.ShapeDtypeStruct(charge.shape, charge.dtype),
        in_specs=[vm],
        out_specs=hbm,
        scratch_shapes=[pltpu.SemaphoreType.DMA],
        name="emit",
        compiler_params=pltpu.CompilerParams(vmem_limit_bytes=1024 * 1024),
    )(solved)


def solution(mesh):
    run = functools.partial(body, mesh.shape["gx"], mesh.shape["gy"])
    spec = P("gx", "gy")
    return jax.shard_map(run, mesh=mesh, in_specs=(spec,), out_specs=spec, check_vma=False)
```
